128 devices in a mesh: gx: 8 (over z_hi, x), gy: 16 (over z_lo, y, core).
Axes of the slice: x: 4, y: 4, z: 4 (z_hi: 2, z_lo: 2; z = z_hi * 2 + z_lo), core: 2. Of those that a mesh axis runs over, the one named last changes fastest.
Arguments:
- coarse: bfloat16 [12, 128, 512], P(None, ('gx', 'gy')), may hold values from -6 to 6
- weight_one: bfloat16 [3, 3, 12, 64], replicated, may hold values from -0.625 to 0.625
- weight_two: bfloat16 [3, 3, 64, 64], replicated, may hold values from -0.25 to 0.25
- weight_three: bfloat16 [3, 3, 64, 256], replicated, may hold values from -0.25 to 0.25
- weight_four: bfloat16 [3, 3, 64, 256], replicated, may hold values from -0.25 to 0.25
- weight_five: bfloat16 [3, 3, 64, 12], replicated, may hold values from -0.25 to 0.25
- bias_one: float32 [64], replicated, may hold values from -3 to 3
- bias_two: float32 [64], replicated, may hold values from -3 to 3
- bias_three: float32 [256], replicated, may hold values from -3 to 3
- bias_four: float32 [256], replicated, may hold values from -3 to 3
- bias_five: float32 [12], replicated, may hold values from -3 to 3
- cotangent: bfloat16 [12, 512, 2048], P(None, 'gx', 'gy'), may hold values from -6 to 6
Outputs:
- fine: float32 [12, 512, 2048], P(None, 'gx', 'gy')
- grad_w1: float32 [3, 3, 12, 64], replicated
- grad_w2: float32 [3, 3, 64, 64], replicated
- grad_w3: float32 [3, 3, 64, 256], replicated
- grad_w4: float32 [3, 3, 64, 256], replicated
- grad_w5: float32 [3, 3, 64, 12], replicated
- grad_b1: float32 [64], replicated
- grad_b2: float32 [64], replicated
- grad_b3: float32 [256], replicated
- grad_b4: float32 [256], replicated
- grad_b5: float32 [12], replicated
The draws below stay inside these ranges and needn't reach their ends.
All inputs are finite; a program needn't handle non-finite values.
Results may differ from the reference program's by a relative error of at most 0.013.
Values may be sent and summed in bfloat16 or wider, within the bound.
A program may use at most 128 MiB of HBM per device.

```python
import jax
import jax.numpy as jnp
from jax import lax

CH = 12
C = 64
NX = 128
NY = 512


def level_of(stream_key, extent, cuts, smallest, top_value):
    def one(position, blocks):
        draws = jax.random.uniform(jax.random.fold_in(jax.random.fold_in(stream_key, 6), position), (blocks,), jnp.float32, smallest / len(cuts), top_value / len(cuts))
        return jnp.repeat(jnp.exp(draws), extent[position] // blocks).reshape((-1,) + (1,) * (len(extent) - position - 1))

    factor_of = one(*cuts[0])
    for cut in cuts[1:]:
        factor_of = factor_of * one(*cut)
    return factor_of


def gaussian(stream_key, extent, spread, limit, shards=(), kind=jnp.bfloat16):
    array = jax.random.normal(stream_key, extent, jnp.float32) * spread
    if len(shards) > 0:
        array = level_of(stream_key, extent, shards, -0.22, 0.18) * array
    return jnp.clip(array, min=-limit, max=limit).astype(kind)


def setup_inputs(seed: int = 0) -> dict:
    arg_keys = jax.random.split(jax.random.key(seed), 13)
    return {
        "coarse": gaussian(arg_keys[0], (CH, NX, NY), 1.0, 6.0, ((1, 128),)),
        "weight_one": gaussian(arg_keys[1], (3, 3, CH, C), (9 * CH) ** -0.5, 0.625),
        "weight_two": gaussian(arg_keys[2], (3, 3, C, C), (9 * C) ** -0.5, 0.25),
        "weight_three": gaussian(arg_keys[3], (3, 3, C, 4 * C), (9 * C) ** -0.5, 0.25),
        "weight_four": gaussian(arg_keys[4], (3, 3, C, 4 * C), (9 * C) ** -0.5, 0.25),
        "weight_five": gaussian(arg_keys[5], (3, 3, C, CH), (9 * C) ** -0.5, 0.25),
        "bias_one": gaussian(arg_keys[6], (C,), 0.3, 3.0, (), jnp.float32),
        "bias_two": gaussian(arg_keys[7], (C,), 0.3, 3.0, (), jnp.float32),
        "bias_three": gaussian(arg_keys[8], (4 * C,), 0.3, 3.0, (), jnp.float32),
        "bias_four": gaussian(arg_keys[9], (4 * C,), 0.3, 3.0, (), jnp.float32),
        "bias_five": gaussian(arg_keys[10], (CH,), 0.3, 3.0, (), jnp.float32),
        "cotangent": gaussian(arg_keys[11], (CH, 4 * NX, 4 * NY), 1.0, 6.0, ((1, 8), (2, 16))),
    }


def conv_valid(padded, weight, bias):
    rows = padded.shape[1] - 2
    cols = padded.shape[2] - 2
    values = padded.astype(jnp.float32)
    kernel = weight.astype(jnp.float32)
    total = jnp.zeros((weight.shape[3], rows, cols), jnp.float32) + bias[:, None, None]
    for row_off in range(3):
        for col_off in range(3):
            total = total + jnp.einsum('chw,co->ohw', values[:, row_off:row_off + rows, col_off:col_off + cols], kernel[row_off, col_off])
    return total

def conv_back(padded, weight):
    rows = padded.shape[1] - 2
    cols = padded.shape[2] - 2
    values = padded.astype(jnp.float32)
    kernel = weight.astype(jnp.float32)
    total = jnp.zeros((weight.shape[2], rows, cols), jnp.float32)
    for row_off in range(3):
        for col_off in range(3):
            total = total + jnp.einsum('ohw,co->chw', values[:, 2 - row_off:2 - row_off + rows, 2 - col_off:2 - col_off + cols], kernel[row_off, col_off])
    return total

def weight_grad(padded, grad):
    rows = grad.shape[1]
    cols = grad.shape[2]
    values = padded.astype(jnp.float32)
    grad_f = grad.astype(jnp.float32)
    pieces = []
    for row_off in range(3):
        for col_off in range(3):
            pieces.append(jnp.einsum('chw,ohw->co', values[:, row_off:row_off + rows, col_off:col_off + cols], grad_f))
    stacked = jnp.stack(pieces)
    return stacked.reshape(3, 3, stacked.shape[1], stacked.shape[2])

def squash(value):
    return jnp.tanh(value)

def slopes(act):
    act_f = act.astype(jnp.float32)
    return 1.0 - act_f * act_f

def shuffle(value):
    chans, rows, cols = value.shape
    return value.reshape(chans // 4, 2, 2, rows, cols).transpose(0, 3, 1, 4, 2).reshape(chans // 4, 2 * rows, 2 * cols)

def unshuffle(value):
    chans, rows, cols = value.shape
    return value.reshape(chans, rows // 2, 2, cols // 2, 2).transpose(0, 2, 4, 1, 3).reshape(4 * chans, rows // 2, cols // 2)

def padded_one(value):
    return jnp.pad(value, ((0, 0), (1, 1), (1, 1)))

def reference(coarse, weight_one, weight_two, weight_three, weight_four, weight_five, bias_one, bias_two, bias_three, bias_four, bias_five, cotangent):
    pad_zero = padded_one(coarse)
    act_one = squash(conv_valid(pad_zero, weight_one, bias_one)).astype(jnp.bfloat16)
    pad_one = padded_one(act_one)
    act_two = squash(conv_valid(pad_one, weight_two, bias_two)).astype(jnp.bfloat16)
    pad_two = padded_one(act_two)
    act_three = shuffle(squash(conv_valid(pad_two, weight_three, bias_three))).astype(jnp.bfloat16)
    pad_three = padded_one(act_three)
    act_four = shuffle(squash(conv_valid(pad_three, weight_four, bias_four))).astype(jnp.bfloat16)
    pad_four = padded_one(act_four)
    fine = conv_valid(pad_four, weight_five, bias_five)
    scale = jnp.float32(16 * NX * NY) ** (-0.5)
    grad_w5 = scale * weight_grad(pad_four, cotangent)
    grad_b5 = scale * lax.optimization_barrier(jnp.sum(cotangent.astype(jnp.float32), axis=(1, 2)))
    back_four = unshuffle(conv_back(padded_one(cotangent), weight_five) * slopes(act_four)).astype(jnp.bfloat16)
    grad_w4 = scale * weight_grad(pad_three, back_four)
    grad_b4 = scale * lax.optimization_barrier(jnp.sum(back_four.astype(jnp.float32), axis=(1, 2)))
    back_three = unshuffle(conv_back(padded_one(back_four), weight_four) * slopes(act_three)).astype(jnp.bfloat16)
    grad_w3 = scale * weight_grad(pad_two, back_three)
    grad_b3 = scale * lax.optimization_barrier(jnp.sum(back_three.astype(jnp.float32), axis=(1, 2)))
    back_two = (conv_back(padded_one(back_three), weight_three) * slopes(act_two)).astype(jnp.bfloat16)
    grad_w2 = scale * weight_grad(pad_one, back_two)
    grad_b2 = scale * lax.optimization_barrier(jnp.sum(back_two.astype(jnp.float32), axis=(1, 2)))
    back_one = (conv_back(padded_one(back_two), weight_two) * slopes(act_one)).astype(jnp.bfloat16)
    grad_w1 = scale * weight_grad(pad_zero, back_one)
    grad_b1 = scale * lax.optimization_barrier(jnp.sum(back_one.astype(jnp.float32), axis=(1, 2)))
    return (fine, grad_w1, grad_w2, grad_w3, grad_w4, grad_w5, grad_b1, grad_b2, grad_b3, grad_b4, grad_b5)
```

```python
import jax
import jax.numpy as jnp
from jax import lax
from jax.sharding import PartitionSpec as P


def padded_2(block, sides, width):
    for axis, dim in sides:
        count = lax.axis_size(axis)
        forward = [(i, i + 1) for i in range(count - 1)]
        backward = [(target, source) for source, target in forward]
        low = lax.ppermute(
            lax.slice_in_dim(block, block.shape[dim] - width, None, axis=dim), axis, forward
        )
        high = lax.ppermute(lax.slice_in_dim(block, 0, width, axis=dim), axis, backward)
        block = jnp.concatenate([low, block, high], axis=dim)
    return block


def conv_valid(padded, weight, bias):
    rows = padded.shape[1] - 2
    cols = padded.shape[2] - 2
    total = jnp.zeros((weight.shape[3], rows, cols), jnp.float32) + bias[:, None, None]
    for row_off in range(3):
        for col_off in range(3):
            total = total + jnp.einsum(
                "chw,co->ohw",
                padded[:, row_off : row_off + rows, col_off : col_off + cols],
                weight[row_off, col_off],
                preferred_element_type=jnp.float32,
            )
    return total


def conv_back(padded, weight):
    rows = padded.shape[1] - 2
    cols = padded.shape[2] - 2
    total = jnp.zeros((weight.shape[2], rows, cols), jnp.float32)
    for row_off in range(3):
        for col_off in range(3):
            total = total + jnp.einsum(
                "ohw,co->chw",
                padded[:, 2 - row_off : 2 - row_off + rows, 2 - col_off : 2 - col_off + cols],
                weight[row_off, col_off],
                preferred_element_type=jnp.float32,
            )
    return total


def weight_grad(padded, grad):
    rows = grad.shape[1]
    cols = grad.shape[2]
    pieces = []
    for row_off in range(3):
        for col_off in range(3):
            pieces.append(
                jnp.einsum(
                    "chw,ohw->co",
                    padded[:, row_off : row_off + rows, col_off : col_off + cols],
                    grad,
                    preferred_element_type=jnp.float32,
                )
            )
    stacked = jnp.stack(pieces)
    return stacked.reshape(3, 3, stacked.shape[1], stacked.shape[2])


def squash(value):
    return jnp.tanh(value)


def slopes(act):
    act_f = act.astype(jnp.float32)
    return 1.0 - act_f * act_f


def shuffle(value):
    chans, rows, cols = value.shape
    return (
        value.reshape(chans // 4, 2, 2, rows, cols)
        .transpose(0, 3, 1, 4, 2)
        .reshape(chans // 4, 2 * rows, 2 * cols)
    )


def unshuffle(value):
    chans, rows, cols = value.shape
    return (
        value.reshape(chans, rows // 2, 2, cols // 2, 2)
        .transpose(0, 2, 4, 1, 3)
        .reshape(4 * chans, rows // 2, cols // 2)
    )


def inside(halo, rows, cols, grain):
    row = lax.axis_index("gx") * rows * grain - halo + jnp.arange(rows * grain + 2 * halo)
    col = lax.axis_index("gy") * cols * grain - halo + jnp.arange(cols * grain + 2 * halo)
    row_ok = (row >= 0) & (row < rows * grain * lax.axis_size("gx"))
    col_ok = (col >= 0) & (col < cols * grain * lax.axis_size("gy"))
    return (row_ok[:, None] & col_ok[None, :])[None]


def trim(value, width):
    return value[:, width : value.shape[1] - width, width : value.shape[2] - width]


def local_terms(padded, grad):
    return (weight_grad(padded, grad), jnp.sum(grad.astype(jnp.float32), axis=(1, 2)))


def local(
    coarse,
    weight_one,
    weight_two,
    weight_three,
    weight_four,
    weight_five,
    bias_one,
    bias_two,
    bias_three,
    bias_four,
    bias_five,
    cotangent,
):
    tile = lax.all_to_all(coarse, "gy", split_axis=2, concat_axis=1, tiled=True)
    rows = tile.shape[1]
    cols = tile.shape[2]
    sides = (("gx", 1), ("gy", 2))
    zero = jnp.bfloat16(0)
    pad_zero = padded_2(tile, sides, 6)
    pad_cot = padded_2(cotangent, sides, 11)

    def clip(value, halo, grain):
        return jnp.where(inside(halo, rows, cols, grain), value.astype(jnp.bfloat16), zero)

    act_one = clip(squash(conv_valid(pad_zero, weight_one, bias_one)), 5, 1)
    act_two = clip(squash(conv_valid(act_one, weight_two, bias_two)), 4, 1)
    act_three = clip(shuffle(squash(conv_valid(act_two, weight_three, bias_three))), 6, 2)
    act_four = clip(shuffle(squash(conv_valid(act_three, weight_four, bias_four))), 10, 4)
    pad_four = trim(act_four, 9)
    fine = conv_valid(pad_four, weight_five, bias_five)
    layer_five = local_terms(pad_four, cotangent)
    back_four = unshuffle(clip(conv_back(pad_cot, weight_five) * slopes(act_four), 10, 4))
    layer_four = local_terms(trim(act_three, 5), trim(back_four, 5))
    back_three = unshuffle(clip(conv_back(back_four, weight_four) * slopes(trim(act_three, 2)), 4, 2))
    layer_three = local_terms(trim(act_two, 3), trim(back_three, 2))
    back_two = clip(conv_back(back_three, weight_three) * slopes(trim(act_two, 3)), 1, 1)
    layer_two = local_terms(trim(act_one, 4), trim(back_two, 1))
    back_one = (conv_back(back_two, weight_two) * slopes(trim(act_one, 5))).astype(jnp.bfloat16)
    layer_one = local_terms(trim(pad_zero, 5), back_one)
    totals = lax.psum(
        (
            layer_one[0],
            layer_two[0],
            layer_three[0],
            layer_four[0],
            layer_five[0],
            layer_one[1],
            layer_two[1],
            layer_three[1],
            layer_four[1],
            layer_five[1],
        ),
        ("gx", "gy"),
    )
    cells = 16 * rows * lax.axis_size("gx") * cols * lax.axis_size("gy")
    scale = jnp.float32(cells) ** (-0.5)
    return (fine,) + tuple((scale * total for total in totals))


def solution(mesh):
    in_specs = (
        P(None, ("gx", "gy"), None),
        P(),
        P(),
        P(),
        P(),
        P(),
        P(),
        P(),
        P(),
        P(),
        P(),
        P(None, "gx", "gy"),
    )
    out_specs = (P(None, "gx", "gy"), P(), P(), P(), P(), P(), P(), P(), P(), P(), P())
    return jax.shard_map(local, mesh=mesh, in_specs=in_specs, out_specs=out_specs, check_vma=False)
```

```python
import functools

import jax
import jax.numpy as jnp
from jax import lax
from jax.experimental import pallas as pl
from jax.experimental.pallas import tpu as pltpu
from jax.sharding import PartitionSpec as P


def padded_2(block, sides, width):
    for axis, dim in sides:
        count = lax.axis_size(axis)
        forward = [(i, i + 1) for i in range(count - 1)]
        backward = [(target, source) for source, target in forward]
        low = lax.ppermute(
            lax.slice_in_dim(block, block.shape[dim] - width, None, axis=dim), axis, forward
        )
        high = lax.ppermute(lax.slice_in_dim(block, 0, width, axis=dim), axis, backward)
        block = jnp.concatenate([low, block, high], axis=dim)
    return block


def conv_valid(padded, weight, bias):
    rows = padded.shape[1] - 2
    cols = padded.shape[2] - 2
    total = jnp.zeros((weight.shape[3], rows, cols), jnp.float32) + bias[:, None, None]
    for row_off in range(3):
        for col_off in range(3):
            total = total + jnp.einsum(
                "chw,co->ohw",
                padded[:, row_off : row_off + rows, col_off : col_off + cols],
                weight[row_off, col_off],
                preferred_element_type=jnp.float32,
            )
    return total


def conv_back(padded, weight):
    rows = padded.shape[1] - 2
    cols = padded.shape[2] - 2
    total = jnp.zeros((weight.shape[2], rows, cols), jnp.float32)
    for row_off in range(3):
        for col_off in range(3):
            total = total + jnp.einsum(
                "ohw,co->chw",
                padded[:, 2 - row_off : 2 - row_off + rows, 2 - col_off : 2 - col_off + cols],
                weight[row_off, col_off],
                preferred_element_type=jnp.float32,
            )
    return total


def weight_grad(padded, grad):
    rows = grad.shape[1]
    cols = grad.shape[2]
    pieces = []
    for row_off in range(3):
        for col_off in range(3):
            pieces.append(
                jnp.einsum(
                    "chw,ohw->co",
                    padded[:, row_off : row_off + rows, col_off : col_off + cols],
                    grad,
                    preferred_element_type=jnp.float32,
                )
            )
    stacked = jnp.stack(pieces)
    return stacked.reshape(3, 3, stacked.shape[1], stacked.shape[2])


def squash(value):
    return jnp.tanh(value)


def slopes(act):
    act_f = act.astype(jnp.float32)
    return 1.0 - act_f * act_f


def shuffle(value):
    chans, rows, cols = value.shape
    return (
        value.reshape(chans // 4, 2, 2, rows, cols)
        .transpose(0, 3, 1, 4, 2)
        .reshape(chans // 4, 2 * rows, 2 * cols)
    )


def unshuffle(value):
    chans, rows, cols = value.shape
    return (
        value.reshape(chans, rows // 2, 2, cols // 2, 2)
        .transpose(0, 2, 4, 1, 3)
        .reshape(4 * chans, rows // 2, cols // 2)
    )


def tile_rim(value):
    return padded_2(value, (("gx", 1), ("gy", 2)), 1)


def grad_rim(value):
    return padded_2(value, (("gx", 1), ("gy", 2)), 1)


def local_terms(padded, grad):
    return (weight_grad(padded, grad), jnp.sum(grad.astype(jnp.float32), axis=(1, 2)))


MESH_ID = pl.DeviceIdType.MESH
PACK = 3072
HALF = PACK // 2
THIRD = HALF // 3
PARTS = (THIRD // 4, THIRD // 16, THIRD // 64)


def coordinates():
    gx = lax.axis_index("gx")
    gy = lax.axis_index("gy")
    return (gx % 4, (gy // 2) % 4, (gx // 4) * 2 + gy // 8), gy % 2


def device_at(place, core):
    x, y, z = place
    return ((z // 2) * 4 + x, (z % 2) * 8 + y * 2 + core)


def along(place, axis, step):
    moved = list(place)
    moved[axis] = (place[axis] + step) % 4
    return moved


def rows_at(start, count):
    return pl.ds(pl.multiple_of(start, 8), count)


def total_kernel(
    scale,
    pack,
    out_w1,
    out_w2,
    out_w3,
    out_w4,
    out_w5,
    out_b1,
    out_b2,
    out_b3,
    out_b4,
    out_b5,
    pair_in,
    pair_sum,
    in_a,
    sum_a,
    in_b,
    sum_b,
    in_c,
    whole,
    pair_send,
    pair_recv,
    down_send,
    down_recv,
    up_send,
    up_recv,
):
    place, core = coordinates()
    partner = device_at(place, 1 - core)
    barrier = pltpu.get_barrier_semaphore()
    peers = [partner] + [
        device_at(along(place, axis, step), core) for axis in range(3) for step in (1, 2, 3)
    ]
    for peer in peers:
        pl.semaphore_signal(barrier, inc=1, device_id=peer, device_id_type=MESH_ID)
    pl.semaphore_wait(barrier, len(peers))

    def send(src, dst, send_sem, recv_sem, peer):
        copy = pltpu.make_async_remote_copy(
            src_ref=src,
            dst_ref=dst,
            send_sem=send_sem,
            recv_sem=recv_sem,
            device_id=peer,
            device_id_type=MESH_ID,
        )
        copy.start()
        return copy

    sent = []
    pairs = []
    for third in range(3):
        pairs.append(
            send(
                pack.at[rows_at((1 - core) * HALF + third * THIRD, THIRD)],
                pair_in.at[pl.ds(third * THIRD, THIRD)],
                pair_send.at[third],
                pair_recv.at[third],
                partner,
            )
        )
    stage_in = (in_a, in_b, in_c)
    stage_from = (pair_sum, sum_a, sum_b)
    spans = (THIRD, PARTS[0], PARTS[1])

    def scatter(third, stage):
        axis = (third + stage) % 3
        part = PARTS[stage]
        copies = []
        for step in (1, 2, 3):
            quarter = (place[axis] + step) % 4
            copies.append(
                send(
                    stage_from[stage].at[rows_at(third * spans[stage] + quarter * part, part)],
                    stage_in[stage].at[third, step - 1],
                    down_send.at[stage, third, step - 1],
                    down_recv.at[stage, third, step - 1],
                    device_at(along(place, axis, step), core),
                )
            )
        return copies

    def collect(third, stage, copies):
        axis = (third + stage) % 3
        part = PARTS[stage]
        value = stage_from[stage][rows_at(third * spans[stage] + place[axis] * part, part), :]
        for step in (1, 2, 3):
            copies[step - 1].wait_recv()
            value = value + stage_in[stage][third, step - 1]
        return value

    def row_of(third, level):
        row = core * HALF + third * THIRD
        for stage in range(level):
            row = row + place[(third + stage) % 3] * PARTS[stage]
        return row

    flying = []
    for third in range(3):
        pairs[third].wait_recv()
        own = pack[rows_at(core * HALF + third * THIRD, THIRD), :]
        pair_sum[pl.ds(third * THIRD, THIRD), :] = own + pair_in[pl.ds(third * THIRD, THIRD), :]
        flying.append(scatter(third, 0))
    for stage in range(2):
        arrived = flying
        sent = sent + flying
        flying = []
        for third in range(3):
            part = PARTS[stage]
            stage_from[stage + 1][pl.ds(third * part, part), :] = collect(
                third, stage, arrived[third]
            )
            flying.append(scatter(third, stage + 1))
    sent = sent + flying

    def gather(third, stage):
        axis = (third + stage) % 3
        part = PARTS[stage]
        block = whole.at[rows_at(row_of(third, stage + 1), part)]
        return [
            send(
                block,
                block,
                up_send.at[stage, third, step - 1],
                up_recv.at[stage, third, step - 1],
                device_at(along(place, axis, step), core),
            )
            for step in (1, 2, 3)
        ]

    rising = []
    for third in range(3):
        whole[rows_at(row_of(third, 3), PARTS[2]), :] = collect(third, 2, flying[third])
        rising.append(gather(third, 2))
    for stage in (1, 0):
        arrived = rising
        sent = sent + rising
        rising = []
        for third in range(3):
            for copy in arrived[third]:
                copy.wait_recv()
            rising.append(gather(third, stage))
    sent = sent + rising
    finals = []
    for third in range(3):
        for copy in rising[third]:
            copy.wait_recv()
        block = whole.at[rows_at(row_of(third, 0), THIRD)]
        finals.append(
            send(block, block, pair_send.at[3 + third], pair_recv.at[3 + third], partner)
        )
    for copy in finals:
        copy.wait_recv()
    for copies in sent:
        for copy in copies:
            copy.wait_send()
    for copy in pairs + finals:
        copy.wait_send()

    for index, target in ((0, out_w4), (1152, out_w3)):
        target[:, 0:128] = whole[index : index + 576, :] * scale
        target[:, 128:256] = whole[index + 576 : index + 1152, :] * scale
    out_w2[...] = whole[2304:2880, 0:64] * scale
    out_w5[...] = whole[2304:2880, 64:76] * scale
    for tap in range(9):
        out_w1[tap] = whole[2880 + 12 * tap : 2892 + 12 * tap, 0:64] * scale
    for index, target in ((2992, out_b4), (2994, out_b3)):
        target[:, 0:128] = whole[index : index + 1, :] * scale
        target[:, 128:256] = whole[index + 1 : index + 2, :] * scale
    out_b2[...] = whole[2996:2997, 0:64] * scale
    out_b1[...] = whole[2996:2997, 64:128] * scale
    out_b5[...] = whole[2997:2998, 0:12] * scale


def totals_of(pack, scale):
    shapes = ((9, 12, 64), (576, 64), (576, 256), (576, 256), (576, 12))
    shapes = shapes + ((1, 64), (1, 64), (1, 256), (1, 256), (1, 12))
    vmem = pl.BlockSpec(memory_space=pltpu.VMEM)
    scratch = [pltpu.VMEM((HALF, 128), jnp.float32) for _ in range(2)]
    for part in PARTS[:2]:
        scratch.append(pltpu.VMEM((3, 3, part, 128), jnp.float32))
        scratch.append(pltpu.VMEM((3 * part, 128), jnp.float32))
    scratch.append(pltpu.VMEM((3, 3, PARTS[2], 128), jnp.float32))
    scratch.append(pltpu.VMEM((PACK, 128), jnp.float32))
    scratch += [pltpu.SemaphoreType.DMA((6,))] * 2 + [pltpu.SemaphoreType.DMA((3, 3, 3))] * 4
    return pl.pallas_call(
        functools.partial(total_kernel, scale),
        out_shape=[jax.ShapeDtypeStruct(shape, jnp.float32) for shape in shapes],
        in_specs=[vmem],
        out_specs=[vmem] * 10,
        scratch_shapes=scratch,
        compiler_params=pltpu.CompilerParams(collective_id=1, has_side_effects=True),
        name="grad_totals",
    )(pack)


def local(
    coarse,
    weight_one,
    weight_two,
    weight_three,
    weight_four,
    weight_five,
    bias_one,
    bias_two,
    bias_three,
    bias_four,
    bias_five,
    cotangent,
):
    tile = lax.all_to_all(coarse, "gy", split_axis=2, concat_axis=1, tiled=True)
    rows = tile.shape[1]
    cols = tile.shape[2]
    pad_zero = tile_rim(tile)
    act_one = squash(conv_valid(pad_zero, weight_one, bias_one)).astype(jnp.bfloat16)
    pad_one = tile_rim(act_one)
    act_two = squash(conv_valid(pad_one, weight_two, bias_two)).astype(jnp.bfloat16)
    pad_two = tile_rim(act_two)
    act_three = shuffle(squash(conv_valid(pad_two, weight_three, bias_three))).astype(jnp.bfloat16)
    pad_three = tile_rim(act_three)
    act_four = shuffle(squash(conv_valid(pad_three, weight_four, bias_four))).astype(jnp.bfloat16)
    pad_four = tile_rim(act_four)
    fine = conv_valid(pad_four, weight_five, bias_five)
    layer_five = local_terms(pad_four, cotangent)
    back_four = unshuffle(conv_back(grad_rim(cotangent), weight_five) * slopes(act_four)).astype(
        jnp.bfloat16
    )
    layer_four = local_terms(pad_three, back_four)
    back_three = unshuffle(conv_back(grad_rim(back_four), weight_four) * slopes(act_three)).astype(
        jnp.bfloat16
    )
    layer_three = local_terms(pad_two, back_three)
    back_two = (conv_back(grad_rim(back_three), weight_three) * slopes(act_two)).astype(
        jnp.bfloat16
    )
    layer_two = local_terms(pad_one, back_two)
    back_one = (conv_back(grad_rim(back_two), weight_two) * slopes(act_one)).astype(jnp.bfloat16)
    layer_one = local_terms(pad_zero, back_one)
    flat_four = layer_four[0].reshape(576, 256)
    flat_three = layer_three[0].reshape(576, 256)
    last = jnp.concatenate(
        [
            layer_two[0].reshape(576, 64),
            layer_five[0].reshape(576, 12),
            jnp.zeros((576, 52), jnp.float32),
        ],
        axis=1,
    )
    first = jnp.pad(layer_one[0].reshape(108, 64), ((0, 4), (0, 64)))
    biases = jnp.concatenate(
        [
            layer_four[1],
            layer_three[1],
            layer_two[1],
            layer_one[1],
            layer_five[1],
            jnp.zeros((80 * 128 - 652,), jnp.float32),
        ]
    ).reshape(80, 128)
    pack = jnp.concatenate(
        [
            flat_four[:, :128],
            flat_four[:, 128:],
            flat_three[:, :128],
            flat_three[:, 128:],
            last,
            first,
            biases,
        ]
    )
    cells = 16 * rows * 8 * cols * 16
    totals = totals_of(pack, float(cells) ** -0.5)
    shapes = (
        weight_one.shape,
        weight_two.shape,
        weight_three.shape,
        weight_four.shape,
        weight_five.shape,
        (64,),
        (64,),
        (256,),
        (256,),
        (12,),
    )
    return (fine,) + tuple(total.reshape(shape) for total, shape in zip(totals, shapes))


def solution(mesh):
    in_specs = (
        P(None, ("gx", "gy"), None),
        P(),
        P(),
        P(),
        P(),
        P(),
        P(),
        P(),
        P(),
        P(),
        P(),
        P(None, "gx", "gy"),
    )
    out_specs = (P(None, "gx", "gy"), P(), P(), P(), P(), P(), P(), P(), P(), P(), P())
    return jax.shard_map(local, mesh=mesh, in_specs=in_specs, out_specs=out_specs, check_vma=False)
```

```python
import functools

import jax
import jax.numpy as jnp
from jax import lax
from jax.experimental import pallas as pl
from jax.experimental.pallas import tpu as pltpu
from jax.sharding import PartitionSpec as P

MESH_ID = pl.DeviceIdType.MESH
PACK = 3072
HALF = PACK // 2
THIRD = HALF // 3
PARTS = (THIRD // 4, THIRD // 16, THIRD // 64)


def coordinates():
    gx = lax.axis_index("gx")
    gy = lax.axis_index("gy")
    return (gx % 4, (gy // 2) % 4, (gx // 4) * 2 + gy // 8), gy % 2


def device_at(place, core):
    x, y, z = place
    return ((z // 2) * 4 + x, (z % 2) * 8 + y * 2 + core)


def along(place, axis, step):
    moved = list(place)
    moved[axis] = (place[axis] + step) % 4
    return moved


def rows_at(start, count):
    return pl.ds(pl.multiple_of(start, 8), count)


def total_kernel(
    scale,
    pack,
    out_w1,
    out_w2,
    out_w3,
    out_w4,
    out_w5,
    out_b1,
    out_b2,
    out_b3,
    out_b4,
    out_b5,
    pair_in,
    pair_sum,
    in_a,
    sum_a,
    in_b,
    sum_b,
    in_c,
    whole,
    pair_send,
    pair_recv,
    down_send,
    down_recv,
    up_send,
    up_recv,
):
    place, core = coordinates()
    partner = device_at(place, 1 - core)
    barrier = pltpu.get_barrier_semaphore()
    peers = [partner] + [
        device_at(along(place, axis, step), core) for axis in range(3) for step in (1, 2, 3)
    ]
    for peer in peers:
        pl.semaphore_signal(barrier, inc=1, device_id=peer, device_id_type=MESH_ID)
    pl.semaphore_wait(barrier, len(peers))

    def send(src, dst, send_sem, recv_sem, peer):
        copy = pltpu.make_async_remote_copy(
            src_ref=src,
            dst_ref=dst,
            send_sem=send_sem,
            recv_sem=recv_sem,
            device_id=peer,
            device_id_type=MESH_ID,
        )
        copy.start()
        return copy

    sent = []
    pairs = []
    for third in range(3):
        pairs.append(
            send(
                pack.at[rows_at((1 - core) * HALF + third * THIRD, THIRD)],
                pair_in.at[pl.ds(third * THIRD, THIRD)],
                pair_send.at[third],
                pair_recv.at[third],
                partner,
            )
        )
    stage_in = (in_a, in_b, in_c)
    stage_from = (pair_sum, sum_a, sum_b)
    spans = (THIRD, PARTS[0], PARTS[1])

    def scatter(third, stage):
        axis = (third + stage) % 3
        part = PARTS[stage]
        copies = []
        for step in (1, 2, 3):
            quarter = (place[axis] + step) % 4
            copies.append(
                send(
                    stage_from[stage].at[rows_at(third * spans[stage] + quarter * part, part)],
                    stage_in[stage].at[third, step - 1],
                    down_send.at[stage, third, step - 1],
                    down_recv.at[stage, third, step - 1],
                    device_at(along(place, axis, step), core),
                )
            )
        return copies

    def collect(third, stage, copies):
        axis = (third + stage) % 3
        part = PARTS[stage]
        value = stage_from[stage][rows_at(third * spans[stage] + place[axis] * part, part), :]
        for step in (1, 2, 3):
            copies[step - 1].wait_recv()
            value = value + stage_in[stage][third, step - 1]
        return value

    def row_of(third, level):
        row = core * HALF + third * THIRD
        for stage in range(level):
            row = row + place[(third + stage) % 3] * PARTS[stage]
        return row

    flying = []
    for third in range(3):
        pairs[third].wait_recv()
        own = pack[rows_at(core * HALF + third * THIRD, THIRD), :]
        pair_sum[pl.ds(third * THIRD, THIRD), :] = own + pair_in[pl.ds(third * THIRD, THIRD), :]
        flying.append(scatter(third, 0))
    for stage in range(2):
        arrived = flying
        sent = sent + flying
        flying = []
        for third in range(3):
            part = PARTS[stage]
            stage_from[stage + 1][pl.ds(third * part, part), :] = collect(
                third, stage, arrived[third]
            )
            flying.append(scatter(third, stage + 1))
    sent = sent + flying

    def gather(third, stage):
        axis = (third + stage) % 3
        part = PARTS[stage]
        block = whole.at[rows_at(row_of(third, stage + 1), part)]
        return [
            send(
                block,
                block,
                up_send.at[stage, third, step - 1],
                up_recv.at[stage, third, step - 1],
                device_at(along(place, axis, step), core),
            )
            for step in (1, 2, 3)
        ]

    rising = []
    for third in range(3):
        whole[rows_at(row_of(third, 3), PARTS[2]), :] = collect(third, 2, flying[third])
        rising.append(gather(third, 2))
    for stage in (1, 0):
        arrived = rising
        sent = sent + rising
        rising = []
        for third in range(3):
            for copy in arrived[third]:
                copy.wait_recv()
            rising.append(gather(third, stage))
    sent = sent + rising
    finals = []
    for third in range(3):
        for copy in rising[third]:
            copy.wait_recv()
        block = whole.at[rows_at(row_of(third, 0), THIRD)]
        finals.append(
            send(block, block, pair_send.at[3 + third], pair_recv.at[3 + third], partner)
        )
    for copy in finals:
        copy.wait_recv()
    for copies in sent:
        for copy in copies:
            copy.wait_send()
    for copy in pairs + finals:
        copy.wait_send()

    for index, target in ((0, out_w4), (1152, out_w3)):
        target[:, 0:128] = whole[index : index + 576, :] * scale
        target[:, 128:256] = whole[index + 576 : index + 1152, :] * scale
    out_w2[...] = whole[2304:2880, 0:64] * scale
    out_w5[...] = whole[2304:2880, 64:76] * scale
    for tap in range(9):
        out_w1[tap] = whole[2880 + 12 * tap : 2892 + 12 * tap, 0:64] * scale
    for index, target in ((2992, out_b4), (2994, out_b3)):
        target[:, 0:128] = whole[index : index + 1, :] * scale
        target[:, 128:256] = whole[index + 1 : index + 2, :] * scale
    out_b2[...] = whole[2996:2997, 0:64] * scale
    out_b1[...] = whole[2996:2997, 64:128] * scale
    out_b5[...] = whole[2997:2998, 0:12] * scale


def totals_of(pack, scale):
    shapes = ((9, 12, 64), (576, 64), (576, 256), (576, 256), (576, 12))
    shapes = shapes + ((1, 64), (1, 64), (1, 256), (1, 256), (1, 12))
    vmem = pl.BlockSpec(memory_space=pltpu.VMEM)
    scratch = [pltpu.VMEM((HALF, 128), jnp.float32) for _ in range(2)]
    for part in PARTS[:2]:
        scratch.append(pltpu.VMEM((3, 3, part, 128), jnp.float32))
        scratch.append(pltpu.VMEM((3 * part, 128), jnp.float32))
    scratch.append(pltpu.VMEM((3, 3, PARTS[2], 128), jnp.float32))
    scratch.append(pltpu.VMEM((PACK, 128), jnp.float32))
    scratch += [pltpu.SemaphoreType.DMA((6,))] * 2 + [pltpu.SemaphoreType.DMA((3, 3, 3))] * 4
    return pl.pallas_call(
        functools.partial(total_kernel, scale),
        out_shape=[jax.ShapeDtypeStruct(shape, jnp.float32) for shape in shapes],
        in_specs=[vmem],
        out_specs=[vmem] * 10,
        scratch_shapes=scratch,
        compiler_params=pltpu.CompilerParams(collective_id=1, has_side_effects=True),
        name="grad_totals",
    )(pack)


def gather_kernel(coarse, cot, rows_out, cot_out, keep_sem, row_send, row_recv, far_send, far_recv, cot_send, cot_recv):
    gx = lax.axis_index("gx")
    gy = lax.axis_index("gy")

    def peer(step_x, step_y):
        return ((gx + step_x + 8) % 8, (gy + step_y + 16) % 16)

    barrier = pltpu.get_barrier_semaphore()
    for step_x in (-1, 0, 1):
        for step_y in range(16):
            if step_x != 0 or step_y != 0:
                pl.semaphore_signal(
                    barrier, inc=1, device_id=peer(step_x, step_y), device_id_type=MESH_ID
                )
    locals_ = [
        pltpu.make_async_copy(
            cot, cot_out.at[:, pl.ds(16, 64), pl.ds(128, 128)], keep_sem.at[0]
        ),
        pltpu.make_async_copy(
            coarse.at[:, pl.ds(window(gy), 256)], rows_out.at[6 + gy], keep_sem.at[1]
        ),
    ]
    for copy in locals_:
        copy.start()
    pl.semaphore_wait(barrier, 47)

    def remote(src, dst, send_sem, recv_sem, target):
        return pltpu.make_async_remote_copy(
            src_ref=src,
            dst_ref=dst,
            send_sem=send_sem,
            recv_sem=recv_sem,
            device_id=target,
            device_id_type=MESH_ID,
        )

    def row_copy(step, dst_row, send_sem, recv_sem, step_x):
        target = peer(step_x, step)
        return remote(
            coarse.at[:, pl.ds(window(target[1]), 256)],
            rows_out.at[dst_row],
            send_sem,
            recv_sem,
            target,
        )

    copies = []
    parts = ((16, 48, 0), (64, 0, 16), (16, 0, 80))
    for index_x, step_x in enumerate((1, 0, -1)):
        count, src_row, dst_row = parts[index_x]
        for index_y, step_y in enumerate((1, 0, -1)):
            if step_x == 0 and step_y == 0:
                continue
            copies.append(
                remote(
                    cot.at[:, pl.ds(src_row, count), :],
                    cot_out.at[:, pl.ds(dst_row, count), pl.ds(128 * index_y, 128)],
                    cot_send.at[index_x, index_y],
                    cot_recv.at[index_x, index_y],
                    peer(step_x, step_y),
                )
            )
    for step in range(1, 16):
        copies.append(row_copy(step, 6 + gy, row_send.at[step], row_recv.at[step], 0))
    for copy in copies:
        copy.start()

    def far(step_x, dst_row, slot):
        return [
            row_copy(step, dst_row, far_send.at[step], far_recv.at[slot], step_x)
            for step in range(16)
        ]

    @pl.when(gy < 6)
    def _():
        for copy in far(-1, 22 + gy, 6 + gy):
            copy.start()

    @pl.when(gy >= 10)
    def _():
        for copy in far(1, gy - 10, gy - 10):
            copy.start()

    for copy in locals_:
        copy.wait()
    for copy in copies[:8]:
        copy.wait()
    for step in range(1, 16):
        row_copy(step, 6 + (gy - step + 16) % 16, row_send.at[step], row_recv.at[step], 0).wait()
    for slot in range(12):
        dst_row = slot if slot < 6 else 16 + slot
        row_copy(1, dst_row, far_send.at[0], far_recv.at[slot], 0).wait_recv()

    @pl.when(gy < 6)
    def _():
        for copy in far(-1, 22 + gy, 6 + gy):
            copy.wait_send()

    @pl.when(gy >= 10)
    def _():
        for copy in far(1, gy - 10, gy - 10):
            copy.wait_send()


def window(gy):
    return pl.multiple_of(jnp.clip(jnp.right_shift(gy * 32 - 8, 7), 0, 2) * 128, 128)


def gather_of(coarse, cot):
    vmem = pl.BlockSpec(memory_space=pltpu.VMEM)
    dma = pltpu.SemaphoreType.DMA
    return pl.pallas_call(
        gather_kernel,
        out_shape=[
            jax.ShapeDtypeStruct((28, 16, 256), jnp.bfloat16),
            jax.ShapeDtypeStruct((12, 96, 384), jnp.bfloat16),
        ],
        in_specs=[vmem] * 2,
        out_specs=[vmem] * 2,
        scratch_shapes=[dma((2,)), dma((16,)), dma((16,)), dma((16,)), dma((12,)), dma((3, 3)), dma((3, 3))],
        compiler_params=pltpu.CompilerParams(collective_id=0, has_side_effects=True),
        name="rim_gather",
    )(coarse, cot)


STRIDE = 48
ROWS = 30
SPAN = ROWS * STRIDE
BF = jnp.bfloat16
F32 = jnp.float32


def start_of(halo):
    return (7 - halo) * STRIDE - 16


def count_of(halo):
    return (16 + 2 * halo) * STRIDE + 32


def mm(lhs, rhs):
    return lax.dot_general(lhs, rhs, (((1,), (0,)), ((), ())), preferred_element_type=F32)


def mm_nt(lhs, rhs):
    return lax.dot_general(lhs, rhs, (((1,), (1,)), ((), ())), preferred_element_type=F32)


def mm_tn(lhs, rhs):
    return lax.dot_general(lhs, rhs, (((0,), (0,)), ((), ())), preferred_element_type=F32)


def iota(shape, dim):
    return lax.broadcasted_iota(jnp.int32, shape, dim)


def over(value, divisor):
    return lax.shift_right_logical(value * ((1 << 16) // divisor + 1), 16)


def one_hot(flag):
    return jnp.where(flag, 1.0, 0.0).astype(F32).astype(BF)


def three_parts(value):
    high = value.astype(BF)
    rest = value - high.astype(F32)
    middle = rest.astype(BF)
    return high, middle, (rest - middle.astype(F32)).astype(BF)


def exact_right(value, selector):
    parts = three_parts(value)
    return (mm(parts[2], selector) + mm(parts[1], selector)) + mm(parts[0], selector)


def blocks(total, chunk, body):
    def step(index, carry):
        body(pl.multiple_of(index * chunk, 16))
        return carry

    lax.fori_loop(0, total // chunk, step, 0)


def slab(start, count):
    if isinstance(start, int):
        return pl.ds(start, count)
    return pl.ds(pl.multiple_of(start, 16), count)


def inner(ref, shift, lanes):
    first = 7 + shift
    picked = [ref[(first + row) * STRIDE : (first + row) * STRIDE + 32, lanes] for row in range(16)]
    return jnp.concatenate(picked, axis=0)


ROW_SOURCE = (((1, -1), (0, 0), (1, 0)), ((0, 0), (1, 0), (0, 1)))
BACK_SOURCE = ((1, -1), (0, 0), (1, 0), (0, 1))
FINE_SOURCE = ((3, -1), (0, 0), (1, 0), (2, 0), (3, 0), (0, 1))
PAIR_ORDER = (1, 2, 3, 0)
FINE_ORDER = (1, 2, 3, 4, 5, 0)


def compute_kernel(
    where_am_i,
    rows_in,
    cot_in,
    w1,
    w2,
    w3,
    w4,
    w5,
    b1,
    b2,
    b3,
    b4,
    b5,
    fine,
    pack,
    mask,
    t_c1,
    m_c1,
    x1,
    t64,
    x2,
    x3,
    t3,
    x4,
    t4,
    x5,
    ay,
    t_cot,
    m_cot,
    xc,
    g5,
    t_g4,
    g4,
    t_g3,
    g3,
    g2,
    v1,
    v3,
    v4,
    v4f,
    v4b,
    v3b,
    v2b,
    v5f,
    v5b,
    acc,
    z5,
    turned,
    lined,
    wide,
):
    gx, gy = where_am_i()
    base_row = gx * 16
    base_col = gy * 32

    place = iota((SPAN, 128), 0)
    line = over(place, STRIDE)
    col = place - line * STRIDE
    left = jnp.where(col >= 40, 1, 0)
    row = line - 7 + left + base_row
    col = col - left * STRIDE + base_col
    ok = (row >= 0) & (row < 128) & (col >= 0) & (col < 512)
    mask[...] = jnp.where(ok, 1.0, 0.0)

    def kept(start, count):
        return mask[slab(start, count), 0:1]

    lane = iota((256, 256), 1)
    natural = iota((256, 256), 0)
    wanted = (lane - over(lane, 64) * 64) * 4 + over(lane, 64)
    to_phase = one_hot(natural == wanted)
    wanted_back = (natural - over(natural, 64) * 64) * 4 + over(natural, 64)
    to_natural = one_hot(lane == wanted_back)
    v3[...] = mm(w3[...], to_phase).astype(BF)
    v4[...] = mm(w4[...], to_phase).astype(BF)
    bias3 = exact_right(jnp.broadcast_to(b3[...], (8, 256)), to_phase)[0:1]
    bias4 = exact_right(jnp.broadcast_to(b4[...], (8, 256)), to_phase)[0:1]

    v1[...] = jnp.zeros(v1.shape, BF)
    for r in range(3):
        for s in range(3):
            v1[s * 48 + r * 16 : s * 48 + r * 16 + 12, :] = w1[r * 3 + s]
    for r in range(3):
        for position, c4 in enumerate(PAIR_ORDER):
            for q in range(2):
                s = c4 - q
                target = (slice(position * 64, position * 64 + 64), slice(q * 256, q * 256 + 256))
                if 0 <= s <= 2:
                    v4f[r, target[0], target[1]] = v4[(r * 3 + s) * 64 : (r * 3 + s) * 64 + 64, :]
                else:
                    v4f[r, target[0], target[1]] = jnp.zeros((64, 256), BF)
    for u in range(4):
        for a in range(2):
            for b in range(2):
                for position, v in enumerate(PAIR_ORDER):
                    r, s = a + 2 - u, b + 2 - v
                    at = (slice((2 * a + b) * 64, (2 * a + b) * 64 + 64),)
                    at = at + (slice(position * 256, position * 256 + 256),)
                    if 0 <= r <= 2 and 0 <= s <= 2:
                        tap = (r * 3 + s) * 64
                        v4b[u, at[0], at[1]] = v4[tap : tap + 64, :]
                    else:
                        v4b[u, at[0], at[1]] = jnp.zeros((64, 256), BF)
    for u in range(3):
        for v in range(3):
            tap = ((2 - u) * 3 + 2 - v) * 64
            v3b[u, :, v * 256 : v * 256 + 256] = v3[tap : tap + 64, :]
            v2b[u, :, v * 64 : v * 64 + 64] = w2[tap : tap + 64, :]

    lanes5 = iota((16, 192), 1)
    spread = one_hot((lanes5 - over(lanes5, 12) * 12) == iota((16, 192), 0))[0:12]
    wide[:, 0:192] = mm(w5[...], spread)
    lanes5 = iota((64, 192), 1)
    cell5 = over(lanes5, 12)
    col5 = over(cell5, 4)
    row5 = cell5 - col5 * 4
    for t in range(6):
        for position, v in enumerate(FINE_ORDER):
            value = jnp.zeros((64, 192), F32)
            for r in range(max(0, t - 3), min(2, t) + 1):
                for s in range(max(0, v - 3), min(2, v) + 1):
                    tap = (r * 3 + s) * 64
                    value = jnp.where(
                        (row5 == t - r) & (col5 == v - s), wide[tap : tap + 64, 0:192], value
                    )
            v5f[t, position * 64 : position * 64 + 64, :] = value.astype(BF)
    lanes6 = iota((16, 432), 1)
    spread = one_hot((lanes6 - over(lanes6, 12) * 12) == iota((16, 432), 0))[0:12]
    wide[...] = mm(w5[...], spread)
    lanes6 = iota((64, 432), 1)
    cell6 = over(lanes6, 12)
    col6 = over(cell6, 6)
    row6 = cell6 - col6 * 6
    for big_r in range(4):
        for big_c in range(4):
            value = jnp.zeros((64, 432), F32)
            for r in range(3):
                for s in range(3):
                    tap = (r * 3 + s) * 64
                    value = jnp.where(
                        (row6 == big_r + 2 - r) & (col6 == big_c + 2 - s),
                        wide[tap : tap + 64, :],
                        value,
                    )
            at = (big_r * 4 + big_c) * 64
            v5b[at : at + 64, :] = value.astype(BF)

    spot = iota((144, 256), 0)
    tap_col = over(spot, 48)
    want = spot - tap_col * 48 - 8 + tap_col - 1 + base_col
    first = jnp.clip(jnp.right_shift(base_col - 8, 7), 0, 2) * 128
    pick = one_hot((want == iota((144, 256), 1) + first) & (want >= 0) & (want < 512))
    tall = iota((448, 256), 0)
    tall_row = over(tall, 16) - 6 + base_row
    known = rows_in[...].reshape(448, 256).astype(F32)
    known = jnp.where((tall_row >= 0) & (tall_row < 128), known, 0.0).astype(BF)
    m_c1[...] = mm_nt(pick, known)
    t_c1[...] = jnp.zeros(t_c1.shape, F32)
    for i in range(-5, 21):
        for s in range(3):
            at = (i + 7) * STRIDE - 8
            t_c1[at : at + 48, s * 48 : s * 48 + 48] = m_c1[
                s * 48 : s * 48 + 48, (i + 5) * 16 : (i + 5) * 16 + 48
            ]
    x1[...] = t_c1[...].astype(BF)

    for ref in (t64, t3, t_g3, t_g4):
        ref[0:8, :] = jnp.zeros((8, ref.shape[1]), F32)
    for ref in (t3, t_g3, t_g4):
        ref[ref.shape[0] - 8 :, :] = jnp.zeros((8, ref.shape[1]), F32)
    for big_r in range(4):
        t4[big_r, 0:8, :] = jnp.zeros((8, 256), F32)
        t4[big_r, 1096:1104, :] = jnp.zeros((8, 256), F32)
    begin, count = start_of(3), count_of(3)
    for a in range(2):
        x4[a, begin - 48 : begin, :] = jnp.zeros((48, 256), BF)
        x4[a, begin + count : begin + count + 48, :] = jnp.zeros((48, 256), BF)

    def three_shifts(target, begin, count):
        t64[8 + count : 16 + count, :] = jnp.zeros((8, 64), F32)
        for s in range(3):
            target[begin : begin + count, s * 64 : s * 64 + 64] = t64[7 + s : 7 + s + count, :].astype(BF)

    begin, count = start_of(5), count_of(5)

    def one(at):
        z = mm(x1[slab(begin + at, 256), :], v1[...]) + b1[...]
        t64[pl.ds(pl.multiple_of(8 + at, 8), 256), :] = (
            jnp.tanh(z) * kept(begin + at, 256)
        )

    blocks(count, 256, one)
    three_shifts(x2, begin, count)

    begin2, count2 = start_of(4), count_of(4)

    def two(at):
        z = b2[...]
        for r in range(3):
            z = z + mm(x2[slab(begin2 + 48 * (r - 1) + at, 592), :], w2[192 * r : 192 * r + 192, :])
        t64[pl.ds(pl.multiple_of(8 + at, 8), 592), :] = jnp.tanh(z) * kept(begin2 + at, 592)

    blocks(count2, 592, two)
    three_shifts(x3, begin2, count2)

    begin3, count3 = start_of(3), count_of(3)

    def three(at):
        z = bias3
        for r in range(3):
            z = z + mm(x3[slab(begin3 + 48 * (r - 1) + at, 272), :], v3[192 * r : 192 * r + 192, :])
        t3[pl.ds(pl.multiple_of(8 + at, 8), 272), :] = jnp.tanh(z) * kept(begin3 + at, 272)

    blocks(count3, 272, three)
    for a in range(2):
        at = slice(begin3, begin3 + count3)
        x4[a, at, 0:128] = t3[8 : 8 + count3, a * 128 : a * 128 + 128].astype(BF)
        x4[a, at, 128:192] = t3[9 : 9 + count3, a * 128 : a * 128 + 64].astype(BF)
        x4[a, at, 192:256] = t3[7 : 7 + count3, a * 128 + 64 : a * 128 + 128].astype(BF)

    def four(at):
        for p in range(2):
            z = jnp.concatenate([bias4, bias4], axis=1)
            for r in range(3):
                a, d = ROW_SOURCE[p][r]
                z = z + mm(x4[a, slab(begin3 + 48 * d + at, 272), :], v4f[r])
            z = jnp.tanh(z) * kept(begin3 + at, 272)
            for half in range(2):
                for q in range(2):
                    t4[2 * p + half, pl.ds(pl.multiple_of(8 + at, 8), 272), q * 128 : q * 128 + 128] = z[
                        :, q * 256 + half * 128 : q * 256 + half * 128 + 128
                    ]

    blocks(count3, 272, four)
    for big_r in range(4):
        at = slice(begin3, begin3 + count3)
        x5[big_r, at, 0:256] = t4[big_r, 8 : 8 + count3, :].astype(BF)
        x5[big_r, at, 256:320] = t4[big_r, 9 : 9 + count3, 0:64].astype(BF)
        x5[big_r, at, 320:384] = t4[big_r, 7 : 7 + count3, 192:256].astype(BF)

    z = jnp.zeros((512, 192), F32)
    for t in range(6):
        big_r, d = FINE_SOURCE[t]
        z = z + mm(inner(x5.at[big_r], d, slice(0, 384)), v5f[t])
    z5[...] = z
    for i in range(16):
        for big_c in range(4):
            turned[big_c * 32 : big_c * 32 + 32, i * 48 : i * 48 + 48] = z5[
                i * 32 : i * 32 + 32, big_c * 48 : big_c * 48 + 48
            ]
    spot = iota((128, 128), 0)
    column = over(spot, 32)
    weave = one_hot(iota((128, 128), 1) == (spot - column * 32) * 4 + column)
    parts = three_parts(turned[...])
    lined[...] = (mm_tn(parts[2], weave) + mm_tn(parts[1], weave)) + mm_tn(parts[0], weave)
    for o in range(12):
        fine[o] = lined[pl.ds(o, 64, stride=12), :] + b5[0:1, o : o + 1]

    fine_row = iota((96, 128), 0) - 16 + gx * 64
    row_ok = (fine_row >= 0) & (fine_row < 512)
    for o in range(12):
        for third in range(3):
            value = cot_in[o, :, third * 128 : third * 128 + 128].astype(F32)
            ay[third, pl.ds(o, 96, stride=12), :] = jnp.where(row_ok, value, 0.0)
    spot = iota((288, 384), 0)
    tap_col = over(spot, 48)
    want = (spot - tap_col * 48 - 8) * 4 + tap_col - 1
    real = want + gy * 128
    pick = one_hot((iota((288, 384), 1) == want + 128) & (real >= 0) & (real < 2048))
    value = None
    for third in range(3):
        term = mm_nt(pick[:, third * 128 : third * 128 + 128], ay[third].astype(BF))
        value = term if value is None else value + term
    m_cot[...] = value
    t_cot[...] = jnp.zeros(t_cot.shape, F32)
    for i in range(-3, 19):
        for v in range(6):
            at = (i + 7) * STRIDE - 8
            t_cot[at : at + 48, v * 72 : v * 72 + 72] = m_cot[
                v * 48 : v * 48 + 48, (4 * i + 15) * 12 : (4 * i + 15) * 12 + 72
            ]
    xc[...] = t_cot[...].astype(BF)
    for big_c in range(4):
        at = (big_c + 1) * 72 + 12
        g5[:, big_c * 48 : big_c * 48 + 48] = inner(t_cot, 0, slice(at, at + 48)).astype(BF)

    lanes5 = iota((384, 192), 1)
    cell5 = over(lanes5, 12)
    col5 = over(cell5, 4)
    row5 = cell5 - col5 * 4
    for r in range(3):
        acc[r, 0:384, 0:192] = jnp.zeros((384, 192), F32)
    for t in range(6):
        big_r, d = FINE_SOURCE[t]
        z5[0:384, :] = mm_tn(inner(x5.at[big_r], d, slice(0, 384)), g5[...])
        for r in range(max(0, t - 3), min(2, t) + 1):
            acc[r, 0:384, 0:192] = jnp.where(row5 == t - r, z5[0:384, :], acc[r, 0:384, 0:192])
    fold_lane = iota((192, 128), 0)
    fold = one_hot((fold_lane - over(fold_lane, 12) * 12) + 64 == iota((192, 128), 1))
    col5 = col5[0:64]
    for r in range(3):
        for s in range(3):
            value = jnp.zeros((64, 192), F32)
            for big_c in range(4):
                position = FINE_ORDER.index(big_c + s)
                value = jnp.where(
                    col5 == big_c, acc[r, position * 64 : position * 64 + 64, 0:192], value
                )
            at = 2304 + (r * 3 + s) * 64
            pack[at : at + 64, :] = exact_right(value, fold)
    sums5 = jnp.sum(g5[...].astype(F32), axis=0, keepdims=True)
    fold_zero = one_hot((fold_lane - over(fold_lane, 12) * 12) == iota((192, 128), 1))
    pack[2988:3072, :] = jnp.zeros((84, 128), F32)
    pack[2997:2998, :] = exact_right(jnp.broadcast_to(sums5, (8, 192)), fold_zero)[0:1]

    def back_four(at):
        here = slab(begin3 + at, 272)
        keep = kept(begin3 + at, 272)
        for big_r in range(4):
            value = mm_nt(xc[here, :], v5b[big_r * 256 : big_r * 256 + 256, :])
            act = x5[big_r, here, 0:256].astype(F32)
            t_g4[pl.ds(pl.multiple_of(8 + at, 8), 272), big_r * 256 : big_r * 256 + 256] = (
                value * (1.0 - act * act) * keep
            )

    blocks(count3, 272, back_four)
    for p in range(2):
        at = slice(begin3, begin3 + count3)
        for half in range(2):
            src = (2 * p + half) * 256
            dst = half * 128
            for q in range(2):
                g4[p, at, q * 256 + dst : q * 256 + dst + 128] = t_g4[
                    8 : 8 + count3, src + q * 128 : src + q * 128 + 128
                ].astype(BF)
            g4[p, at, 512 + dst : 640 + dst] = t_g4[9 : 9 + count3, src : src + 128].astype(BF)
            g4[p, at, 768 + dst : 896 + dst] = t_g4[7 : 7 + count3, src + 128 : src + 256].astype(BF)

    sums4 = jnp.zeros((1, 256), F32)
    for p in range(2):
        value = inner(g4.at[p], 0, slice(0, 512))
        sums = jnp.sum(value.astype(F32), axis=0, keepdims=True)
        sums4 = sums4 + sums[:, 0:256] + sums[:, 256:512]
        for r in range(3):
            a, d = ROW_SOURCE[p][r]
            term = mm_tn(inner(x4.at[a], d, slice(0, 256)), value)
            if p == 0:
                acc[r, 0:256, :] = term
            else:
                acc[r, 0:256, :] = acc[r, 0:256, :] + term
    for r in range(3):
        for s in range(3):
            one_at = PAIR_ORDER.index(s) * 64
            two_at = PAIR_ORDER.index(s + 1) * 64
            value = acc[r, one_at : one_at + 64, 0:256] + acc[r, two_at : two_at + 64, 256:512]
            value = exact_right(value, to_natural)
            at = (r * 3 + s) * 64
            pack[at : at + 64, :] = value[:, 0:128]
            pack[576 + at : 640 + at, :] = value[:, 128:256]
    sums4 = exact_right(jnp.broadcast_to(sums4, (8, 256)), to_natural)
    pack[2992:2993, :] = sums4[0:1, 0:128]
    pack[2993:2994, :] = sums4[0:1, 128:256]

    begin2, count2 = start_of(2), count_of(2)

    def back_three(at):
        value = None
        for u in range(4):
            p, d = BACK_SOURCE[u]
            term = mm_nt(g4[p, slab(begin2 + 48 * d + at, 496), :], v4b[u])
            value = term if value is None else value + term
        here = slab(begin2 + at, 496)
        act = jnp.concatenate([x4[0, here, 0:128], x4[1, here, 0:128]], axis=1).astype(F32)
        t_g3[pl.ds(pl.multiple_of(8 + at, 8), 496), :] = (
            value * (1.0 - act * act) * kept(begin2 + at, 496)
        )

    blocks(count2, 496, back_three)
    for v in range(3):
        g3[begin2 : begin2 + count2, v * 256 : v * 256 + 256] = t_g3[7 + v : 7 + v + count2, :].astype(BF)

    value = inner(g3, 0, slice(256, 512))
    sums3 = jnp.sum(value.astype(F32), axis=0, keepdims=True)
    for r in range(3):
        term = mm_tn(inner(x3, r - 1, slice(0, 192)), value)
        term = exact_right(term, to_natural)
        at = 1152 + r * 192
        pack[at : at + 192, :] = term[:, 0:128]
        pack[576 + at : 768 + at, :] = term[:, 128:256]
    sums3 = exact_right(jnp.broadcast_to(sums3, (8, 256)), to_natural)
    pack[2994:2995, :] = sums3[0:1, 0:128]
    pack[2995:2996, :] = sums3[0:1, 128:256]

    begin1, count1 = start_of(1), count_of(1)

    def back_two(at):
        value = None
        for u in range(3):
            term = mm_nt(g3[slab(begin1 + 48 * (u - 1) + at, 448), :], v3b[u])
            value = term if value is None else value + term
        act = x3[slab(begin1 + at, 448), 64:128].astype(F32)
        t64[pl.ds(pl.multiple_of(8 + at, 8), 448), :] = (
            value * (1.0 - act * act) * kept(begin1 + at, 448)
        )

    blocks(count1, 448, back_two)
    three_shifts(g2, begin1, count1)

    value = inner(g2, 0, slice(64, 128))
    sums2 = jnp.sum(value.astype(F32), axis=0, keepdims=True)
    for r in range(3):
        at = 2304 + r * 192
        pack[at : at + 192, 0:64] = mm_tn(inner(x2, r - 1, slice(0, 192)), value)
    value = None
    for u in range(3):
        term = mm_nt(inner(g2, u - 1, slice(0, 192)), v2b[u])
        value = term if value is None else value + term
    act = inner(x2, 0, slice(64, 128)).astype(F32)
    value = (value * (1.0 - act * act)).astype(BF)
    sums1 = jnp.sum(value.astype(F32), axis=0, keepdims=True)
    pack[2996:2997, 0:64] = sums2
    pack[2996:2997, 64:128] = sums1
    term = mm_tn(inner(x1, 0, slice(0, 144)), value)
    for r in range(3):
        for s in range(3):
            at = 2880 + (r * 3 + s) * 12
            pack[at : at + 12, 0:64] = term[s * 48 + r * 16 : s * 48 + r * 16 + 12, :]
            pack[at : at + 12, 64:128] = jnp.zeros((12, 64), F32)


def compute_of(where_am_i, rows_in, cot_in, weights, biases):
    count3 = count_of(3) + 16
    scratch = (
        ((SPAN, 128), F32),
        ((SPAN, 144), F32),
        ((144, 448), F32),
        ((SPAN, 144), BF),
        ((count_of(5) + 16, 64), F32),
        ((SPAN, 192), BF),
        ((SPAN, 192), BF),
        ((count3, 256), F32),
        ((2, SPAN, 256), BF),
        ((4, count3, 256), F32),
        ((4, SPAN, 384), BF),
        ((3, 1152, 128), F32),
        ((SPAN, 432), F32),
        ((288, 1152), F32),
        ((SPAN, 432), BF),
        ((512, 192), BF),
        ((count3, 1024), F32),
        ((2, SPAN, 1024), BF),
        ((count_of(2) + 16, 256), F32),
        ((SPAN, 768), BF),
        ((SPAN, 192), BF),
        ((144, 64), BF),
        ((576, 256), BF),
        ((576, 256), BF),
        ((3, 256, 512), BF),
        ((4, 256, 1024), BF),
        ((3, 64, 768), BF),
        ((3, 64, 192), BF),
        ((6, 384, 192), BF),
        ((1024, 432), BF),
        ((3, 384, 512), F32),
        ((512, 192), F32),
        ((128, 768), F32),
        ((768, 128), F32),
        ((576, 432), F32),
    )
    vmem = pl.BlockSpec(memory_space=pltpu.VMEM)
    return pl.pallas_call(
        functools.partial(compute_kernel, where_am_i),
        out_shape=[
            jax.ShapeDtypeStruct((12, 64, 128), F32),
            jax.ShapeDtypeStruct((3072, 128), F32),
        ],
        in_specs=[vmem] * 12,
        out_specs=[vmem] * 2,
        scratch_shapes=[pltpu.VMEM(shape, kind) for shape, kind in scratch],
        compiler_params=pltpu.CompilerParams(vmem_limit_bytes=66000000),
        name="slab_compute",
    )(rows_in, cot_in, *weights, *biases)


def place():
    return lax.axis_index("gx"), lax.axis_index("gy")


def local(
    coarse,
    weight_one,
    weight_two,
    weight_three,
    weight_four,
    weight_five,
    bias_one,
    bias_two,
    bias_three,
    bias_four,
    bias_five,
    cotangent,
):
    row = jnp.pad(coarse.reshape(12, 512), ((0, 4), (0, 0)))
    rows_in, cot_in = gather_of(row, cotangent)
    weights = (
        weight_one.reshape(9, 12, 64),
        weight_two.reshape(576, 64),
        weight_three.reshape(576, 256),
        weight_four.reshape(576, 256),
        weight_five.reshape(576, 12),
    )
    biases = tuple(
        bias.reshape(1, -1) for bias in (bias_one, bias_two, bias_three, bias_four, bias_five)
    )
    fine, pack = compute_of(place, rows_in, cot_in, weights, biases)
    totals = totals_of(pack, float(16 * 128 * 512) ** -0.5)
    shapes = (
        weight_one.shape,
        weight_two.shape,
        weight_three.shape,
        weight_four.shape,
        weight_five.shape,
        (64,),
        (64,),
        (256,),
        (256,),
        (12,),
    )
    return (fine,) + tuple(total.reshape(shape) for total, shape in zip(totals, shapes))


def solution(mesh):
    in_specs = (
        P(None, ("gx", "gy"), None),
        P(),
        P(),
        P(),
        P(),
        P(),
        P(),
        P(),
        P(),
        P(),
        P(),
        P(None, "gx", "gy"),
    )
    out_specs = (P(None, "gx", "gy"), P(), P(), P(), P(), P(), P(), P(), P(), P(), P())
    return jax.shard_map(local, mesh=mesh, in_specs=in_specs, out_specs=out_specs, check_vma=False)
```

```python
import functools

import jax
import jax.numpy as jnp
from jax import lax
from jax.experimental import pallas as pl
from jax.experimental.pallas import tpu as pltpu
from jax.sharding import PartitionSpec as P

MESH_ID = pl.DeviceIdType.MESH


def coordinates():
    gx = lax.axis_index("gx")
    gy = lax.axis_index("gy")
    return (gx % 4, (gy // 2) % 4, (gx // 4) * 2 + gy // 8), gy % 2


def device_at(place, core):
    x, y, z = place
    return ((z // 2) * 4 + x, (z % 2) * 8 + y * 2 + core)


def along(place, axis, step):
    moved = list(place)
    moved[axis] = (place[axis] + step) % 4
    return moved


def rows_at(start, count):
    return pl.ds(pl.multiple_of(start, 8), count)


FLOWS = (
    (0, 512, (0, 1, 2)),
    (512, 512, (1, 2, 0)),
    (1024, 256, (2, 0, 1)),
    (1280, 512, (1, 2, 0)),
    (1792, 512, (2, 0, 1)),
    (2304, 256, (0, 1, 2)),
    (2560, 256, (0, 1, 2)),
    (2816, 256, (1, 2, 0)),
)
WHEN_READY = (0, 0, 0, 2, 2, 2, 3, 3)


class Flow:
    def __init__(self, number, place, core, pack, whole, base, rows, order):
        self.number, self.place, self.core = number, place, core
        self.pack, self.whole = pack, whole
        self.base, self.order = base, order
        self.sizes = (rows // 2, rows // 8, rows // 32)
        self.sent = []
        self.now = []

    def send(self, src, dst, sem, index, peer):
        copy = pltpu.make_async_remote_copy(
            src_ref=src,
            dst_ref=dst,
            send_sem=self.sems[sem].at[index],
            recv_sem=self.sems[sem + 1].at[index],
            device_id=peer,
            device_id_type=MESH_ID,
        )
        copy.start()
        self.sent.append(copy)
        self.now.append(copy)

    def arrive(self):
        for copy in self.now:
            copy.wait_recv()
        self.now = []

    def to_partner(self, src, dst, index):
        self.send(src, dst, 0, (self.number, index), device_at(self.place, 1 - self.core))

    def to_axis(self, turn, hop, views):
        axis = self.order[turn]
        for step in (1, 2, 3):
            src, dst = views(axis, step)
            self.send(
                src,
                dst,
                2,
                (self.number, hop, step - 1),
                device_at(along(self.place, axis, step), self.core),
            )

    def row(self, level):
        row = self.base + self.core * self.sizes[0]
        for turn in range(level):
            row = row + self.place[self.order[turn]] * self.sizes[turn + 1]
        return row

    def advance(self, stage):
        pair_in, pair_sum, in_a, sum_a, in_b, sum_b, in_c = self.refs
        half, fourth, small = self.sizes
        two, eight, many = self.base // 2, self.base // 8, self.base // 32
        if stage == 0:
            self.to_partner(
                self.pack.at[rows_at(self.base + (1 - self.core) * half, half)],
                pair_in.at[pl.ds(two, half)],
                0,
            )
            return
        self.arrive()
        if stage == 1:
            own = self.pack[rows_at(self.base + self.core * half, half), :]
            pair_sum[pl.ds(two, half), :] = own + pair_in[pl.ds(two, half), :]
            self.to_axis(
                0,
                0,
                lambda axis, step: (
                    pair_sum.at[rows_at(two + (self.place[axis] + step) % 4 * fourth, fourth)],
                    in_a.at[step - 1, pl.ds(eight, fourth)],
                ),
            )
        elif stage == 2:
            value = pair_sum[rows_at(two + self.place[self.order[0]] * fourth, fourth), :]
            for step in range(3):
                value = value + in_a[step, pl.ds(eight, fourth), :]
            sum_a[pl.ds(eight, fourth), :] = value
            self.to_axis(
                1,
                1,
                lambda axis, step: (
                    sum_a.at[rows_at(eight + (self.place[axis] + step) % 4 * small, small)],
                    in_b.at[step - 1, pl.ds(many, small)],
                ),
            )
        elif stage == 3:
            value = sum_a[rows_at(eight + self.place[self.order[1]] * small, small), :]
            for step in range(3):
                value = value + in_b[step, pl.ds(many, small), :]
            in_c[0, pl.ds(many, small), :] = value
            self.to_axis(
                2,
                2,
                lambda axis, step: (
                    in_c.at[0, pl.ds(many, small)],
                    in_c.at[step, pl.ds(many, small)],
                ),
            )
        elif stage == 4:
            here = self.place[self.order[2]]
            terms = [in_c[(here - other + 4) % 4, pl.ds(many, small), :] for other in range(4)]
            self.whole[rows_at(self.row(2), small), :] = (terms[0] + terms[1]) + (
                terms[2] + terms[3]
            )
            block = self.whole.at[rows_at(self.row(2), small)]
            self.to_axis(1, 3, lambda axis, step: (block, block))
        elif stage == 5:
            block = self.whole.at[rows_at(self.row(1), fourth)]
            self.to_axis(0, 4, lambda axis, step: (block, block))
        elif stage == 6:
            block = self.whole.at[rows_at(self.row(0), half)]
            self.to_partner(block, block, 1)

    def drain(self):
        for copy in self.sent:
            copy.wait_send()


def window(gy):
    return pl.multiple_of(jnp.clip(jnp.right_shift(gy * 32 - 8, 7), 0, 2) * 128, 128)


STRIDE = 48
ROWS = 30
SPAN = ROWS * STRIDE
BF = jnp.bfloat16
F32 = jnp.float32


def start_of(halo):
    return (7 - halo) * STRIDE - 16


def count_of(halo):
    return (16 + 2 * halo) * STRIDE + 32


def mm(lhs, rhs):
    return lax.dot_general(lhs, rhs, (((1,), (0,)), ((), ())), preferred_element_type=F32)


def mm_nt(lhs, rhs):
    return lax.dot_general(lhs, rhs, (((1,), (1,)), ((), ())), preferred_element_type=F32)


def mm_tn(lhs, rhs):
    return lax.dot_general(lhs, rhs, (((0,), (0,)), ((), ())), preferred_element_type=F32)


def iota(shape, dim):
    return lax.broadcasted_iota(jnp.int32, shape, dim)


def over(value, divisor):
    return lax.shift_right_logical(value * ((1 << 16) // divisor + 1), 16)


def one_hot(flag):
    return jnp.where(flag, 1.0, 0.0).astype(F32).astype(BF)


def three_parts(value):
    high = value.astype(BF)
    rest = value - high.astype(F32)
    middle = rest.astype(BF)
    return high, middle, (rest - middle.astype(F32)).astype(BF)


def exact_right(value, selector):
    parts = three_parts(value)
    return (mm(parts[2], selector) + mm(parts[1], selector)) + mm(parts[0], selector)


def blocks(total, chunk, body):
    def step(index, carry):
        body(pl.multiple_of(index * chunk, 16))
        return carry

    lax.fori_loop(0, total // chunk, step, 0)


def slab(start, count):
    if isinstance(start, int):
        return pl.ds(start, count)
    return pl.ds(pl.multiple_of(start, 16), count)


def inner(ref, shift, lanes):
    first = 7 + shift
    picked = [ref[(first + row) * STRIDE : (first + row) * STRIDE + 32, lanes] for row in range(16)]
    return jnp.concatenate(picked, axis=0)


ROW_SOURCE = (((1, -1), (0, 0), (1, 0)), ((0, 0), (1, 0), (0, 1)))
BACK_SOURCE = ((1, -1), (0, 0), (1, 0), (0, 1))
FINE_SOURCE = ((3, -1), (0, 0), (1, 0), (2, 0), (3, 0), (0, 1))
PAIR_ORDER = (1, 2, 3, 0)
FINE_ORDER = (1, 2, 3, 4, 5, 0)


def train_kernel(
    coarse,
    cot,
    w1,
    w2,
    w3,
    w4,
    w5,
    b1,
    b2,
    b3,
    b4,
    b5,
    fine,
    whole,
    rows_in,
    cot_in,
    known,
    pack,
    mask,
    t_c1,
    m_c1,
    x1,
    t64,
    x2,
    x3,
    t3,
    x4,
    t4,
    x5,
    ay,
    t_cot,
    m_cot,
    xc,
    g5,
    t_g4,
    g4,
    t_g3,
    g3,
    g2,
    v1,
    v3,
    v4,
    v4f,
    v4b,
    v3b,
    v2b,
    v5f,
    v5b,
    acc,
    z5,
    turned,
    lined,
    wide,
    pair_in,
    pair_sum,
    in_a,
    sum_a,
    in_b,
    sum_b,
    in_c,
    keep_sem,
    row_send,
    row_recv,
    far_send,
    far_recv,
    cot_send,
    cot_recv,
    pair_send,
    pair_recv,
    hop_send,
    hop_recv,
):
    gx = lax.axis_index("gx")
    gy = lax.axis_index("gy")

    def peer(step_x, step_y):
        return ((gx + step_x + 8) % 8, (gy + step_y + 16) % 16)

    barrier = pltpu.get_barrier_semaphore()
    for step_x in (-1, 0, 1):
        for step_y in range(16):
            if step_x != 0 or step_y != 0:
                pl.semaphore_signal(
                    barrier, inc=1, device_id=peer(step_x, step_y), device_id_type=MESH_ID
                )
    spot_now, core = coordinates()
    partner = device_at(spot_now, 1 - core)
    for axis in range(3):
        for step in (1, 2, 3):
            pl.semaphore_signal(
                barrier,
                inc=1,
                device_id=device_at(along(spot_now, axis, step), core),
                device_id_type=MESH_ID,
            )
    locals_ = [
        pltpu.make_async_copy(
            cot, cot_in.at[1, :, pl.ds(16, 64), :], keep_sem.at[0]
        ),
        pltpu.make_async_copy(
            coarse.at[:, pl.ds(window(gy), 256)], rows_in.at[6 + gy], keep_sem.at[1]
        ),
    ]
    for copy in locals_:
        copy.start()
    pl.semaphore_wait(barrier, 56)

    def remote(src, dst, send_sem, recv_sem, target):
        return pltpu.make_async_remote_copy(
            src_ref=src,
            dst_ref=dst,
            send_sem=send_sem,
            recv_sem=recv_sem,
            device_id=target,
            device_id_type=MESH_ID,
        )

    def row_copy(step, dst_row, send_sem, recv_sem, step_x):
        target = peer(step_x, step)
        return remote(
            coarse.at[:, pl.ds(window(target[1]), 256)],
            rows_in.at[dst_row],
            send_sem,
            recv_sem,
            target,
        )

    copies = []
    parts = ((16, 48, 0), (64, 0, 16), (16, 0, 80))
    for index_x, step_x in enumerate((1, 0, -1)):
        count, src_row, dst_row = parts[index_x]
        for index_y, step_y in enumerate((1, 0, -1)):
            if step_x == 0 and step_y == 0:
                continue
            copies.append(
                remote(
                    cot.at[:, pl.ds(src_row, count), :],
                    cot_in.at[index_y, :, pl.ds(dst_row, count), :],
                    cot_send.at[index_x, index_y],
                    cot_recv.at[index_x, index_y],
                    peer(step_x, step_y),
                )
            )
    for step in range(1, 16):
        copies.append(row_copy(step, 6 + gy, row_send.at[step], row_recv.at[step], 0))
    for copy in copies:
        copy.start()

    def far(step_x, dst_row, slot):
        return [
            row_copy(step, dst_row, far_send.at[step], far_recv.at[slot], step_x)
            for step in range(16)
        ]

    @pl.when(gy < 6)
    def _():
        for copy in far(-1, 22 + gy, 6 + gy):
            copy.start()

    @pl.when(gy >= 10)
    def _():
        for copy in far(1, gy - 10, gy - 10):
            copy.start()

    def await_rows():
        locals_[1].wait()
        for step in range(1, 16):
            row_copy(
                step, 6 + (gy - step + 16) % 16, row_send.at[step], row_recv.at[step], 0
            ).wait_recv()
        for slot in range(12):
            dst_row = slot if slot < 6 else 16 + slot
            row_copy(1, dst_row, far_send.at[0], far_recv.at[slot], 0).wait_recv()

    def await_cot():
        locals_[0].wait()
        for copy in copies[:8]:
            copy.wait_recv()

    def drain_gather():
        for copy in copies:
            copy.wait_send()

        @pl.when(gy < 6)
        def _():
            for copy in far(-1, 22 + gy, 6 + gy):
                copy.wait_send()

        @pl.when(gy >= 10)
        def _():
            for copy in far(1, gy - 10, gy - 10):
                copy.wait_send()


    flows = [
        Flow(number, spot_now, core, pack, whole, *FLOWS[number])
        for number in range(len(FLOWS))
    ]
    refs = (pair_in, pair_sum, in_a, sum_a, in_b, sum_b, in_c)
    sems = (pair_send, pair_recv, hop_send, hop_recv)
    for flow in flows:
        flow.refs = refs
        flow.sems = sems

    def progress(point):
        for number, flow in enumerate(flows):
            stage = point - WHEN_READY[number]
            if 0 <= stage < 8:
                flow.advance(stage)

    base_row = gx * 16
    base_col = gy * 32

    place = iota((SPAN, 128), 0)
    line = over(place, STRIDE)
    col = place - line * STRIDE
    left = jnp.where(col >= 40, 1, 0)
    row = line - 7 + left + base_row
    col = col - left * STRIDE + base_col
    ok = (row >= 0) & (row < 128) & (col >= 0) & (col < 512)
    mask[...] = jnp.where(ok, 1.0, 0.0)

    def kept(start, count):
        return mask[slab(start, count), 0:1]

    lane = iota((256, 256), 1)
    natural = iota((256, 256), 0)
    wanted = (lane - over(lane, 64) * 64) * 4 + over(lane, 64)
    to_phase = one_hot(natural == wanted)
    wanted_back = (natural - over(natural, 64) * 64) * 4 + over(natural, 64)
    to_natural = one_hot(lane == wanted_back)
    v3[...] = mm(w3[...], to_phase).astype(BF)
    v4[...] = mm(w4[...], to_phase).astype(BF)
    bias3 = exact_right(jnp.broadcast_to(b3[...], (8, 256)), to_phase)[0:1]
    bias4 = exact_right(jnp.broadcast_to(b4[...], (8, 256)), to_phase)[0:1]

    v1[...] = jnp.zeros(v1.shape, BF)
    for r in range(3):
        for s in range(3):
            v1[s * 48 + r * 16 : s * 48 + r * 16 + 12, :] = w1[r * 3 + s]
    for r in range(3):
        for position, c4 in enumerate(PAIR_ORDER):
            for q in range(2):
                s = c4 - q
                target = (slice(position * 64, position * 64 + 64), slice(q * 256, q * 256 + 256))
                if 0 <= s <= 2:
                    v4f[r, target[0], target[1]] = v4[(r * 3 + s) * 64 : (r * 3 + s) * 64 + 64, :]
                else:
                    v4f[r, target[0], target[1]] = jnp.zeros((64, 256), BF)
    for u in range(4):
        for a in range(2):
            for b in range(2):
                for position, v in enumerate(PAIR_ORDER):
                    r, s = a + 2 - u, b + 2 - v
                    at = (slice((2 * a + b) * 64, (2 * a + b) * 64 + 64),)
                    at = at + (slice(position * 256, position * 256 + 256),)
                    if 0 <= r <= 2 and 0 <= s <= 2:
                        tap = (r * 3 + s) * 64
                        v4b[u, at[0], at[1]] = v4[tap : tap + 64, :]
                    else:
                        v4b[u, at[0], at[1]] = jnp.zeros((64, 256), BF)
    for u in range(3):
        for v in range(3):
            tap = ((2 - u) * 3 + 2 - v) * 64
            v3b[u, :, v * 256 : v * 256 + 256] = v3[tap : tap + 64, :]
            v2b[u, :, v * 64 : v * 64 + 64] = w2[tap : tap + 64, :]

    def spread_out(width, group):
        lanes = iota((12, width), 1)
        spread = one_hot((lanes - over(lanes, group) * group) == iota((12, width), 0))
        for tap in range(9):
            wide[tap * 64 : tap * 64 + 64, 0:width] = mm_tn(w5[tap], spread)

    spread_out(256, 16)
    lanes5 = iota((64, 256), 1)
    cell5 = over(lanes5, 16)
    col5 = over(cell5, 4)
    row5 = cell5 - col5 * 4
    for t in range(6):
        for position, v in enumerate(FINE_ORDER):
            value = jnp.zeros((64, 256), F32)
            for r in range(max(0, t - 3), min(2, t) + 1):
                for s in range(max(0, v - 3), min(2, v) + 1):
                    tap = (r * 3 + s) * 64
                    value = jnp.where(
                        (row5 == t - r) & (col5 == v - s), wide[tap : tap + 64, 0:256], value
                    )
            v5f[t, position * 64 : position * 64 + 64, :] = value.astype(BF)
    spread_out(432, 12)
    lanes6 = iota((64, 432), 1)
    cell6 = over(lanes6, 12)
    col6 = over(cell6, 6)
    row6 = cell6 - col6 * 6
    for big_r in range(4):
        for big_c in range(4):
            value = jnp.zeros((64, 432), F32)
            for r in range(3):
                for s in range(3):
                    tap = (r * 3 + s) * 64
                    value = jnp.where(
                        (row6 == big_r + 2 - r) & (col6 == big_c + 2 - s),
                        wide[tap : tap + 64, :],
                        value,
                    )
            at = (big_r * 4 + big_c) * 64
            v5b[at : at + 64, :] = value.astype(BF)

    t64[0:8, :] = jnp.zeros((8, 64), F32)
    for ref in (t3, t4, t_g3, t_g4):
        for tile in range(ref.shape[0]):
            ref[tile, 0:8, :] = jnp.zeros((8, 128), F32)
            ref[tile, ref.shape[1] - 8 :, :] = jnp.zeros((8, 128), F32)
    begin, count = start_of(3), count_of(3)
    for a in range(2):
        x4[a, begin - 48 : begin, :] = jnp.zeros((48, 256), BF)
        x4[a, begin + count : begin + count + 48, :] = jnp.zeros((48, 256), BF)

    t_c1[...] = jnp.zeros(t_c1.shape, F32)
    t_cot[...] = jnp.zeros(t_cot.shape, F32)
    known[...] = jnp.zeros(known.shape, F32)
    for first, last in ((1152, 1280), (2432, 2560), (2816, 3072)):
        pack[first:last, :] = jnp.zeros((last - first, 128), F32)

    spot = iota((144, 256), 0)
    tap_col = over(spot, 48)
    want = spot - tap_col * 48 - 8 + tap_col - 1 + base_col
    first = jnp.clip(jnp.right_shift(base_col - 8, 7), 0, 2) * 128
    pick = one_hot((want == iota((144, 256), 1) + first) & (want >= 0) & (want < 512))
    await_rows()
    for k in range(28):
        present = (base_row - 6 + k >= 0) & (base_row - 6 + k < 128)
        known[k * 16 : k * 16 + 12, :] = jnp.where(present, rows_in[k].astype(F32), 0.0)
    m_c1[...] = mm_nt(pick, known[...].astype(BF))
    for i in range(-5, 21):
        for s in range(3):
            at = (i + 7) * STRIDE - 8
            t_c1[at : at + 48, s * 48 : s * 48 + 48] = m_c1[
                s * 48 : s * 48 + 48, (i + 5) * 16 : (i + 5) * 16 + 48
            ]
    x1[...] = t_c1[...].astype(BF)

    def three_shifts(target, begin, count):
        t64[8 + count : 16 + count, :] = jnp.zeros((8, 64), F32)
        for s in range(3):
            target[begin : begin + count, s * 64 : s * 64 + 64] = t64[7 + s : 7 + s + count, :].astype(BF)

    begin, count = start_of(5), count_of(5)

    def one(at):
        z = mm(x1[slab(begin + at, 256), :], v1[...]) + b1[...]
        t64[pl.ds(pl.multiple_of(8 + at, 8), 256), :] = (
            jnp.tanh(z) * kept(begin + at, 256)
        )

    blocks(count, 256, one)
    three_shifts(x2, begin, count)

    begin2, count2 = start_of(4), count_of(4)

    def two(at):
        z = b2[...]
        for r in range(3):
            z = z + mm(x2[slab(begin2 + 48 * (r - 1) + at, 592), :], w2[192 * r : 192 * r + 192, :])
        t64[pl.ds(pl.multiple_of(8 + at, 8), 592), :] = jnp.tanh(z) * kept(begin2 + at, 592)

    blocks(count2, 592, two)
    three_shifts(x3, begin2, count2)

    begin3, count3 = start_of(3), count_of(3)

    def three(at):
        z = bias3
        for r in range(3):
            z = z + mm(x3[slab(begin3 + 48 * (r - 1) + at, 272), :], v3[192 * r : 192 * r + 192, :])
        z = jnp.tanh(z) * kept(begin3 + at, 272)
        for a in range(2):
            t3[a, pl.ds(pl.multiple_of(8 + at, 8), 272), :] = z[:, a * 128 : a * 128 + 128]

    blocks(count3, 272, three)
    for a in range(2):
        at = slice(begin3, begin3 + count3)
        x4[a, at, 0:128] = t3[a, 8 : 8 + count3, :].astype(BF)
        x4[a, at, 128:192] = t3[a, 9 : 9 + count3, 0:64].astype(BF)
        x4[a, at, 192:256] = t3[a, 7 : 7 + count3, 64:128].astype(BF)

    def four(at):
        for p in range(2):
            z = jnp.concatenate([bias4, bias4], axis=1)
            for r in range(3):
                a, d = ROW_SOURCE[p][r]
                z = z + mm(x4[a, slab(begin3 + 48 * d + at, 272), :], v4f[r])
            z = jnp.tanh(z) * kept(begin3 + at, 272)
            for half in range(2):
                for q in range(2):
                    t4[4 * p + 2 * half + q, pl.ds(pl.multiple_of(8 + at, 8), 272), :] = z[
                        :, q * 256 + half * 128 : q * 256 + half * 128 + 128
                    ]

    blocks(count3, 272, four)
    for big_r in range(4):
        at = slice(begin3, begin3 + count3)
        x5[big_r, at, 0:128] = t4[2 * big_r, 8 : 8 + count3, :].astype(BF)
        x5[big_r, at, 128:256] = t4[2 * big_r + 1, 8 : 8 + count3, :].astype(BF)
        x5[big_r, at, 256:320] = t4[2 * big_r, 9 : 9 + count3, 0:64].astype(BF)
        x5[big_r, at, 320:384] = t4[2 * big_r + 1, 7 : 7 + count3, 64:128].astype(BF)

    await_cot()
    fine_row = iota((96, 128), 0) - 16 + gx * 64
    row_ok = (fine_row >= 0) & (fine_row < 512)
    for o in range(12):
        for third in range(3):
            value = cot_in[third, o].astype(F32)
            ay[third, pl.ds(o, 96, stride=12), :] = jnp.where(row_ok, value, 0.0)
    spot = iota((288, 384), 0)
    tap_col = over(spot, 48)
    want = (spot - tap_col * 48 - 8) * 4 + tap_col - 1
    real = want + gy * 128
    pick = one_hot((iota((288, 384), 1) == want + 128) & (real >= 0) & (real < 2048))
    value = None
    for third in range(3):
        term = mm_nt(pick[:, third * 128 : third * 128 + 128], ay[third].astype(BF))
        value = term if value is None else value + term
    m_cot[...] = value
    for i in range(-3, 19):
        for v in range(6):
            at = (i + 7) * STRIDE - 8
            t_cot[at : at + 48, v * 72 : v * 72 + 72] = m_cot[
                v * 48 : v * 48 + 48, (4 * i + 15) * 12 : (4 * i + 15) * 12 + 72
            ]
    xc[...] = t_cot[...].astype(BF)
    for big_c in range(4):
        at = (big_c + 1) * 72 + 12
        g5[:, big_c * 48 : big_c * 48 + 48] = inner(t_cot, 0, slice(at, at + 48)).astype(BF)

    lanes5 = iota((384, 192), 1)
    cell5 = over(lanes5, 12)
    col5 = over(cell5, 4)
    row5 = cell5 - col5 * 4
    for r in range(3):
        acc[r, 0:384, 0:192] = jnp.zeros((384, 192), F32)
    for t in range(6):
        big_r, d = FINE_SOURCE[t]
        z5[0:384, 0:192] = mm_tn(inner(x5.at[big_r], d, slice(0, 384)), g5[...])
        for r in range(max(0, t - 3), min(2, t) + 1):
            acc[r, 0:384, 0:192] = jnp.where(row5 == t - r, z5[0:384, 0:192], acc[r, 0:384, 0:192])
    fold_lane = iota((16, 192), 1)
    fold = one_hot((fold_lane - over(fold_lane, 12) * 12) == iota((16, 192), 0))
    col5 = col5[0:64]
    for r in range(3):
        for s in range(3):
            value = jnp.zeros((64, 192), F32)
            for big_c in range(4):
                position = FINE_ORDER.index(big_c + s)
                value = jnp.where(
                    col5 == big_c, acc[r, position * 64 : position * 64 + 64, 0:192], value
                )
            tap = r * 3 + s
            parts = three_parts(value)
            value = (mm_nt(fold, parts[2]) + mm_nt(fold, parts[1])) + mm_nt(fold, parts[0])
            at = 1152 + 16 * (tap // 2)
            pack[at : at + 16, 64 * (tap % 2) : 64 * (tap % 2) + 64] = value
    sums5 = jnp.sum(g5[...].astype(F32), axis=0, keepdims=True)
    fold_lane = iota((192, 128), 0)
    fold = one_hot((fold_lane - over(fold_lane, 12) * 12) == iota((192, 128), 1))
    pack[1234:1235, :] = exact_right(jnp.broadcast_to(sums5, (8, 192)), fold)[0:1]

    def back_four(at):
        here = slab(begin3 + at, 272)
        keep = kept(begin3 + at, 272)
        for big_r in range(4):
            value = mm_nt(xc[here, :], v5b[big_r * 256 : big_r * 256 + 256, :])
            act = x5[big_r, here, 0:256].astype(F32)
            value = value * (1.0 - act * act) * keep
            for q in range(2):
                t_g4[2 * big_r + q, pl.ds(pl.multiple_of(8 + at, 8), 272), :] = value[
                    :, q * 128 : q * 128 + 128
                ]

    blocks(count3, 272, back_four)
    for p in range(2):
        at = slice(begin3, begin3 + count3)
        for half in range(2):
            src = (2 * p + half) * 2
            dst = half * 128
            for q in range(2):
                g4[p, at, q * 256 + dst : q * 256 + dst + 128] = t_g4[
                    src + q, 8 : 8 + count3, :
                ].astype(BF)
            g4[p, at, 512 + dst : 640 + dst] = t_g4[src, 9 : 9 + count3, :].astype(BF)
            g4[p, at, 768 + dst : 896 + dst] = t_g4[src + 1, 7 : 7 + count3, :].astype(BF)

    sums4 = jnp.zeros((1, 256), F32)
    for p in range(2):
        value = inner(g4.at[p], 0, slice(0, 512))
        sums = jnp.sum(value.astype(F32), axis=0, keepdims=True)
        sums4 = sums4 + sums[:, 0:256] + sums[:, 256:512]
        for r in range(3):
            a, d = ROW_SOURCE[p][r]
            term = mm_tn(inner(x4.at[a], d, slice(0, 256)), value)
            if p == 0:
                acc[r, 0:256, :] = term
            else:
                acc[r, 0:256, :] = acc[r, 0:256, :] + term
    for r in range(3):
        for s in range(3):
            one_at = PAIR_ORDER.index(s) * 64
            two_at = PAIR_ORDER.index(s + 1) * 64
            value = acc[r, one_at : one_at + 64, 0:256] + acc[r, two_at : two_at + 64, 256:512]
            value = exact_right(value, to_natural)
            at = (r * 3 + s) * 64
            pack[at : at + 64, :] = value[:, 0:128]
            pack[576 + at : 640 + at, :] = value[:, 128:256]
    sums4 = exact_right(jnp.broadcast_to(sums4, (8, 256)), to_natural)
    pack[1232:1233, :] = sums4[0:1, 0:128]
    pack[1233:1234, :] = sums4[0:1, 128:256]

    progress(0)

    begin2, count2 = start_of(2), count_of(2)

    def back_three(at):
        value = None
        for u in range(4):
            p, d = BACK_SOURCE[u]
            term = mm_nt(g4[p, slab(begin2 + 48 * d + at, 496), :], v4b[u])
            value = term if value is None else value + term
        here = slab(begin2 + at, 496)
        act = jnp.concatenate([x4[0, here, 0:128], x4[1, here, 0:128]], axis=1).astype(F32)
        value = value * (1.0 - act * act) * kept(begin2 + at, 496)
        for a in range(2):
            t_g3[a, pl.ds(pl.multiple_of(8 + at, 8), 496), :] = value[:, a * 128 : a * 128 + 128]

    blocks(count2, 496, back_three)
    for v in range(3):
        for a in range(2):
            at = v * 256 + a * 128
            g3[begin2 : begin2 + count2, at : at + 128] = t_g3[a, 7 + v : 7 + v + count2, :].astype(BF)

    progress(1)

    value = inner(g3, 0, slice(256, 512))
    sums3 = jnp.sum(value.astype(F32), axis=0, keepdims=True)
    for r in range(3):
        term = mm_tn(inner(x3, r - 1, slice(0, 192)), value)
        term = exact_right(term, to_natural)
        at = 1280 + r * 192
        pack[at : at + 192, :] = term[:, 0:128]
        pack[576 + at : 768 + at, :] = term[:, 128:256]
    sums3 = exact_right(jnp.broadcast_to(sums3, (8, 256)), to_natural)
    pack[2432:2433, :] = sums3[0:1, 0:128]
    pack[2433:2434, :] = sums3[0:1, 128:256]

    progress(2)

    begin1, count1 = start_of(1), count_of(1)

    def back_two(at):
        value = None
        for u in range(3):
            term = mm_nt(g3[slab(begin1 + 48 * (u - 1) + at, 448), :], v3b[u])
            value = term if value is None else value + term
        act = x3[slab(begin1 + at, 448), 64:128].astype(F32)
        t64[pl.ds(pl.multiple_of(8 + at, 8), 448), :] = (
            value * (1.0 - act * act) * kept(begin1 + at, 448)
        )

    blocks(count1, 448, back_two)
    three_shifts(g2, begin1, count1)

    value = inner(g2, 0, slice(64, 128))
    sums2 = jnp.sum(value.astype(F32), axis=0, keepdims=True)
    for r in range(3):
        term = mm_tn(inner(x2, r - 1, slice(0, 192)), value)
        for s in range(3):
            tap = r * 3 + s
            at = 2560 + 64 * (tap // 2)
            pack[at : at + 64, 64 * (tap % 2) : 64 * (tap % 2) + 64] = term[s * 64 : s * 64 + 64, :]
    value = None
    for u in range(3):
        term = mm_nt(inner(g2, u - 1, slice(0, 192)), v2b[u])
        value = term if value is None else value + term
    act = inner(x2, 0, slice(64, 128)).astype(F32)
    value = (value * (1.0 - act * act)).astype(BF)
    sums1 = jnp.sum(value.astype(F32), axis=0, keepdims=True)
    pack[2960:2961, 0:64] = sums2
    pack[2960:2961, 64:128] = sums1
    term = mm_tn(inner(x1, 0, slice(0, 144)), value)
    for r in range(3):
        for s in range(3):
            tap = r * 3 + s
            at = 2880 + 16 * (tap // 2)
            pack[at : at + 16, 64 * (tap % 2) : 64 * (tap % 2) + 64] = term[
                s * 48 + r * 16 : s * 48 + r * 16 + 16, :
            ]
    progress(3)

    z = jnp.zeros((512, 256), F32)
    for t in range(6):
        big_r, d = FINE_SOURCE[t]
        z = z + mm(inner(x5.at[big_r], d, slice(0, 384)), v5f[t])
    z5[...] = z
    progress(4)
    for i in range(16):
        for big_c in range(4):
            turned[big_c * 32 : big_c * 32 + 32, i * 64 : i * 64 + 64] = z5[
                i * 32 : i * 32 + 32, big_c * 64 : big_c * 64 + 64
            ]
    progress(5)
    spot = iota((128, 128), 0)
    column = over(spot, 32)
    weave = one_hot(iota((128, 128), 1) == (spot - column * 32) * 4 + column)
    parts = three_parts(turned[...])
    lined[...] = (mm_tn(parts[2], weave) + mm_tn(parts[1], weave)) + mm_tn(parts[0], weave)
    progress(6)
    for o in range(12):
        fine[o] = lined[pl.ds(o, 64, stride=16), :] + b5[0:1, o : o + 1]
    for point in range(7, 11):
        progress(point)
    drain_gather()
    for flow in flows:
        flow.drain()


def train_of(coarse, cot, weights, biases):
    count3 = count_of(3) + 16
    scratch = (
        ((28, 12, 256), BF),
        ((3, 12, 96, 128), BF),
        ((448, 256), F32),
        ((3072, 128), F32),
        ((SPAN, 128), F32),
        ((SPAN, 144), F32),
        ((144, 448), F32),
        ((SPAN, 144), BF),
        ((count_of(5) + 16, 64), F32),
        ((SPAN, 192), BF),
        ((SPAN, 192), BF),
        ((2, count3, 128), F32),
        ((2, SPAN, 256), BF),
        ((8, count3, 128), F32),
        ((4, SPAN, 384), BF),
        ((3, 1152, 128), F32),
        ((SPAN, 432), F32),
        ((288, 1152), F32),
        ((SPAN, 432), BF),
        ((512, 192), BF),
        ((8, count3, 128), F32),
        ((2, SPAN, 1024), BF),
        ((2, count_of(2) + 16, 128), F32),
        ((SPAN, 768), BF),
        ((SPAN, 192), BF),
        ((144, 64), BF),
        ((576, 256), BF),
        ((576, 256), BF),
        ((3, 256, 512), BF),
        ((4, 256, 1024), BF),
        ((3, 64, 768), BF),
        ((3, 64, 192), BF),
        ((6, 384, 256), BF),
        ((1024, 432), BF),
        ((3, 384, 512), F32),
        ((512, 256), F32),
        ((128, 1024), F32),
        ((1024, 128), F32),
        ((576, 432), F32),
        ((1536, 128), F32),
        ((1536, 128), F32),
        ((3, 384, 128), F32),
        ((384, 128), F32),
        ((3, 96, 128), F32),
        ((96, 128), F32),
        ((4, 96, 128), F32),
    )
    counts = ((2,), (16,), (16,), (16,), (12,), (3, 3), (3, 3), (8, 2), (8, 2), (8, 5, 3), (8, 5, 3))
    vmem = pl.BlockSpec(memory_space=pltpu.VMEM)
    return pl.pallas_call(
        train_kernel,
        out_shape=[
            jax.ShapeDtypeStruct((12, 64, 128), F32),
            jax.ShapeDtypeStruct((3072, 128), F32),
        ],
        in_specs=[vmem] * 12,
        out_specs=[vmem] * 2,
        scratch_shapes=[pltpu.VMEM(shape, kind) for shape, kind in scratch]
        + [pltpu.SemaphoreType.DMA(shape) for shape in counts],
        compiler_params=pltpu.CompilerParams(
            vmem_limit_bytes=66000000, collective_id=0, has_side_effects=True
        ),
        name="train_tile",
    )(coarse, cot, *weights, *biases)


def unpack_kernel(
    scale, fine_in, whole, fine, out_w1, out_w2, out_w3, out_w4, out_w5, out_b1, out_b2, out_b3, out_b4, out_b5
):
    fine[...] = fine_in[...]
    for index, target in ((0, out_w4), (1280, out_w3)):
        target[:, 0:128] = whole[index : index + 576, :] * scale
        target[:, 128:256] = whole[index + 576 : index + 1152, :] * scale
    for tap in range(9):
        lanes = slice(64 * (tap % 2), 64 * (tap % 2) + 64)
        at = 2560 + 64 * (tap // 2)
        out_w2[tap * 64 : tap * 64 + 64, :] = whole[at : at + 64, lanes] * scale
        at = 16 * (tap // 2)
        out_w1[tap] = whole[2880 + at : 2892 + at, lanes] * scale
        out_w5[tap] = whole[1152 + at : 1164 + at, lanes] * scale
    for index, target in ((1232, out_b4), (2432, out_b3)):
        target[:, 0:128] = whole[index : index + 1, :] * scale
        target[:, 128:256] = whole[index + 1 : index + 2, :] * scale
    out_b2[...] = whole[2960:2961, 0:64] * scale
    out_b1[...] = whole[2960:2961, 64:128] * scale
    out_b5[...] = whole[1234:1235, 0:12] * scale


def unpack_of(fine, whole, scale):
    shapes = ((12, 64, 128), (9, 12, 64), (576, 64), (576, 256), (576, 256), (9, 12, 64))
    shapes = shapes + ((1, 64), (1, 64), (1, 256), (1, 256), (1, 12))
    vmem = pl.BlockSpec(memory_space=pltpu.VMEM)
    return pl.pallas_call(
        functools.partial(unpack_kernel, scale),
        out_shape=[jax.ShapeDtypeStruct(shape, F32) for shape in shapes],
        in_specs=[vmem] * 2,
        out_specs=[vmem] * 11,
        name="unpack",
    )(fine, whole)


def local(
    coarse,
    weight_one,
    weight_two,
    weight_three,
    weight_four,
    weight_five,
    bias_one,
    bias_two,
    bias_three,
    bias_four,
    bias_five,
    cotangent,
):
    weights = (
        weight_one.reshape(9, 12, 64),
        weight_two.reshape(576, 64),
        weight_three.reshape(576, 256),
        weight_four.reshape(576, 256),
        weight_five.transpose(0, 1, 3, 2).reshape(9, 12, 64),
    )
    biases = tuple(
        bias.reshape(1, -1) for bias in (bias_one, bias_two, bias_three, bias_four, bias_five)
    )
    fine, whole = train_of(coarse.reshape(12, 512), cotangent, weights, biases)
    results = unpack_of(fine, whole, float(16 * 128 * 512) ** -0.5)
    return (
        results[0],
        results[1].reshape(3, 3, 12, 64),
        results[2].reshape(3, 3, 64, 64),
        results[3].reshape(3, 3, 64, 256),
        results[4].reshape(3, 3, 64, 256),
        results[5].reshape(3, 3, 12, 64).transpose(0, 1, 3, 2),
    ) + tuple(result.reshape(-1) for result in results[6:])


def solution(mesh):
    in_specs = (
        P(None, ("gx", "gy"), None),
        P(),
        P(),
        P(),
        P(),
        P(),
        P(),
        P(),
        P(),
        P(),
        P(),
        P(None, "gx", "gy"),
    )
    out_specs = (P(None, "gx", "gy"), P(), P(), P(), P(), P(), P(), P(), P(), P(), P())
    return jax.shard_map(local, mesh=mesh, in_specs=in_specs, out_specs=out_specs, check_vma=False)
```

```python
import functools

import jax
import jax.numpy as jnp
from jax import lax
from jax.experimental import pallas as pl
from jax.experimental.pallas import tpu as pltpu
from jax.sharding import PartitionSpec as P

MESH_ID = pl.DeviceIdType.MESH


def coordinates():
    gx = lax.axis_index("gx")
    gy = lax.axis_index("gy")
    return (gx % 4, (gy // 2) % 4, (gx // 4) * 2 + gy // 8), gy % 2


def device_at(place, core):
    x, y, z = place
    return ((z // 2) * 4 + x, (z % 2) * 8 + y * 2 + core)


def along(place, axis, step):
    moved = list(place)
    moved[axis] = (place[axis] + step) % 4
    return moved


def rows_at(start, count):
    return pl.ds(pl.multiple_of(start, 16), count)


PACK = 2816
FLOWS = (
    (0, 512, (0, 1, 2), False),
    (512, 512, (1, 2, 0), False),
    (1024, 128, (2, 0, 1), True),
    (1152, 512, (1, 2, 0), False),
    (1664, 512, (2, 0, 1), False),
    (2176, 128, (0, 1, 2), True),
    (2304, 256, (0, 1, 2), True),
    (2560, 128, (1, 2, 0), True),
    (2688, 128, (2, 0, 1), True),
)
LAYER_FOUR, LAYER_THREE, OTHERS = (0, 1, 2), (3, 4, 5), (6, 7, 8)


def first_place(tap):
    if tap < 5:
        return 2560 + 12 * tap, slice(64, 128)
    at = 2624 + 16 * ((tap - 5) // 2)
    return at, slice(64 * ((tap - 5) % 2), 64 * ((tap - 5) % 2) + 64)


def last_place(tap):
    return 2656 + 12 * (tap // 2), slice(64 * (tap % 2), 64 * (tap % 2) + 64)


class Flow:
    def __init__(self, number, place, core, pack, whole, base, rows, order, short):
        self.number, self.place, self.core = number, place, core
        self.pack, self.whole = pack, whole
        self.base, self.order = base, order
        self.eighth, self.short = rows // 8, short
        before = [flow for flow in FLOWS[:number] if flow[3] == short]
        self.late_at = sum(flow[1] for flow in before) // (8 if short else 32)
        self.hop = 0
        self.sent = []
        self.now = []

    def send(self, src, dst, slot, peer):
        copy = pltpu.make_async_remote_copy(
            src_ref=src,
            dst_ref=dst,
            send_sem=self.sems[0].at[self.number, self.hop + slot],
            recv_sem=self.sems[1].at[self.number, self.hop + slot],
            device_id=peer,
            device_id_type=MESH_ID,
        )
        copy.start()
        self.sent.append(copy)
        self.now.append(copy)

    def arrive(self):
        for copy in self.now:
            copy.wait_recv()
        self.now = []

    def to_eight(self, views):
        axis = self.order[0]
        for other in range(2):
            for step in range(4):
                slot = other * 4 + step
                if slot > 0:
                    core = (self.core + other) % 2
                    spot = along(self.place, axis, step)
                    src, dst = views(slot, spot[axis] * 2 + core)
                    self.send(src, dst, slot, device_at(spot, core))
        self.hop += 8

    def to_axis(self, turn, views):
        axis = self.order[turn]
        for step in (1, 2, 3):
            src, dst = views(axis, step)
            self.send(src, dst, step, device_at(along(self.place, axis, step), self.core))
        self.hop += 4

    def advance(self, stage):
        in_a, sum_a, in_b, in_c, in_d = self.refs
        eighth, small = self.eighth, self.eighth // 4
        mine = self.place[self.order[0]] * 2 + self.core
        eight, many = self.base // 8, self.late_at
        row = self.base + mine * eighth
        if stage == 0:
            self.to_eight(
                lambda slot, chunk: (
                    self.pack.at[rows_at(self.base + chunk * eighth, eighth)],
                    in_a.at[slot, pl.ds(eight, eighth)],
                )
            )
            return
        self.arrive()
        if stage == 1:
            value = self.pack[rows_at(row, eighth), :]
            for slot in range(1, 8):
                value = value + in_a[slot, pl.ds(eight, eighth), :]
            if self.short:
                at = self.late_at
                in_d[0, pl.ds(at, eighth), :] = value
                for step_b in range(4):
                    for step_c in range(4):
                        slot = step_b * 4 + step_c
                        if slot > 0:
                            spot = along(self.place, self.order[1], step_b)
                            spot = along(spot, self.order[2], step_c)
                            self.send(
                                in_d.at[0, pl.ds(at, eighth)],
                                in_d.at[slot, pl.ds(at, eighth)],
                                slot,
                                device_at(spot, self.core),
                            )
                self.hop += 16
            else:
                sum_a[pl.ds(eight, eighth), :] = value
                self.to_axis(
                    1,
                    lambda axis, step: (
                        sum_a.at[rows_at(eight + (self.place[axis] + step) % 4 * small, small)],
                        in_b.at[step - 1, pl.ds(many, small)],
                    ),
                )
            return
        if self.short:
            if stage == 2:
                at = self.late_at
                total = None
                for spot_b in range(4):
                    for spot_c in range(4):
                        slot = (self.place[self.order[1]] - spot_b + 4) % 4 * 4
                        slot = slot + (self.place[self.order[2]] - spot_c + 4) % 4
                        term = in_d[slot, pl.ds(at, eighth), :]
                        total = term if total is None else total + term
                self.whole[rows_at(row, eighth), :] = total.astype(jnp.bfloat16)
                self.spread(row)
            return
        if stage == 2:
            value = sum_a[rows_at(eight + self.place[self.order[1]] * small, small), :]
            for step in range(3):
                value = value + in_b[step, pl.ds(many, small), :]
            in_c[0, pl.ds(many, small), :] = value
            self.to_axis(
                2,
                lambda axis, step: (
                    in_c.at[0, pl.ds(many, small)],
                    in_c.at[step, pl.ds(many, small)],
                ),
            )
        elif stage == 3:
            here = self.place[self.order[2]]
            terms = [in_c[(here - other + 4) % 4, pl.ds(many, small), :] for other in range(4)]
            at = row + self.place[self.order[1]] * small
            total = (terms[0] + terms[1]) + (terms[2] + terms[3])
            self.whole[rows_at(at, small), :] = total.astype(jnp.bfloat16)
            block = self.whole.at[rows_at(at, small)]
            self.to_axis(1, lambda axis, step: (block, block))
        elif stage == 4:
            self.spread(row)

    def spread(self, row):
        block = self.whole.at[rows_at(row, self.eighth)]
        self.to_eight(lambda slot, chunk: (block, block))

    def drain(self):
        for copy in self.sent:
            copy.wait_send()


def window(gy):
    return pl.multiple_of(jnp.clip(jnp.right_shift(gy * 32 - 8, 7), 0, 2) * 128, 128)


STRIDE = 48
ROWS = 30
SPAN = ROWS * STRIDE
BF = jnp.bfloat16
F32 = jnp.float32


def start_of(halo):
    return (7 - halo) * STRIDE - 16


def count_of(halo):
    return (16 + 2 * halo) * STRIDE + 32


def mm(lhs, rhs):
    return lax.dot_general(lhs, rhs, (((1,), (0,)), ((), ())), preferred_element_type=F32)


def mm_nt(lhs, rhs):
    return lax.dot_general(lhs, rhs, (((1,), (1,)), ((), ())), preferred_element_type=F32)


def mm_tn(lhs, rhs):
    return lax.dot_general(lhs, rhs, (((0,), (0,)), ((), ())), preferred_element_type=F32)


def iota(shape, dim):
    return lax.broadcasted_iota(jnp.int32, shape, dim)


def over(value, divisor):
    return lax.shift_right_logical(value * ((1 << 16) // divisor + 1), 16)


def one_hot(flag):
    return jnp.where(flag, 1.0, 0.0).astype(F32).astype(BF)


def three_parts(value):
    high = value.astype(BF)
    rest = value - high.astype(F32)
    middle = rest.astype(BF)
    return high, middle, (rest - middle.astype(F32)).astype(BF)


def exact_right(value, selector):
    parts = three_parts(value)
    return (mm(parts[2], selector) + mm(parts[1], selector)) + mm(parts[0], selector)


def blocks(total, chunk, body):
    def step(index, carry):
        body(pl.multiple_of(index * chunk, 16))
        return carry

    lax.fori_loop(0, total // chunk, step, 0)


def slab(start, count):
    if isinstance(start, int):
        return pl.ds(start, count)
    return pl.ds(pl.multiple_of(start, 16), count)


def inner(ref, shift, lanes):
    first = 7 + shift
    picked = [ref[(first + row) * STRIDE : (first + row) * STRIDE + 32, lanes] for row in range(16)]
    return jnp.concatenate(picked, axis=0)


ROW_SOURCE = (((1, -1), (0, 0), (1, 0)), ((0, 0), (1, 0), (0, 1)))
BACK_SOURCE = ((1, -1), (0, 0), (1, 0), (0, 1))
FINE_SOURCE = ((3, -1), (0, 0), (1, 0), (2, 0), (3, 0), (0, 1))
PAIR_ORDER = (1, 2, 3, 0)
FINE_ORDER = (1, 2, 3, 4, 5, 0)


def train_kernel(
    coarse,
    cot,
    w1,
    w2,
    w3,
    w4,
    w5,
    b1,
    b2,
    b3,
    b4,
    b5,
    fine,
    whole,
    rows_in,
    cot_in,
    known,
    pack,
    mask,
    t_c1,
    m_c1,
    x1,
    t64,
    x2,
    x3,
    t3,
    x4,
    t4,
    x5,
    ay,
    t_cot,
    m_cot,
    xc,
    g5,
    t_g4,
    g4,
    t_g3,
    g3,
    g2,
    v1,
    v3,
    v4,
    v4f,
    v4b,
    v3b,
    v2b,
    v5f,
    v5b,
    acc,
    z5,
    turned,
    lined,
    wide,
    in_a,
    sum_a,
    in_b,
    in_c,
    in_d,
    keep_sem,
    row_send,
    row_recv,
    far_send,
    far_recv,
    cot_send,
    cot_recv,
    hop_send,
    hop_recv,
):
    gx = lax.axis_index("gx")
    gy = lax.axis_index("gy")

    def peer(step_x, step_y):
        return ((gx + step_x + 8) % 8, (gy + step_y + 16) % 16)

    barrier = pltpu.get_barrier_semaphore()
    for step_x in (-1, 0, 1):
        for step_y in range(16):
            if step_x != 0 or step_y != 0:
                pl.semaphore_signal(
                    barrier, inc=1, device_id=peer(step_x, step_y), device_id_type=MESH_ID
                )
    spot_now, core = coordinates()
    partner = device_at(spot_now, 1 - core)
    helpers = [partner]
    for axis in range(3):
        for step in (1, 2, 3):
            near = along(spot_now, axis, step)
            helpers += [device_at(near, core), device_at(near, 1 - core)]
            for more in (1, 2, 3):
                helpers.append(device_at(along(near, (axis + 1) % 3, more), core))
    for helper in helpers:
        pl.semaphore_signal(barrier, inc=1, device_id=helper, device_id_type=MESH_ID)
    locals_ = [
        pltpu.make_async_copy(
            cot, cot_in.at[1, :, pl.ds(16, 64), :], keep_sem.at[0]
        ),
        pltpu.make_async_copy(
            coarse.at[:, pl.ds(window(gy), 256)], rows_in.at[6 + gy], keep_sem.at[1]
        ),
    ]
    for copy in locals_:
        copy.start()
    pl.semaphore_wait(barrier, 47 + len(helpers))

    def remote(src, dst, send_sem, recv_sem, target):
        return pltpu.make_async_remote_copy(
            src_ref=src,
            dst_ref=dst,
            send_sem=send_sem,
            recv_sem=recv_sem,
            device_id=target,
            device_id_type=MESH_ID,
        )

    def row_copy(step, dst_row, send_sem, recv_sem, step_x):
        target = peer(step_x, step)
        return remote(
            coarse.at[:, pl.ds(window(target[1]), 256)],
            rows_in.at[dst_row],
            send_sem,
            recv_sem,
            target,
        )

    cot_copies = []
    parts = ((16, 48, 0), (64, 0, 16), (16, 0, 80))
    for index_x, step_x in enumerate((1, 0, -1)):
        count, src_row, dst_row = parts[index_x]
        for index_y, step_y in enumerate((1, 0, -1)):
            if step_x == 0 and step_y == 0:
                continue
            cot_copies.append(
                remote(
                    cot.at[:, pl.ds(src_row, count), :],
                    cot_in.at[index_y, :, pl.ds(dst_row, count), :],
                    cot_send.at[index_x, index_y],
                    cot_recv.at[index_x, index_y],
                    peer(step_x, step_y),
                )
            )
    for copy in cot_copies:
        copy.start()

    copies = []
    for step in range(1, 16):
        copies.append(row_copy(step, 6 + gy, row_send.at[step], row_recv.at[step], 0))
    for copy in copies:
        copy.start()

    def far(step_x, dst_row, slot):
        return [
            row_copy(step, dst_row, far_send.at[step], far_recv.at[slot], step_x)
            for step in range(16)
        ]

    @pl.when(gy < 6)
    def _():
        for copy in far(-1, 22 + gy, 6 + gy):
            copy.start()

    @pl.when(gy >= 10)
    def _():
        for copy in far(1, gy - 10, gy - 10):
            copy.start()

    def await_rows():
        locals_[1].wait()
        for step in range(1, 16):
            row_copy(
                step, 6 + (gy - step + 16) % 16, row_send.at[step], row_recv.at[step], 0
            ).wait_recv()
        for slot in range(12):
            dst_row = slot if slot < 6 else 16 + slot
            row_copy(1, dst_row, far_send.at[0], far_recv.at[slot], 0).wait_recv()

    def await_cot():
        locals_[0].wait()
        for copy in cot_copies:
            copy.wait_recv()

    def drain_gather():
        for copy in copies + cot_copies:
            copy.wait_send()

        @pl.when(gy < 6)
        def _():
            for copy in far(-1, 22 + gy, 6 + gy):
                copy.wait_send()

        @pl.when(gy >= 10)
        def _():
            for copy in far(1, gy - 10, gy - 10):
                copy.wait_send()


    flows = [
        Flow(number, spot_now, core, pack, whole, *FLOWS[number])
        for number in range(len(FLOWS))
    ]
    refs = (in_a, sum_a, in_b, in_c, in_d)
    sems = (hop_send, hop_recv)
    for flow in flows:
        flow.refs = refs
        flow.sems = sems

    def progress(numbers, stage):
        for number in numbers:
            flows[number].advance(stage)

    base_row = gx * 16
    base_col = gy * 32

    place = iota((SPAN, 128), 0)
    line = over(place, STRIDE)
    col = place - line * STRIDE
    left = jnp.where(col >= 40, 1, 0)
    row = line - 7 + left + base_row
    col = col - left * STRIDE + base_col
    ok = (row >= 0) & (row < 128) & (col >= 0) & (col < 512)
    mask[...] = jnp.where(ok, 1.0, 0.0)

    def kept(start, count):
        return mask[slab(start, count), 0:1]

    lane = iota((256, 256), 1)
    natural = iota((256, 256), 0)
    wanted = (lane - over(lane, 64) * 64) * 4 + over(lane, 64)
    to_phase = one_hot(natural == wanted)
    wanted_back = (natural - over(natural, 64) * 64) * 4 + over(natural, 64)
    to_natural = one_hot(lane == wanted_back)
    v3[...] = mm(w3[...], to_phase).astype(BF)
    v4[...] = mm(w4[...], to_phase).astype(BF)
    bias3 = exact_right(jnp.broadcast_to(b3[...], (8, 256)), to_phase)[0:1]
    bias4 = exact_right(jnp.broadcast_to(b4[...], (8, 256)), to_phase)[0:1]

    v1[...] = jnp.zeros(v1.shape, BF)
    for r in range(3):
        for s in range(3):
            v1[s * 48 + r * 16 : s * 48 + r * 16 + 12, :] = w1[r * 3 + s]
    for r in range(3):
        for position, c4 in enumerate(PAIR_ORDER):
            for q in range(2):
                s = c4 - q
                target = (slice(position * 64, position * 64 + 64), slice(q * 256, q * 256 + 256))
                if 0 <= s <= 2:
                    v4f[r, target[0], target[1]] = v4[(r * 3 + s) * 64 : (r * 3 + s) * 64 + 64, :]
                else:
                    v4f[r, target[0], target[1]] = jnp.zeros((64, 256), BF)
    for u in range(4):
        for a in range(2):
            for b in range(2):
                for position, v in enumerate(PAIR_ORDER):
                    r, s = a + 2 - u, b + 2 - v
                    at = (slice((2 * a + b) * 64, (2 * a + b) * 64 + 64),)
                    at = at + (slice(position * 256, position * 256 + 256),)
                    if 0 <= r <= 2 and 0 <= s <= 2:
                        tap = (r * 3 + s) * 64
                        v4b[u, at[0], at[1]] = v4[tap : tap + 64, :]
                    else:
                        v4b[u, at[0], at[1]] = jnp.zeros((64, 256), BF)
    for u in range(3):
        for v in range(3):
            tap = ((2 - u) * 3 + 2 - v) * 64
            v3b[u, :, v * 256 : v * 256 + 256] = v3[tap : tap + 64, :]
            v2b[u, :, v * 64 : v * 64 + 64] = w2[tap : tap + 64, :]

    def spread_out(width, group):
        lanes = iota((12, width), 1)
        spread = one_hot((lanes - over(lanes, group) * group) == iota((12, width), 0))
        for tap in range(9):
            wide[tap * 64 : tap * 64 + 64, 0:width] = mm_tn(w5[tap], spread)

    spread_out(256, 16)
    lanes5 = iota((64, 256), 1)
    cell5 = over(lanes5, 16)
    col5 = over(cell5, 4)
    row5 = cell5 - col5 * 4
    for t in range(6):
        for position, v in enumerate(FINE_ORDER):
            value = jnp.zeros((64, 256), F32)
            for r in range(max(0, t - 3), min(2, t) + 1):
                for s in range(max(0, v - 3), min(2, v) + 1):
                    tap = (r * 3 + s) * 64
                    value = jnp.where(
                        (row5 == t - r) & (col5 == v - s), wide[tap : tap + 64, 0:256], value
                    )
            v5f[t, position * 64 : position * 64 + 64, :] = value.astype(BF)
    spread_out(432, 12)
    lanes6 = iota((64, 432), 1)
    cell6 = over(lanes6, 12)
    col6 = over(cell6, 6)
    row6 = cell6 - col6 * 6
    for big_r in range(4):
        for big_c in range(4):
            value = jnp.zeros((64, 432), F32)
            for r in range(3):
                for s in range(3):
                    tap = (r * 3 + s) * 64
                    value = jnp.where(
                        (row6 == big_r + 2 - r) & (col6 == big_c + 2 - s),
                        wide[tap : tap + 64, :],
                        value,
                    )
            at = (big_r * 4 + big_c) * 64
            v5b[at : at + 64, :] = value.astype(BF)

    t64[0:8, :] = jnp.zeros((8, 64), F32)
    for ref in (t3, t4, t_g3, t_g4):
        for tile in range(ref.shape[0]):
            ref[tile, 0:8, :] = jnp.zeros((8, 128), F32)
            ref[tile, ref.shape[1] - 8 :, :] = jnp.zeros((8, 128), F32)
    begin, count = start_of(3), count_of(3)
    for a in range(2):
        x4[a, begin - 48 : begin, :] = jnp.zeros((48, 256), BF)
        x4[a, begin + count : begin + count + 48, :] = jnp.zeros((48, 256), BF)

    t_c1[...] = jnp.zeros(t_c1.shape, F32)
    t_cot[...] = jnp.zeros(t_cot.shape, F32)
    known[...] = jnp.zeros(known.shape, F32)
    for first, last in ((2560, 2816),):
        pack[first:last, :] = jnp.zeros((last - first, 128), F32)

    await_cot()
    fine_row = iota((96, 128), 0) - 16 + gx * 64
    row_ok = (fine_row >= 0) & (fine_row < 512)
    for o in range(12):
        for third in range(3):
            value = cot_in[third, o].astype(F32)
            ay[third, pl.ds(o, 96, stride=12), :] = jnp.where(row_ok, value, 0.0)
    spot = iota((288, 384), 0)
    tap_col = over(spot, 48)
    want = (spot - tap_col * 48 - 8) * 4 + tap_col - 1
    real = want + gy * 128
    pick = one_hot((iota((288, 384), 1) == want + 128) & (real >= 0) & (real < 2048))
    value = None
    for third in range(3):
        term = mm_nt(pick[:, third * 128 : third * 128 + 128], ay[third].astype(BF))
        value = term if value is None else value + term
    m_cot[...] = value
    for i in range(-3, 19):
        for v in range(6):
            at = (i + 7) * STRIDE - 8
            t_cot[at : at + 48, v * 72 : v * 72 + 72] = m_cot[
                v * 48 : v * 48 + 48, (4 * i + 15) * 12 : (4 * i + 15) * 12 + 72
            ]
    xc[...] = t_cot[...].astype(BF)
    for big_c in range(4):
        at = (big_c + 1) * 72 + 12
        g5[:, big_c * 48 : big_c * 48 + 48] = inner(t_cot, 0, slice(at, at + 48)).astype(BF)

    spot = iota((144, 256), 0)
    tap_col = over(spot, 48)
    want = spot - tap_col * 48 - 8 + tap_col - 1 + base_col
    first = jnp.clip(jnp.right_shift(base_col - 8, 7), 0, 2) * 128
    pick = one_hot((want == iota((144, 256), 1) + first) & (want >= 0) & (want < 512))
    await_rows()
    for k in range(28):
        present = (base_row - 6 + k >= 0) & (base_row - 6 + k < 128)
        known[k * 16 : k * 16 + 12, :] = jnp.where(present, rows_in[k].astype(F32), 0.0)
    m_c1[...] = mm_nt(pick, known[...].astype(BF))
    for i in range(-5, 21):
        for s in range(3):
            at = (i + 7) * STRIDE - 8
            t_c1[at : at + 48, s * 48 : s * 48 + 48] = m_c1[
                s * 48 : s * 48 + 48, (i + 5) * 16 : (i + 5) * 16 + 48
            ]
    x1[...] = t_c1[...].astype(BF)

    def three_shifts(target, begin, count):
        t64[8 + count : 16 + count, :] = jnp.zeros((8, 64), F32)
        for s in range(3):
            target[begin : begin + count, s * 64 : s * 64 + 64] = t64[7 + s : 7 + s + count, :].astype(BF)

    begin, count = start_of(5), count_of(5)

    def one(at):
        z = mm(x1[slab(begin + at, 256), :], v1[...]) + b1[...]
        t64[pl.ds(pl.multiple_of(8 + at, 8), 256), :] = (
            jnp.tanh(z) * kept(begin + at, 256)
        )

    blocks(count, 256, one)
    three_shifts(x2, begin, count)

    begin2, count2 = start_of(4), count_of(4)

    def two(at):
        z = b2[...]
        for r in range(3):
            z = z + mm(x2[slab(begin2 + 48 * (r - 1) + at, 592), :], w2[192 * r : 192 * r + 192, :])
        t64[pl.ds(pl.multiple_of(8 + at, 8), 592), :] = jnp.tanh(z) * kept(begin2 + at, 592)

    blocks(count2, 592, two)
    three_shifts(x3, begin2, count2)

    begin3, count3 = start_of(3), count_of(3)

    def three(at):
        z = bias3
        for r in range(3):
            z = z + mm(x3[slab(begin3 + 48 * (r - 1) + at, 272), :], v3[192 * r : 192 * r + 192, :])
        z = jnp.tanh(z) * kept(begin3 + at, 272)
        for a in range(2):
            t3[a, pl.ds(pl.multiple_of(8 + at, 8), 272), :] = z[:, a * 128 : a * 128 + 128]

    blocks(count3, 272, three)
    for a in range(2):
        at = slice(begin3, begin3 + count3)
        x4[a, at, 0:128] = t3[a, 8 : 8 + count3, :].astype(BF)
        x4[a, at, 128:192] = t3[a, 9 : 9 + count3, 0:64].astype(BF)
        x4[a, at, 192:256] = t3[a, 7 : 7 + count3, 64:128].astype(BF)

    def four(at):
        for p in range(2):
            z = jnp.concatenate([bias4, bias4], axis=1)
            for r in range(3):
                a, d = ROW_SOURCE[p][r]
                z = z + mm(x4[a, slab(begin3 + 48 * d + at, 272), :], v4f[r])
            z = jnp.tanh(z) * kept(begin3 + at, 272)
            for half in range(2):
                for q in range(2):
                    t4[4 * p + 2 * half + q, pl.ds(pl.multiple_of(8 + at, 8), 272), :] = z[
                        :, q * 256 + half * 128 : q * 256 + half * 128 + 128
                    ]

    blocks(count3, 272, four)
    for big_r in range(4):
        at = slice(begin3, begin3 + count3)
        x5[big_r, at, 0:128] = t4[2 * big_r, 8 : 8 + count3, :].astype(BF)
        x5[big_r, at, 128:256] = t4[2 * big_r + 1, 8 : 8 + count3, :].astype(BF)
        x5[big_r, at, 256:320] = t4[2 * big_r, 9 : 9 + count3, 0:64].astype(BF)
        x5[big_r, at, 320:384] = t4[2 * big_r + 1, 7 : 7 + count3, 64:128].astype(BF)

    def back_four(at):
        here = slab(begin3 + at, 272)
        keep = kept(begin3 + at, 272)
        for big_r in range(4):
            value = mm_nt(xc[here, :], v5b[big_r * 256 : big_r * 256 + 256, :])
            act = x5[big_r, here, 0:256].astype(F32)
            value = value * (1.0 - act * act) * keep
            for q in range(2):
                t_g4[2 * big_r + q, pl.ds(pl.multiple_of(8 + at, 8), 272), :] = value[
                    :, q * 128 : q * 128 + 128
                ]

    blocks(count3, 272, back_four)
    for p in range(2):
        at = slice(begin3, begin3 + count3)
        for half in range(2):
            src = (2 * p + half) * 2
            dst = half * 128
            for q in range(2):
                g4[p, at, q * 256 + dst : q * 256 + dst + 128] = t_g4[
                    src + q, 8 : 8 + count3, :
                ].astype(BF)
            g4[p, at, 512 + dst : 640 + dst] = t_g4[src, 9 : 9 + count3, :].astype(BF)
            g4[p, at, 768 + dst : 896 + dst] = t_g4[src + 1, 7 : 7 + count3, :].astype(BF)

    sums4 = jnp.zeros((1, 256), F32)
    for p in range(2):
        value = inner(g4.at[p], 0, slice(0, 512))
        sums = jnp.sum(value.astype(F32), axis=0, keepdims=True)
        sums4 = sums4 + sums[:, 0:256] + sums[:, 256:512]
        for r in range(3):
            a, d = ROW_SOURCE[p][r]
            term = mm_tn(inner(x4.at[a], d, slice(0, 256)), value)
            if p == 0:
                acc[r, 0:256, :] = term
            else:
                acc[r, 0:256, :] = acc[r, 0:256, :] + term
    for r in range(3):
        for s in range(3):
            one_at = PAIR_ORDER.index(s) * 64
            two_at = PAIR_ORDER.index(s + 1) * 64
            value = acc[r, one_at : one_at + 64, 0:256] + acc[r, two_at : two_at + 64, 256:512]
            value = exact_right(value, to_natural)
            at = (r * 3 + s) * 64
            pack[at : at + 64, :] = value[:, 0:128]
            pack[576 + at : 640 + at, :] = value[:, 128:256]
    sums4 = exact_right(jnp.broadcast_to(sums4, (8, 256)), to_natural)
    pack[2720:2721, :] = sums4[0:1, 0:128]
    pack[2721:2722, :] = sums4[0:1, 128:256]

    progress(LAYER_FOUR, 0)

    begin2, count2 = start_of(2), count_of(2)

    def back_three(at):
        value = None
        for u in range(4):
            p, d = BACK_SOURCE[u]
            term = mm_nt(g4[p, slab(begin2 + 48 * d + at, 496), :], v4b[u])
            value = term if value is None else value + term
        here = slab(begin2 + at, 496)
        act = jnp.concatenate([x4[0, here, 0:128], x4[1, here, 0:128]], axis=1).astype(F32)
        value = value * (1.0 - act * act) * kept(begin2 + at, 496)
        for a in range(2):
            t_g3[a, pl.ds(pl.multiple_of(8 + at, 8), 496), :] = value[:, a * 128 : a * 128 + 128]

    blocks(count2, 496, back_three)
    for v in range(3):
        for a in range(2):
            at = v * 256 + a * 128
            g3[begin2 : begin2 + count2, at : at + 128] = t_g3[a, 7 + v : 7 + v + count2, :].astype(BF)

    value = inner(g3, 0, slice(256, 512))
    sums3 = jnp.sum(value.astype(F32), axis=0, keepdims=True)
    for r in range(3):
        term = mm_tn(inner(x3, r - 1, slice(0, 192)), value)
        term = exact_right(term, to_natural)
        at = 1152 + r * 192
        pack[at : at + 192, :] = term[:, 0:128]
        pack[576 + at : 768 + at, :] = term[:, 128:256]
    sums3 = exact_right(jnp.broadcast_to(sums3, (8, 256)), to_natural)
    pack[2722:2723, :] = sums3[0:1, 0:128]
    pack[2723:2724, :] = sums3[0:1, 128:256]

    progress(LAYER_THREE, 0)
    progress(LAYER_FOUR, 1)

    lanes5 = iota((384, 192), 1)
    cell5 = over(lanes5, 12)
    col5 = over(cell5, 4)
    row5 = cell5 - col5 * 4
    for r in range(3):
        acc[r, 0:384, 0:192] = jnp.zeros((384, 192), F32)
    for t in range(6):
        big_r, d = FINE_SOURCE[t]
        z5[0:384, 0:192] = mm_tn(inner(x5.at[big_r], d, slice(0, 384)), g5[...])
        for r in range(max(0, t - 3), min(2, t) + 1):
            acc[r, 0:384, 0:192] = jnp.where(row5 == t - r, z5[0:384, 0:192], acc[r, 0:384, 0:192])
    fold_lane = iota((16, 192), 1)
    fold = one_hot((fold_lane - over(fold_lane, 12) * 12) == iota((16, 192), 0))
    col5 = col5[0:64]
    for r in range(3):
        for s in range(3):
            value = jnp.zeros((64, 192), F32)
            for big_c in range(4):
                position = FINE_ORDER.index(big_c + s)
                value = jnp.where(
                    col5 == big_c, acc[r, position * 64 : position * 64 + 64, 0:192], value
                )
            tap = r * 3 + s
            parts = three_parts(value)
            value = (mm_nt(fold, parts[2]) + mm_nt(fold, parts[1])) + mm_nt(fold, parts[0])
            at, lanes = last_place(tap)
            pack[at : at + 12, lanes] = value[0:12]
    sums5 = jnp.sum(g5[...].astype(F32), axis=0, keepdims=True)
    fold_lane = iota((192, 128), 0)
    fold = one_hot((fold_lane - over(fold_lane, 12) * 12) == iota((192, 128), 1))
    pack[2725:2726, :] = exact_right(jnp.broadcast_to(sums5, (8, 192)), fold)[0:1]

    begin1, count1 = start_of(1), count_of(1)

    def back_two(at):
        value = None
        for u in range(3):
            term = mm_nt(g3[slab(begin1 + 48 * (u - 1) + at, 448), :], v3b[u])
            value = term if value is None else value + term
        act = x3[slab(begin1 + at, 448), 64:128].astype(F32)
        t64[pl.ds(pl.multiple_of(8 + at, 8), 448), :] = (
            value * (1.0 - act * act) * kept(begin1 + at, 448)
        )

    blocks(count1, 448, back_two)
    three_shifts(g2, begin1, count1)

    progress(LAYER_FOUR, 2)
    progress(LAYER_THREE, 1)

    value = inner(g2, 0, slice(64, 128))
    sums2 = jnp.sum(value.astype(F32), axis=0, keepdims=True)
    for r in range(3):
        term = mm_tn(inner(x2, r - 1, slice(0, 192)), value)
        for s in range(3):
            tap = r * 3 + s
            at = 2304 + 64 * (tap // 2)
            pack[at : at + 64, 64 * (tap % 2) : 64 * (tap % 2) + 64] = term[s * 64 : s * 64 + 64, :]
    value = None
    for u in range(3):
        term = mm_nt(inner(g2, u - 1, slice(0, 192)), v2b[u])
        value = term if value is None else value + term
    act = inner(x2, 0, slice(64, 128)).astype(F32)
    value = (value * (1.0 - act * act)).astype(BF)
    sums1 = jnp.sum(value.astype(F32), axis=0, keepdims=True)
    pack[2724:2725, 0:64] = sums2
    pack[2724:2725, 64:128] = sums1
    term = mm_tn(inner(x1, 0, slice(0, 144)), value)
    for r in range(3):
        for s in range(3):
            tap = r * 3 + s
            at, lanes = first_place(tap)
            pack[at : at + 12, lanes] = term[s * 48 + r * 16 : s * 48 + r * 16 + 12, :]
    progress(OTHERS, 0)

    z = jnp.zeros((512, 256), F32)
    for t in range(6):
        big_r, d = FINE_SOURCE[t]
        z = z + mm(inner(x5.at[big_r], d, slice(0, 384)), v5f[t])
    z5[...] = z
    progress(LAYER_FOUR, 3)
    progress(LAYER_THREE, 2)
    for i in range(16):
        for big_c in range(4):
            turned[big_c * 32 : big_c * 32 + 32, i * 64 : i * 64 + 64] = z5[
                i * 32 : i * 32 + 32, big_c * 64 : big_c * 64 + 64
            ]
    progress(OTHERS, 1)
    spot = iota((128, 128), 0)
    column = over(spot, 32)
    weave = one_hot(iota((128, 128), 1) == (spot - column * 32) * 4 + column)
    parts = three_parts(turned[...])
    lined[...] = (mm_tn(parts[2], weave) + mm_tn(parts[1], weave)) + mm_tn(parts[0], weave)
    progress(LAYER_FOUR, 4)
    progress(LAYER_THREE, 3)
    for o in range(12):
        fine[o] = lined[pl.ds(o, 64, stride=16), :] + b5[0:1, o : o + 1]
    progress(OTHERS, 2)
    progress(LAYER_FOUR, 5)
    progress(LAYER_THREE, 4)
    progress(OTHERS, 3)
    progress(LAYER_THREE, 5)
    drain_gather()
    for flow in flows:
        flow.drain()


def train_of(coarse, cot, weights, biases):
    count3 = count_of(3) + 16
    scratch = (
        ((28, 12, 256), BF),
        ((3, 12, 96, 128), BF),
        ((448, 256), F32),
        ((PACK, 128), F32),
        ((SPAN, 128), F32),
        ((SPAN, 144), F32),
        ((144, 448), F32),
        ((SPAN, 144), BF),
        ((count_of(5) + 16, 64), F32),
        ((SPAN, 192), BF),
        ((SPAN, 192), BF),
        ((2, count3, 128), F32),
        ((2, SPAN, 256), BF),
        ((8, count3, 128), F32),
        ((4, SPAN, 384), BF),
        ((3, 1152, 128), F32),
        ((SPAN, 432), F32),
        ((288, 1152), F32),
        ((SPAN, 432), BF),
        ((512, 192), BF),
        ((8, count3, 128), F32),
        ((2, SPAN, 1024), BF),
        ((2, count_of(2) + 16, 128), F32),
        ((SPAN, 768), BF),
        ((SPAN, 192), BF),
        ((144, 64), BF),
        ((576, 256), BF),
        ((576, 256), BF),
        ((3, 256, 512), BF),
        ((4, 256, 1024), BF),
        ((3, 64, 768), BF),
        ((3, 64, 192), BF),
        ((6, 384, 256), BF),
        ((1024, 432), BF),
        ((3, 384, 512), F32),
        ((512, 256), F32),
        ((128, 1024), F32),
        ((1024, 128), F32),
        ((576, 432), F32),
        ((8, PACK // 8, 128), F32),
        ((PACK // 8, 128), F32),
        ((3, 64, 128), F32),
        ((4, 64, 128), F32),
        ((16, 96, 128), F32),
    )
    counts = ((2,), (16,), (16,), (16,), (12,), (3, 3), (3, 3), (9, 32), (9, 32))
    vmem = pl.BlockSpec(memory_space=pltpu.VMEM)
    return pl.pallas_call(
        train_kernel,
        out_shape=[
            jax.ShapeDtypeStruct((12, 64, 128), F32),
            jax.ShapeDtypeStruct((PACK, 128), BF),
        ],
        in_specs=[vmem] * 12,
        out_specs=[vmem] * 2,
        scratch_shapes=[pltpu.VMEM(shape, kind) for shape, kind in scratch]
        + [pltpu.SemaphoreType.DMA(shape) for shape in counts],
        compiler_params=pltpu.CompilerParams(
            vmem_limit_bytes=66000000, collective_id=0, has_side_effects=True
        ),
        name="train_tile",
    )(coarse, cot, *weights, *biases)


def unpack_kernel(
    scale, fine_in, whole_in, fine, out_w1, out_w2, out_w3, out_w4, out_w5, out_b1, out_b2, out_b3, out_b4, out_b5, whole
):
    fine[...] = fine_in[...]
    whole[...] = whole_in[...].astype(F32) * scale
    for index, target in ((0, out_w4), (1152, out_w3)):
        target[:, 0:128] = whole[index : index + 576, :]
        target[:, 128:256] = whole[index + 576 : index + 1152, :]
    for tap in range(9):
        lanes = slice(64 * (tap % 2), 64 * (tap % 2) + 64)
        at = 2304 + 64 * (tap // 2)
        out_w2[tap * 64 : tap * 64 + 64, :] = whole[at : at + 64, lanes]
        first, side = first_place(tap)
        out_w1[tap] = whole[first : first + 12, side]
        first, side = last_place(tap)
        out_w5[tap] = whole[first : first + 12, side]
    for index, target in ((2720, out_b4), (2722, out_b3)):
        target[:, 0:128] = whole[index : index + 1, :]
        target[:, 128:256] = whole[index + 1 : index + 2, :]
    out_b2[...] = whole[2724:2725, 0:64]
    out_b1[...] = whole[2724:2725, 64:128]
    out_b5[...] = whole[2725:2726, 0:12]


def unpack_of(fine, whole, scale):
    shapes = ((12, 64, 128), (9, 12, 64), (576, 64), (576, 256), (576, 256), (9, 12, 64))
    shapes = shapes + ((1, 64), (1, 64), (1, 256), (1, 256), (1, 12))
    vmem = pl.BlockSpec(memory_space=pltpu.VMEM)
    return pl.pallas_call(
        functools.partial(unpack_kernel, scale),
        out_shape=[jax.ShapeDtypeStruct(shape, F32) for shape in shapes],
        in_specs=[vmem] * 2,
        out_specs=[vmem] * 11,
        scratch_shapes=[pltpu.VMEM((PACK, 128), F32)],
        name="unpack",
    )(fine, whole)


def local(
    coarse,
    weight_one,
    weight_two,
    weight_three,
    weight_four,
    weight_five,
    bias_one,
    bias_two,
    bias_three,
    bias_four,
    bias_five,
    cotangent,
):
    weights = (
        weight_one.reshape(9, 12, 64),
        weight_two.reshape(576, 64),
        weight_three.reshape(576, 256),
        weight_four.reshape(576, 256),
        weight_five.transpose(0, 1, 3, 2).reshape(9, 12, 64),
    )
    biases = tuple(
        bias.reshape(1, -1) for bias in (bias_one, bias_two, bias_three, bias_four, bias_five)
    )
    fine, whole = train_of(coarse.reshape(12, 512), cotangent, weights, biases)
    results = unpack_of(fine, whole, float(16 * 128 * 512) ** -0.5)
    return (
        results[0],
        results[1].reshape(3, 3, 12, 64),
        results[2].reshape(3, 3, 64, 64),
        results[3].reshape(3, 3, 64, 256),
        results[4].reshape(3, 3, 64, 256),
        results[5].reshape(3, 3, 12, 64).transpose(0, 1, 3, 2),
    ) + tuple(result.reshape(-1) for result in results[6:])


def solution(mesh):
    in_specs = (
        P(None, ("gx", "gy"), None),
        P(),
        P(),
        P(),
        P(),
        P(),
        P(),
        P(),
        P(),
        P(),
        P(),
        P(None, "gx", "gy"),
    )
    out_specs = (P(None, "gx", "gy"), P(), P(), P(), P(), P(), P(), P(), P(), P(), P())
    return jax.shard_map(local, mesh=mesh, in_specs=in_specs, out_specs=out_specs, check_vma=False)
```

```python
import functools

import jax
import jax.numpy as jnp
from jax import lax
from jax.experimental import pallas as pl
from jax.experimental.pallas import tpu as pltpu
from jax.sharding import PartitionSpec as P

MESH_ID = pl.DeviceIdType.MESH


def coordinates():
    gx = lax.axis_index("gx")
    gy = lax.axis_index("gy")
    return (gx % 4, (gy // 2) % 4, (gx // 4) * 2 + gy // 8), gy % 2


def device_at(place, core):
    x, y, z = place
    return ((z // 2) * 4 + x, (z % 2) * 8 + y * 2 + core)


def along(place, axis, step):
    moved = list(place)
    moved[axis] = (place[axis] + step) % 4
    return moved


def rows_at(start, count):
    return pl.ds(pl.multiple_of(start, 16), count)


PACK = 2816
FLOWS = (
    (0, 512, (0, 1, 2), False),
    (512, 512, (1, 2, 0), False),
    (1024, 128, (2, 0, 1), True),
    (1152, 512, (1, 2, 0), False),
    (1664, 512, (2, 0, 1), False),
    (2176, 128, (0, 1, 2), True),
    (2304, 256, (0, 1, 2), True),
    (2560, 128, (1, 2, 0), True),
    (2688, 128, (2, 0, 1), True),
)
LAYER_FOUR, LAYER_THREE, OTHERS = (0, 1, 2), (3, 4, 5), (6, 7, 8)


def first_place(tap):
    if tap < 5:
        return 2560 + 12 * tap, slice(64, 128)
    at = 2624 + 16 * ((tap - 5) // 2)
    return at, slice(64 * ((tap - 5) % 2), 64 * ((tap - 5) % 2) + 64)


def last_place(tap):
    return 2656 + 12 * (tap // 2), slice(64 * (tap % 2), 64 * (tap % 2) + 64)


class Flow:
    def __init__(self, number, place, core, pack, whole, base, rows, order, short):
        self.number, self.place, self.core = number, place, core
        self.pack, self.whole = pack, whole
        self.base, self.order = base, order
        self.eighth, self.short = rows // 8, short
        before = [flow for flow in FLOWS[:number] if flow[3] == short]
        self.late_at = sum(flow[1] for flow in before) // (8 if short else 32)
        self.hop = 0
        self.sent = []
        self.now = []

    def send(self, src, dst, slot, peer):
        copy = pltpu.make_async_remote_copy(
            src_ref=src,
            dst_ref=dst,
            send_sem=self.sems[0].at[self.number, self.hop + slot],
            recv_sem=self.sems[1].at[self.number, self.hop + slot],
            device_id=peer,
            device_id_type=MESH_ID,
        )
        copy.start()
        self.sent.append(copy)
        self.now.append(copy)

    def arrive(self):
        for copy in self.now:
            copy.wait_recv()
        self.now = []

    def to_eight(self, views):
        axis = self.order[0]
        for other in range(2):
            for step in range(4):
                slot = other * 4 + step
                if slot > 0:
                    core = (self.core + other) % 2
                    spot = along(self.place, axis, step)
                    src, dst = views(slot, spot[axis] * 2 + core)
                    self.send(src, dst, slot, device_at(spot, core))
        self.hop += 8

    def to_axis(self, turn, views):
        axis = self.order[turn]
        for step in (1, 2, 3):
            src, dst = views(axis, step)
            self.send(src, dst, step, device_at(along(self.place, axis, step), self.core))
        self.hop += 4

    def advance(self, stage):
        in_a, sum_a, in_b, in_c, in_d = self.refs
        eighth, small = self.eighth, self.eighth // 4
        mine = self.place[self.order[0]] * 2 + self.core
        eight, many = self.base // 8, self.late_at
        row = self.base + mine * eighth
        if stage == 0:
            self.to_eight(
                lambda slot, chunk: (
                    self.pack.at[rows_at(self.base + chunk * eighth, eighth)],
                    in_a.at[slot, pl.ds(eight, eighth)],
                )
            )
            return
        self.arrive()
        if stage == 1:
            value = self.pack[rows_at(row, eighth), :]
            for slot in range(1, 8):
                value = value + in_a[slot, pl.ds(eight, eighth), :]
            if self.short:
                at = self.late_at
                in_d[0, pl.ds(at, eighth), :] = value
                for step_b in range(4):
                    for step_c in range(4):
                        slot = step_b * 4 + step_c
                        if slot > 0:
                            spot = along(self.place, self.order[1], step_b)
                            spot = along(spot, self.order[2], step_c)
                            self.send(
                                in_d.at[0, pl.ds(at, eighth)],
                                in_d.at[slot, pl.ds(at, eighth)],
                                slot,
                                device_at(spot, self.core),
                            )
                self.hop += 16
            else:
                sum_a[pl.ds(eight, eighth), :] = value
                self.to_axis(
                    1,
                    lambda axis, step: (
                        sum_a.at[rows_at(eight + (self.place[axis] + step) % 4 * small, small)],
                        in_b.at[step - 1, pl.ds(many, small)],
                    ),
                )
            return
        if self.short:
            if stage == 2:
                at = self.late_at
                total = None
                for spot_b in range(4):
                    for spot_c in range(4):
                        slot = (self.place[self.order[1]] - spot_b + 4) % 4 * 4
                        slot = slot + (self.place[self.order[2]] - spot_c + 4) % 4
                        term = in_d[slot, pl.ds(at, eighth), :]
                        total = term if total is None else total + term
                self.whole[rows_at(row, eighth), :] = total.astype(jnp.bfloat16)
                self.spread(row)
            return
        if stage == 2:
            value = sum_a[rows_at(eight + self.place[self.order[1]] * small, small), :]
            for step in range(3):
                value = value + in_b[step, pl.ds(many, small), :]
            in_c[0, pl.ds(many, small), :] = value
            self.to_axis(
                2,
                lambda axis, step: (
                    in_c.at[0, pl.ds(many, small)],
                    in_c.at[step, pl.ds(many, small)],
                ),
            )
        elif stage == 3:
            here = self.place[self.order[2]]
            terms = [in_c[(here - other + 4) % 4, pl.ds(many, small), :] for other in range(4)]
            at = row + self.place[self.order[1]] * small
            total = (terms[0] + terms[1]) + (terms[2] + terms[3])
            self.whole[rows_at(at, small), :] = total.astype(jnp.bfloat16)
            block = self.whole.at[rows_at(at, small)]
            self.to_axis(1, lambda axis, step: (block, block))
        elif stage == 4:
            self.spread(row)

    def spread(self, row):
        block = self.whole.at[rows_at(row, self.eighth)]
        self.to_eight(lambda slot, chunk: (block, block))

    def settle(self):
        for copy in self.sent[: len(self.sent) - len(self.now)]:
            copy.wait_send()
        self.sent = list(self.now)

    def drain(self):
        for copy in self.sent:
            copy.wait_send()


def window(gy):
    return pl.multiple_of(jnp.clip(jnp.right_shift(gy * 32 - 8, 7), 0, 2) * 128, 128)


STRIDE = 48
ROWS = 30
SPAN = ROWS * STRIDE
BF = jnp.bfloat16
F32 = jnp.float32


def start_of(halo):
    return (7 - halo) * STRIDE - 16


def count_of(halo):
    return (16 + 2 * halo) * STRIDE + 32


def mm(lhs, rhs):
    return lax.dot_general(lhs, rhs, (((1,), (0,)), ((), ())), preferred_element_type=F32)


def mm_nt(lhs, rhs):
    return lax.dot_general(lhs, rhs, (((1,), (1,)), ((), ())), preferred_element_type=F32)


def mm_tn(lhs, rhs):
    return lax.dot_general(lhs, rhs, (((0,), (0,)), ((), ())), preferred_element_type=F32)


def iota(shape, dim):
    return lax.broadcasted_iota(jnp.int32, shape, dim)


def over(value, divisor):
    return lax.shift_right_logical(value * ((1 << 16) // divisor + 1), 16)


def one_hot(flag):
    return jnp.where(flag, 1.0, 0.0).astype(F32).astype(BF)


def three_parts(value):
    high = value.astype(BF)
    rest = value - high.astype(F32)
    middle = rest.astype(BF)
    return high, middle, (rest - middle.astype(F32)).astype(BF)


def exact_right(value, selector):
    parts = three_parts(value)
    return (mm(parts[2], selector) + mm(parts[1], selector)) + mm(parts[0], selector)


def blocks(total, chunk, body):
    def step(index, carry):
        body(pl.multiple_of(index * chunk, 16))
        return carry

    lax.fori_loop(0, total // chunk, step, 0)


def slab(start, count):
    if isinstance(start, int):
        return pl.ds(start, count)
    return pl.ds(pl.multiple_of(start, 16), count)


def inner(ref, shift, lanes):
    first = 7 + shift
    picked = [ref[(first + row) * STRIDE : (first + row) * STRIDE + 32, lanes] for row in range(16)]
    return jnp.concatenate(picked, axis=0)


ROW_SOURCE = (((1, -1), (0, 0), (1, 0)), ((0, 0), (1, 0), (0, 1)))
BACK_SOURCE = ((1, -1), (0, 0), (1, 0), (0, 1))
FINE_SOURCE = ((3, -1), (0, 0), (1, 0), (2, 0), (3, 0), (0, 1))
PAIR_ORDER = (1, 2, 3, 0)
FINE_ORDER = (1, 2, 3, 4, 5, 0)


def train_kernel(
    coarse,
    cot,
    w1,
    w2,
    w3,
    w4,
    w5,
    b1,
    b2,
    b3,
    b4,
    b5,
    fine,
    whole,
    rows_in,
    cot_in,
    known,
    pack,
    mask,
    t_c1,
    m_c1,
    x1,
    t64,
    x2,
    x3,
    t3,
    x4,
    t4,
    x5,
    ay,
    t_cot,
    m_cot,
    xc,
    g5,
    t_g4,
    g4,
    t_g3,
    g3,
    g2,
    v1,
    v3,
    v4,
    v4f,
    v4b,
    v3b,
    v2b,
    v5f,
    v5b,
    acc,
    z5,
    turned,
    lined,
    wide,
    in_a,
    sum_a,
    in_b,
    in_c,
    in_d,
    keep_sem,
    row_send,
    row_recv,
    far_send,
    far_recv,
    cot_send,
    cot_recv,
    hop_send,
    hop_recv,
):
    gx = lax.axis_index("gx")
    gy = lax.axis_index("gy")

    def peer(step_x, step_y):
        return ((gx + step_x + 8) % 8, (gy + step_y + 16) % 16)

    barrier = pltpu.get_barrier_semaphore()
    for step_x in (-1, 0, 1):
        for step_y in range(16):
            if step_x != 0 or step_y != 0:
                pl.semaphore_signal(
                    barrier, inc=1, device_id=peer(step_x, step_y), device_id_type=MESH_ID
                )
    spot_now, core = coordinates()
    partner = device_at(spot_now, 1 - core)
    helpers = [partner]
    for axis in range(3):
        for step in (1, 2, 3):
            near = along(spot_now, axis, step)
            helpers += [device_at(near, core), device_at(near, 1 - core)]
            for more in (1, 2, 3):
                helpers.append(device_at(along(near, (axis + 1) % 3, more), core))
    for helper in helpers:
        pl.semaphore_signal(barrier, inc=1, device_id=helper, device_id_type=MESH_ID)
    locals_ = [
        pltpu.make_async_copy(
            cot, cot_in.at[1, :, pl.ds(16, 64), :], keep_sem.at[0]
        ),
        pltpu.make_async_copy(
            coarse.at[:, pl.ds(window(gy), 256)], rows_in.at[6 + gy], keep_sem.at[1]
        ),
    ]
    for copy in locals_:
        copy.start()
    base_row = gx * 16
    base_col = gy * 32

    place = iota((SPAN, 128), 0)
    line = over(place, STRIDE)
    col = place - line * STRIDE
    left = jnp.where(col >= 40, 1, 0)
    row = line - 7 + left + base_row
    col = col - left * STRIDE + base_col
    ok = (row >= 0) & (row < 128) & (col >= 0) & (col < 512)
    mask[...] = jnp.where(ok, 1.0, 0.0)

    def kept(start, count):
        return mask[slab(start, count), 0:1]

    lane = iota((256, 256), 1)
    natural = iota((256, 256), 0)
    wanted = (lane - over(lane, 64) * 64) * 4 + over(lane, 64)
    to_phase = one_hot(natural == wanted)
    wanted_back = (natural - over(natural, 64) * 64) * 4 + over(natural, 64)
    to_natural = one_hot(lane == wanted_back)
    v3[...] = mm(w3[...], to_phase).astype(BF)
    v4[...] = mm(w4[...], to_phase).astype(BF)
    bias3 = exact_right(jnp.broadcast_to(b3[...], (8, 256)), to_phase)[0:1]
    bias4 = exact_right(jnp.broadcast_to(b4[...], (8, 256)), to_phase)[0:1]

    v1[...] = jnp.zeros(v1.shape, BF)
    for r in range(3):
        for s in range(3):
            v1[s * 48 + r * 16 : s * 48 + r * 16 + 12, :] = w1[r * 3 + s]
    for r in range(3):
        for position, c4 in enumerate(PAIR_ORDER):
            for q in range(2):
                s = c4 - q
                target = (slice(position * 64, position * 64 + 64), slice(q * 256, q * 256 + 256))
                if 0 <= s <= 2:
                    v4f[r, target[0], target[1]] = v4[(r * 3 + s) * 64 : (r * 3 + s) * 64 + 64, :]
                else:
                    v4f[r, target[0], target[1]] = jnp.zeros((64, 256), BF)
    for u in range(4):
        for a in range(2):
            for b in range(2):
                for position, v in enumerate(PAIR_ORDER):
                    r, s = a + 2 - u, b + 2 - v
                    at = (slice((2 * a + b) * 64, (2 * a + b) * 64 + 64),)
                    at = at + (slice(position * 256, position * 256 + 256),)
                    if 0 <= r <= 2 and 0 <= s <= 2:
                        tap = (r * 3 + s) * 64
                        v4b[u, at[0], at[1]] = v4[tap : tap + 64, :]
                    else:
                        v4b[u, at[0], at[1]] = jnp.zeros((64, 256), BF)
    for u in range(3):
        for v in range(3):
            tap = ((2 - u) * 3 + 2 - v) * 64
            v3b[u, :, v * 256 : v * 256 + 256] = v3[tap : tap + 64, :]
            v2b[u, :, v * 64 : v * 64 + 64] = w2[tap : tap + 64, :]

    pl.semaphore_wait(barrier, 47 + len(helpers))

    def remote(src, dst, send_sem, recv_sem, target):
        return pltpu.make_async_remote_copy(
            src_ref=src,
            dst_ref=dst,
            send_sem=send_sem,
            recv_sem=recv_sem,
            device_id=target,
            device_id_type=MESH_ID,
        )

    def row_copy(step, dst_row, send_sem, recv_sem, step_x):
        target = peer(step_x, step)
        return remote(
            coarse.at[:, pl.ds(window(target[1]), 256)],
            rows_in.at[dst_row],
            send_sem,
            recv_sem,
            target,
        )

    cot_copies = []
    parts = ((16, 48, 0), (64, 0, 16), (16, 0, 80))
    for index_x, step_x in enumerate((1, 0, -1)):
        count, src_row, dst_row = parts[index_x]
        for index_y, step_y in enumerate((1, 0, -1)):
            if step_x == 0 and step_y == 0:
                continue
            cot_copies.append(
                remote(
                    cot.at[:, pl.ds(src_row, count), :],
                    cot_in.at[index_y, :, pl.ds(dst_row, count), :],
                    cot_send.at[index_x, index_y],
                    cot_recv.at[index_x, index_y],
                    peer(step_x, step_y),
                )
            )
    for copy in cot_copies:
        copy.start()

    copies = []
    for step in range(1, 16):
        copies.append(row_copy(step, 6 + gy, row_send.at[step], row_recv.at[step], 0))
    for copy in copies:
        copy.start()

    def far(step_x, dst_row, slot):
        return [
            row_copy(step, dst_row, far_send.at[step], far_recv.at[slot], step_x)
            for step in range(16)
        ]

    @pl.when(gy < 6)
    def _():
        for copy in far(-1, 22 + gy, 6 + gy):
            copy.start()

    @pl.when(gy >= 10)
    def _():
        for copy in far(1, gy - 10, gy - 10):
            copy.start()

    def await_rows():
        locals_[1].wait()
        for step in range(1, 16):
            row_copy(
                step, 6 + (gy - step + 16) % 16, row_send.at[step], row_recv.at[step], 0
            ).wait_recv()
        for slot in range(12):
            dst_row = slot if slot < 6 else 16 + slot
            row_copy(1, dst_row, far_send.at[0], far_recv.at[slot], 0).wait_recv()

    def await_cot():
        locals_[0].wait()
        for copy in cot_copies:
            copy.wait_recv()

    def drain_gather():
        for copy in copies + cot_copies:
            copy.wait_send()

        @pl.when(gy < 6)
        def _():
            for copy in far(-1, 22 + gy, 6 + gy):
                copy.wait_send()

        @pl.when(gy >= 10)
        def _():
            for copy in far(1, gy - 10, gy - 10):
                copy.wait_send()


    flows = [
        Flow(number, spot_now, core, pack, whole, *FLOWS[number])
        for number in range(len(FLOWS))
    ]
    refs = (in_a, sum_a, in_b, in_c, in_d)
    sems = (hop_send, hop_recv)
    for flow in flows:
        flow.refs = refs
        flow.sems = sems

    def progress(numbers, stage):
        for number in numbers:
            flows[number].advance(stage)

    def spread_out(width, group):
        lanes = iota((12, width), 1)
        spread = one_hot((lanes - over(lanes, group) * group) == iota((12, width), 0))
        for tap in range(9):
            wide[tap * 64 : tap * 64 + 64, 0:width] = mm_tn(w5[tap], spread)

    spread_out(432, 12)
    lanes6 = iota((64, 432), 1)
    cell6 = over(lanes6, 12)
    col6 = over(cell6, 6)
    row6 = cell6 - col6 * 6
    for big_r in range(4):
        for big_c in range(4):
            value = jnp.zeros((64, 432), F32)
            for r in range(3):
                for s in range(3):
                    tap = (r * 3 + s) * 64
                    value = jnp.where(
                        (row6 == big_r + 2 - r) & (col6 == big_c + 2 - s),
                        wide[tap : tap + 64, :],
                        value,
                    )
            at = (big_r * 4 + big_c) * 64
            v5b[at : at + 64, :] = value.astype(BF)

    t64[0:8, :] = jnp.zeros((8, 64), F32)
    for ref in (t3, t4, t_g3, t_g4):
        for tile in range(ref.shape[0]):
            ref[tile, 0:8, :] = jnp.zeros((8, 128), F32)
            ref[tile, ref.shape[1] - 8 :, :] = jnp.zeros((8, 128), F32)
    begin, count = start_of(3), count_of(3)
    for a in range(2):
        x4[a, begin - 48 : begin, :] = jnp.zeros((48, 256), BF)
        x4[a, begin + count : begin + count + 48, :] = jnp.zeros((48, 256), BF)

    t_c1[...] = jnp.zeros(t_c1.shape, F32)
    t_cot[...] = jnp.zeros(t_cot.shape, F32)
    known[...] = jnp.zeros(known.shape, F32)
    for first, last in ((2560, 2816),):
        pack[first:last, :] = jnp.zeros((last - first, 128), F32)

    await_cot()
    fine_row = iota((96, 128), 0) - 16 + gx * 64
    row_ok = (fine_row >= 0) & (fine_row < 512)
    for o in range(12):
        for third in range(3):
            value = cot_in[third, o].astype(F32)
            ay[third, pl.ds(o, 96, stride=12), :] = jnp.where(row_ok, value, 0.0)
    spot = iota((288, 384), 0)
    tap_col = over(spot, 48)
    want = (spot - tap_col * 48 - 8) * 4 + tap_col - 1
    real = want + gy * 128
    pick = one_hot((iota((288, 384), 1) == want + 128) & (real >= 0) & (real < 2048))
    value = None
    for third in range(3):
        term = mm_nt(pick[:, third * 128 : third * 128 + 128], ay[third].astype(BF))
        value = term if value is None else value + term
    m_cot[...] = value
    for i in range(-3, 19):
        for v in range(6):
            at = (i + 7) * STRIDE - 8
            t_cot[at : at + 48, v * 72 : v * 72 + 72] = m_cot[
                v * 48 : v * 48 + 48, (4 * i + 15) * 12 : (4 * i + 15) * 12 + 72
            ]
    xc[...] = t_cot[...].astype(BF)
    for big_c in range(4):
        at = (big_c + 1) * 72 + 12
        g5[:, big_c * 48 : big_c * 48 + 48] = inner(t_cot, 0, slice(at, at + 48)).astype(BF)

    spot = iota((144, 256), 0)
    tap_col = over(spot, 48)
    want = spot - tap_col * 48 - 8 + tap_col - 1 + base_col
    first = jnp.clip(jnp.right_shift(base_col - 8, 7), 0, 2) * 128
    pick = one_hot((want == iota((144, 256), 1) + first) & (want >= 0) & (want < 512))
    await_rows()
    for k in range(28):
        present = (base_row - 6 + k >= 0) & (base_row - 6 + k < 128)
        known[k * 16 : k * 16 + 12, :] = jnp.where(present, rows_in[k].astype(F32), 0.0)
    m_c1[...] = mm_nt(pick, known[...].astype(BF))
    for i in range(-5, 21):
        for s in range(3):
            at = (i + 7) * STRIDE - 8
            t_c1[at : at + 48, s * 48 : s * 48 + 48] = m_c1[
                s * 48 : s * 48 + 48, (i + 5) * 16 : (i + 5) * 16 + 48
            ]
    x1[...] = t_c1[...].astype(BF)

    def three_shifts(target, begin, count):
        t64[8 + count : 16 + count, :] = jnp.zeros((8, 64), F32)
        for s in range(3):
            target[begin : begin + count, s * 64 : s * 64 + 64] = t64[7 + s : 7 + s + count, :].astype(BF)

    begin, count = start_of(5), count_of(5)

    def one(at):
        z = mm(x1[slab(begin + at, 256), :], v1[...]) + b1[...]
        t64[pl.ds(pl.multiple_of(8 + at, 8), 256), :] = (
            jnp.tanh(z) * kept(begin + at, 256)
        )

    blocks(count, 256, one)
    three_shifts(x2, begin, count)

    begin2, count2 = start_of(4), count_of(4)

    def two(at):
        z = b2[...]
        for r in range(3):
            z = z + mm(x2[slab(begin2 + 48 * (r - 1) + at, 592), :], w2[192 * r : 192 * r + 192, :])
        t64[pl.ds(pl.multiple_of(8 + at, 8), 592), :] = jnp.tanh(z) * kept(begin2 + at, 592)

    blocks(count2, 592, two)
    three_shifts(x3, begin2, count2)

    begin3, count3 = start_of(3), count_of(3)

    def three(at):
        z = bias3
        for r in range(3):
            z = z + mm(x3[slab(begin3 + 48 * (r - 1) + at, 272), :], v3[192 * r : 192 * r + 192, :])
        z = jnp.tanh(z) * kept(begin3 + at, 272)
        for a in range(2):
            t3[a, pl.ds(pl.multiple_of(8 + at, 8), 272), :] = z[:, a * 128 : a * 128 + 128]

    blocks(count3, 272, three)
    for a in range(2):
        at = slice(begin3, begin3 + count3)
        x4[a, at, 0:128] = t3[a, 8 : 8 + count3, :].astype(BF)
        x4[a, at, 128:192] = t3[a, 9 : 9 + count3, 0:64].astype(BF)
        x4[a, at, 192:256] = t3[a, 7 : 7 + count3, 64:128].astype(BF)

    def four(at):
        for p in range(2):
            z = jnp.concatenate([bias4, bias4], axis=1)
            for r in range(3):
                a, d = ROW_SOURCE[p][r]
                z = z + mm(x4[a, slab(begin3 + 48 * d + at, 272), :], v4f[r])
            z = jnp.tanh(z) * kept(begin3 + at, 272)
            for half in range(2):
                for q in range(2):
                    t4[4 * p + 2 * half + q, pl.ds(pl.multiple_of(8 + at, 8), 272), :] = z[
                        :, q * 256 + half * 128 : q * 256 + half * 128 + 128
                    ]

    blocks(count3, 272, four)
    for big_r in range(4):
        at = slice(begin3, begin3 + count3)
        x5[big_r, at, 0:128] = t4[2 * big_r, 8 : 8 + count3, :].astype(BF)
        x5[big_r, at, 128:256] = t4[2 * big_r + 1, 8 : 8 + count3, :].astype(BF)
        x5[big_r, at, 256:320] = t4[2 * big_r, 9 : 9 + count3, 0:64].astype(BF)
        x5[big_r, at, 320:384] = t4[2 * big_r + 1, 7 : 7 + count3, 64:128].astype(BF)

    def back_four(at):
        here = slab(begin3 + at, 272)
        keep = kept(begin3 + at, 272)
        for big_r in range(4):
            value = mm_nt(xc[here, :], v5b[big_r * 256 : big_r * 256 + 256, :])
            act = x5[big_r, here, 0:256].astype(F32)
            value = value * (1.0 - act * act) * keep
            for q in range(2):
                t_g4[2 * big_r + q, pl.ds(pl.multiple_of(8 + at, 8), 272), :] = value[
                    :, q * 128 : q * 128 + 128
                ]

    blocks(count3, 272, back_four)
    for p in range(2):
        at = slice(begin3, begin3 + count3)
        for half in range(2):
            src = (2 * p + half) * 2
            dst = half * 128
            for q in range(2):
                g4[p, at, q * 256 + dst : q * 256 + dst + 128] = t_g4[
                    src + q, 8 : 8 + count3, :
                ].astype(BF)
            g4[p, at, 512 + dst : 640 + dst] = t_g4[src, 9 : 9 + count3, :].astype(BF)
            g4[p, at, 768 + dst : 896 + dst] = t_g4[src + 1, 7 : 7 + count3, :].astype(BF)

    sums4 = jnp.zeros((1, 256), F32)
    for p in range(2):
        value = inner(g4.at[p], 0, slice(0, 512))
        sums = jnp.sum(value.astype(F32), axis=0, keepdims=True)
        sums4 = sums4 + sums[:, 0:256] + sums[:, 256:512]
        for r in range(3):
            a, d = ROW_SOURCE[p][r]
            term = mm_tn(inner(x4.at[a], d, slice(0, 256)), value)
            if p == 0:
                acc[r, 0:256, :] = term
            else:
                acc[r, 0:256, :] = acc[r, 0:256, :] + term
    for r in range(3):
        for s in range(3):
            one_at = PAIR_ORDER.index(s) * 64
            two_at = PAIR_ORDER.index(s + 1) * 64
            value = acc[r, one_at : one_at + 64, 0:256] + acc[r, two_at : two_at + 64, 256:512]
            value = exact_right(value, to_natural)
            at = (r * 3 + s) * 64
            pack[at : at + 64, :] = value[:, 0:128]
            pack[576 + at : 640 + at, :] = value[:, 128:256]
    sums4 = exact_right(jnp.broadcast_to(sums4, (8, 256)), to_natural)
    pack[2720:2721, :] = sums4[0:1, 0:128]
    pack[2721:2722, :] = sums4[0:1, 128:256]

    progress(LAYER_FOUR, 0)

    begin2, count2 = start_of(2), count_of(2)

    def back_three(at):
        value = None
        for u in range(4):
            p, d = BACK_SOURCE[u]
            term = mm_nt(g4[p, slab(begin2 + 48 * d + at, 496), :], v4b[u])
            value = term if value is None else value + term
        here = slab(begin2 + at, 496)
        act = jnp.concatenate([x4[0, here, 0:128], x4[1, here, 0:128]], axis=1).astype(F32)
        value = value * (1.0 - act * act) * kept(begin2 + at, 496)
        for a in range(2):
            t_g3[a, pl.ds(pl.multiple_of(8 + at, 8), 496), :] = value[:, a * 128 : a * 128 + 128]

    blocks(count2, 496, back_three)
    for v in range(3):
        for a in range(2):
            at = v * 256 + a * 128
            g3[begin2 : begin2 + count2, at : at + 128] = t_g3[a, 7 + v : 7 + v + count2, :].astype(BF)

    value = inner(g3, 0, slice(256, 512))
    sums3 = jnp.sum(value.astype(F32), axis=0, keepdims=True)
    for r in range(3):
        term = mm_tn(inner(x3, r - 1, slice(0, 192)), value)
        term = exact_right(term, to_natural)
        at = 1152 + r * 192
        pack[at : at + 192, :] = term[:, 0:128]
        pack[576 + at : 768 + at, :] = term[:, 128:256]
    sums3 = exact_right(jnp.broadcast_to(sums3, (8, 256)), to_natural)
    pack[2722:2723, :] = sums3[0:1, 0:128]
    pack[2723:2724, :] = sums3[0:1, 128:256]

    progress(LAYER_THREE, 0)
    progress(LAYER_FOUR, 1)

    lanes5 = iota((384, 192), 1)
    cell5 = over(lanes5, 12)
    col5 = over(cell5, 4)
    row5 = cell5 - col5 * 4
    for r in range(3):
        acc[r, 0:384, 0:192] = jnp.zeros((384, 192), F32)
    for t in range(6):
        big_r, d = FINE_SOURCE[t]
        z5[0:384, 0:192] = mm_tn(inner(x5.at[big_r], d, slice(0, 384)), g5[...])
        for r in range(max(0, t - 3), min(2, t) + 1):
            acc[r, 0:384, 0:192] = jnp.where(row5 == t - r, z5[0:384, 0:192], acc[r, 0:384, 0:192])
    fold_lane = iota((16, 192), 1)
    fold = one_hot((fold_lane - over(fold_lane, 12) * 12) == iota((16, 192), 0))
    col5 = col5[0:64]
    for r in range(3):
        for s in range(3):
            value = jnp.zeros((64, 192), F32)
            for big_c in range(4):
                position = FINE_ORDER.index(big_c + s)
                value = jnp.where(
                    col5 == big_c, acc[r, position * 64 : position * 64 + 64, 0:192], value
                )
            tap = r * 3 + s
            parts = three_parts(value)
            value = (mm_nt(fold, parts[2]) + mm_nt(fold, parts[1])) + mm_nt(fold, parts[0])
            at, lanes = last_place(tap)
            pack[at : at + 12, lanes] = value[0:12]
    sums5 = jnp.sum(g5[...].astype(F32), axis=0, keepdims=True)
    fold_lane = iota((192, 128), 0)
    fold = one_hot((fold_lane - over(fold_lane, 12) * 12) == iota((192, 128), 1))
    pack[2725:2726, :] = exact_right(jnp.broadcast_to(sums5, (8, 192)), fold)[0:1]

    begin1, count1 = start_of(1), count_of(1)

    def back_two(at):
        value = None
        for u in range(3):
            term = mm_nt(g3[slab(begin1 + 48 * (u - 1) + at, 448), :], v3b[u])
            value = term if value is None else value + term
        act = x3[slab(begin1 + at, 448), 64:128].astype(F32)
        t64[pl.ds(pl.multiple_of(8 + at, 8), 448), :] = (
            value * (1.0 - act * act) * kept(begin1 + at, 448)
        )

    blocks(count1, 448, back_two)
    three_shifts(g2, begin1, count1)

    progress(LAYER_FOUR, 2)
    progress(LAYER_THREE, 1)

    value = inner(g2, 0, slice(64, 128))
    sums2 = jnp.sum(value.astype(F32), axis=0, keepdims=True)
    for r in range(3):
        term = mm_tn(inner(x2, r - 1, slice(0, 192)), value)
        for s in range(3):
            tap = r * 3 + s
            at = 2304 + 64 * (tap // 2)
            pack[at : at + 64, 64 * (tap % 2) : 64 * (tap % 2) + 64] = term[s * 64 : s * 64 + 64, :]
    value = None
    for u in range(3):
        term = mm_nt(inner(g2, u - 1, slice(0, 192)), v2b[u])
        value = term if value is None else value + term
    act = inner(x2, 0, slice(64, 128)).astype(F32)
    value = (value * (1.0 - act * act)).astype(BF)
    sums1 = jnp.sum(value.astype(F32), axis=0, keepdims=True)
    pack[2724:2725, 0:64] = sums2
    pack[2724:2725, 64:128] = sums1
    term = mm_tn(inner(x1, 0, slice(0, 144)), value)
    for r in range(3):
        for s in range(3):
            tap = r * 3 + s
            at, lanes = first_place(tap)
            pack[at : at + 12, lanes] = term[s * 48 + r * 16 : s * 48 + r * 16 + 12, :]
    progress(OTHERS, 0)

    spread_out(256, 16)
    lanes5 = iota((64, 256), 1)
    cell5 = over(lanes5, 16)
    col5 = over(cell5, 4)
    row5 = cell5 - col5 * 4
    for t in range(6):
        for position, v in enumerate(FINE_ORDER):
            value = jnp.zeros((64, 256), F32)
            for r in range(max(0, t - 3), min(2, t) + 1):
                for s in range(max(0, v - 3), min(2, v) + 1):
                    tap = (r * 3 + s) * 64
                    value = jnp.where(
                        (row5 == t - r) & (col5 == v - s), wide[tap : tap + 64, 0:256], value
                    )
            v5f[t, position * 64 : position * 64 + 64, :] = value.astype(BF)
    z = jnp.zeros((512, 256), F32)
    for t in range(6):
        big_r, d = FINE_SOURCE[t]
        z = z + mm(inner(x5.at[big_r], d, slice(0, 384)), v5f[t])
    z5[...] = z
    progress(LAYER_FOUR, 3)
    progress(LAYER_THREE, 2)
    for i in range(16):
        for big_c in range(4):
            turned[big_c * 32 : big_c * 32 + 32, i * 64 : i * 64 + 64] = z5[
                i * 32 : i * 32 + 32, big_c * 64 : big_c * 64 + 64
            ]
    progress(OTHERS, 1)
    spot = iota((128, 128), 0)
    column = over(spot, 32)
    weave = one_hot(iota((128, 128), 1) == (spot - column * 32) * 4 + column)
    parts = three_parts(turned[...])
    lined[...] = (mm_tn(parts[2], weave) + mm_tn(parts[1], weave)) + mm_tn(parts[0], weave)
    progress(LAYER_FOUR, 4)
    progress(LAYER_THREE, 3)
    for o in range(12):
        fine[o] = lined[pl.ds(o, 64, stride=16), :] + b5[0:1, o : o + 1]
    drain_gather()
    progress(OTHERS, 2)
    for number in LAYER_FOUR:
        flows[number].settle()
    progress(LAYER_FOUR, 5)
    progress(LAYER_THREE, 4)
    for number in LAYER_THREE + OTHERS:
        flows[number].settle()
    for number in LAYER_FOUR:
        flows[number].drain()
    progress(OTHERS, 3)
    progress(LAYER_THREE, 5)
    for number in LAYER_THREE + OTHERS:
        flows[number].drain()


def train_of(coarse, cot, weights, biases):
    count3 = count_of(3) + 16
    scratch = (
        ((28, 12, 256), BF),
        ((3, 12, 96, 128), BF),
        ((448, 256), F32),
        ((PACK, 128), F32),
        ((SPAN, 128), F32),
        ((SPAN, 144), F32),
        ((144, 448), F32),
        ((SPAN, 144), BF),
        ((count_of(5) + 16, 64), F32),
        ((SPAN, 192), BF),
        ((SPAN, 192), BF),
        ((2, count3, 128), F32),
        ((2, SPAN, 256), BF),
        ((8, count3, 128), F32),
        ((4, SPAN, 384), BF),
        ((3, 1152, 128), F32),
        ((SPAN, 432), F32),
        ((288, 1152), F32),
        ((SPAN, 432), BF),
        ((512, 192), BF),
        ((8, count3, 128), F32),
        ((2, SPAN, 1024), BF),
        ((2, count_of(2) + 16, 128), F32),
        ((SPAN, 768), BF),
        ((SPAN, 192), BF),
        ((144, 64), BF),
        ((576, 256), BF),
        ((576, 256), BF),
        ((3, 256, 512), BF),
        ((4, 256, 1024), BF),
        ((3, 64, 768), BF),
        ((3, 64, 192), BF),
        ((6, 384, 256), BF),
        ((1024, 432), BF),
        ((3, 384, 512), F32),
        ((512, 256), F32),
        ((128, 1024), F32),
        ((1024, 128), F32),
        ((576, 432), F32),
        ((8, PACK // 8, 128), F32),
        ((PACK // 8, 128), F32),
        ((3, 64, 128), F32),
        ((4, 64, 128), F32),
        ((16, 96, 128), F32),
    )
    counts = ((2,), (16,), (16,), (16,), (12,), (3, 3), (3, 3), (9, 32), (9, 32))
    vmem = pl.BlockSpec(memory_space=pltpu.VMEM)
    return pl.pallas_call(
        train_kernel,
        out_shape=[
            jax.ShapeDtypeStruct((12, 64, 128), F32),
            jax.ShapeDtypeStruct((PACK, 128), BF),
        ],
        in_specs=[vmem] * 12,
        out_specs=[vmem] * 2,
        scratch_shapes=[pltpu.VMEM(shape, kind) for shape, kind in scratch]
        + [pltpu.SemaphoreType.DMA(shape) for shape in counts],
        compiler_params=pltpu.CompilerParams(
            vmem_limit_bytes=66000000, collective_id=0, has_side_effects=True
        ),
        name="train_tile",
    )(coarse, cot, *weights, *biases)


def unpack_kernel(
    scale, fine_in, whole_in, fine, out_w1, out_w2, out_w3, out_w4, out_w5, out_b1, out_b2, out_b3, out_b4, out_b5, whole
):
    fine[...] = fine_in[...]
    whole[...] = whole_in[...].astype(F32) * scale
    for index, target in ((0, out_w4), (1152, out_w3)):
        target[:, 0:128] = whole[index : index + 576, :]
        target[:, 128:256] = whole[index + 576 : index + 1152, :]
    for tap in range(9):
        lanes = slice(64 * (tap % 2), 64 * (tap % 2) + 64)
        at = 2304 + 64 * (tap // 2)
        out_w2[tap * 64 : tap * 64 + 64, :] = whole[at : at + 64, lanes]
        first, side = first_place(tap)
        out_w1[tap] = whole[first : first + 12, side]
        first, side = last_place(tap)
        out_w5[tap] = whole[first : first + 12, side]
    for index, target in ((2720, out_b4), (2722, out_b3)):
        target[:, 0:128] = whole[index : index + 1, :]
        target[:, 128:256] = whole[index + 1 : index + 2, :]
    out_b2[...] = whole[2724:2725, 0:64]
    out_b1[...] = whole[2724:2725, 64:128]
    out_b5[...] = whole[2725:2726, 0:12]


def unpack_of(fine, whole, scale):
    shapes = ((12, 64, 128), (9, 12, 64), (576, 64), (576, 256), (576, 256), (9, 12, 64))
    shapes = shapes + ((1, 64), (1, 64), (1, 256), (1, 256), (1, 12))
    vmem = pl.BlockSpec(memory_space=pltpu.VMEM)
    return pl.pallas_call(
        functools.partial(unpack_kernel, scale),
        out_shape=[jax.ShapeDtypeStruct(shape, F32) for shape in shapes],
        in_specs=[vmem] * 2,
        out_specs=[vmem] * 11,
        scratch_shapes=[pltpu.VMEM((PACK, 128), F32)],
        name="unpack",
    )(fine, whole)


def local(
    coarse,
    weight_one,
    weight_two,
    weight_three,
    weight_four,
    weight_five,
    bias_one,
    bias_two,
    bias_three,
    bias_four,
    bias_five,
    cotangent,
):
    weights = (
        weight_one.reshape(9, 12, 64),
        weight_two.reshape(576, 64),
        weight_three.reshape(576, 256),
        weight_four.reshape(576, 256),
        weight_five.transpose(0, 1, 3, 2).reshape(9, 12, 64),
    )
    biases = tuple(
        bias.reshape(1, -1) for bias in (bias_one, bias_two, bias_three, bias_four, bias_five)
    )
    fine, whole = train_of(coarse.reshape(12, 512), cotangent, weights, biases)
    results = unpack_of(fine, whole, float(16 * 128 * 512) ** -0.5)
    return (
        results[0],
        results[1].reshape(3, 3, 12, 64),
        results[2].reshape(3, 3, 64, 64),
        results[3].reshape(3, 3, 64, 256),
        results[4].reshape(3, 3, 64, 256),
        results[5].reshape(3, 3, 12, 64).transpose(0, 1, 3, 2),
    ) + tuple(result.reshape(-1) for result in results[6:])


def solution(mesh):
    in_specs = (
        P(None, ("gx", "gy"), None),
        P(),
        P(),
        P(),
        P(),
        P(),
        P(),
        P(),
        P(),
        P(),
        P(),
        P(None, "gx", "gy"),
    )
    out_specs = (P(None, "gx", "gy"), P(), P(), P(), P(), P(), P(), P(), P(), P(), P())
    return jax.shard_map(local, mesh=mesh, in_specs=in_specs, out_specs=out_specs, check_vma=False)
```

```python
import functools

import jax
import jax.numpy as jnp
from jax import lax
from jax.experimental import pallas as pl
from jax.experimental.pallas import tpu as pltpu
from jax.sharding import PartitionSpec as P

MESH_ID = pl.DeviceIdType.MESH


def coordinates():
    gx = lax.axis_index("gx")
    gy = lax.axis_index("gy")
    return (gx % 4, (gy // 2) % 4, (gx // 4) * 2 + gy // 8), gy % 2


def device_at(place, core):
    x, y, z = place
    return ((z // 2) * 4 + x, (z % 2) * 8 + y * 2 + core)


def along(place, axis, step):
    moved = list(place)
    moved[axis] = (place[axis] + step) % 4
    return moved


def rows_at(start, count):
    return pl.ds(pl.multiple_of(start, 16), count)


PACK = 2816
FLOWS = (
    (0, 512, (0, 1, 2), False),
    (512, 512, (1, 2, 0), False),
    (1024, 128, (2, 0, 1), True),
    (1152, 512, (1, 2, 0), False),
    (1664, 512, (2, 0, 1), False),
    (2176, 128, (0, 1, 2), True),
    (2304, 256, (0, 1, 2), True),
    (2560, 128, (1, 2, 0), True),
    (2688, 128, (2, 0, 1), True),
)
LAYER_FOUR, LAYER_THREE, OTHERS = (0, 1, 2), (3, 4, 5), (6, 7, 8)


def first_place(tap):
    if tap < 5:
        return 2560 + 12 * tap, slice(64, 128)
    at = 2624 + 16 * ((tap - 5) // 2)
    return at, slice(64 * ((tap - 5) % 2), 64 * ((tap - 5) % 2) + 64)


def last_place(tap):
    return 2656 + 12 * (tap // 2), slice(64 * (tap % 2), 64 * (tap % 2) + 64)


class Flow:
    def __init__(self, number, place, core, pack, whole, base, rows, order, short):
        self.number, self.place, self.core = number, place, core
        self.pack, self.whole = pack, whole
        self.base, self.order = base, order
        self.eighth, self.short = rows // 8, short
        before = [flow for flow in FLOWS[:number] if flow[3] == short]
        self.late_at = sum(flow[1] for flow in before) // (8 if short else 32)
        self.hop = 0
        self.sent = []
        self.now = []

    def send(self, src, dst, slot, peer):
        copy = pltpu.make_async_remote_copy(
            src_ref=src,
            dst_ref=dst,
            send_sem=self.sems[0].at[self.number, self.hop + slot],
            recv_sem=self.sems[1].at[self.number, self.hop + slot],
            device_id=peer,
            device_id_type=MESH_ID,
        )
        copy.start()
        self.sent.append(copy)
        self.now.append(copy)

    def arrive(self):
        for copy in self.now:
            copy.wait_recv()
        self.now = []

    def to_eight(self, views):
        axis = self.order[0]
        for other in range(2):
            for step in range(4):
                slot = other * 4 + step
                if slot > 0:
                    core = (self.core + other) % 2
                    spot = along(self.place, axis, step)
                    src, dst = views(slot, spot[axis] * 2 + core)
                    self.send(src, dst, slot, device_at(spot, core))
        self.hop += 8

    def to_axis(self, turn, views):
        axis = self.order[turn]
        for step in (1, 2, 3):
            src, dst = views(axis, step)
            self.send(src, dst, step, device_at(along(self.place, axis, step), self.core))
        self.hop += 4

    def advance(self, stage):
        in_a, sum_a, in_b, in_c, in_d = self.refs
        eighth, small = self.eighth, self.eighth // 4
        mine = self.place[self.order[0]] * 2 + self.core
        eight, many = self.base // 8, self.late_at
        row = self.base + mine * eighth
        if stage == 0:
            self.to_eight(
                lambda slot, chunk: (
                    self.pack.at[rows_at(self.base + chunk * eighth, eighth)],
                    in_a.at[slot, pl.ds(eight, eighth)],
                )
            )
            return
        self.arrive()
        if stage == 1:
            value = self.pack[rows_at(row, eighth), :]
            for slot in range(1, 8):
                value = value + in_a[slot, pl.ds(eight, eighth), :]
            if self.short:
                at = self.late_at
                in_d[0, pl.ds(at, eighth), :] = value
                for step_b in range(4):
                    for step_c in range(4):
                        slot = step_b * 4 + step_c
                        if slot > 0:
                            spot = along(self.place, self.order[1], step_b)
                            spot = along(spot, self.order[2], step_c)
                            self.send(
                                in_d.at[0, pl.ds(at, eighth)],
                                in_d.at[slot, pl.ds(at, eighth)],
                                slot,
                                device_at(spot, self.core),
                            )
                self.hop += 16
            else:
                sum_a[pl.ds(eight, eighth), :] = value
                self.to_axis(
                    1,
                    lambda axis, step: (
                        sum_a.at[rows_at(eight + (self.place[axis] + step) % 4 * small, small)],
                        in_b.at[step - 1, pl.ds(many, small)],
                    ),
                )
            return
        if self.short:
            if stage == 2:
                at = self.late_at
                total = None
                for spot_b in range(4):
                    for spot_c in range(4):
                        slot = (self.place[self.order[1]] - spot_b + 4) % 4 * 4
                        slot = slot + (self.place[self.order[2]] - spot_c + 4) % 4
                        term = in_d[slot, pl.ds(at, eighth), :]
                        total = term if total is None else total + term
                self.whole[rows_at(row, eighth), :] = total.astype(jnp.bfloat16)
                self.spread(row)
            return
        if stage == 2:
            value = sum_a[rows_at(eight + self.place[self.order[1]] * small, small), :]
            for step in range(3):
                value = value + in_b[step, pl.ds(many, small), :]
            in_c[0, pl.ds(many, small), :] = value
            self.to_axis(
                2,
                lambda axis, step: (
                    in_c.at[0, pl.ds(many, small)],
                    in_c.at[step, pl.ds(many, small)],
                ),
            )
        elif stage == 3:
            here = self.place[self.order[2]]
            terms = [in_c[(here - other + 4) % 4, pl.ds(many, small), :] for other in range(4)]
            at = row + self.place[self.order[1]] * small
            total = (terms[0] + terms[1]) + (terms[2] + terms[3])
            self.whole[rows_at(at, small), :] = total.astype(jnp.bfloat16)
            block = self.whole.at[rows_at(at, small)]
            self.to_axis(1, lambda axis, step: (block, block))
        elif stage == 4:
            self.spread(row)

    def spread(self, row):
        block = self.whole.at[rows_at(row, self.eighth)]
        self.to_eight(lambda slot, chunk: (block, block))

    def settle(self):
        for copy in self.sent[: len(self.sent) - len(self.now)]:
            copy.wait_send()
        self.sent = list(self.now)

    def drain(self):
        for copy in self.sent:
            copy.wait_send()


def window(gy):
    return pl.multiple_of(jnp.clip(jnp.right_shift(gy * 32 - 8, 7), 0, 2) * 128, 128)


STRIDE = 48
ROWS = 30
SPAN = ROWS * STRIDE
BF = jnp.bfloat16
F32 = jnp.float32


def start_of(halo):
    return (7 - halo) * STRIDE - 16


def count_of(halo):
    return (16 + 2 * halo) * STRIDE + 32


def mm(lhs, rhs):
    return lax.dot_general(lhs, rhs, (((1,), (0,)), ((), ())), preferred_element_type=F32)


def mm_nt(lhs, rhs):
    return lax.dot_general(lhs, rhs, (((1,), (1,)), ((), ())), preferred_element_type=F32)


def mm_tn(lhs, rhs):
    return lax.dot_general(lhs, rhs, (((0,), (0,)), ((), ())), preferred_element_type=F32)


def iota(shape, dim):
    return lax.broadcasted_iota(jnp.int32, shape, dim)


def over(value, divisor):
    return lax.shift_right_logical(value * ((1 << 16) // divisor + 1), 16)


def one_hot(flag):
    return jnp.where(flag, 1.0, 0.0).astype(F32).astype(BF)


def three_parts(value):
    high = value.astype(BF)
    rest = value - high.astype(F32)
    middle = rest.astype(BF)
    return high, middle, (rest - middle.astype(F32)).astype(BF)


def exact_right(value, selector):
    parts = three_parts(value)
    return (mm(parts[2], selector) + mm(parts[1], selector)) + mm(parts[0], selector)


def blocks(total, chunk, body):
    def step(index, carry):
        body(pl.multiple_of(index * chunk, 16))
        return carry

    lax.fori_loop(0, total // chunk, step, 0)


def slab(start, count):
    if isinstance(start, int):
        return pl.ds(start, count)
    return pl.ds(pl.multiple_of(start, 16), count)


def inner(ref, shift, lanes):
    first = 7 + shift
    picked = [ref[(first + row) * STRIDE : (first + row) * STRIDE + 32, lanes] for row in range(16)]
    return jnp.concatenate(picked, axis=0)


ROW_SOURCE = (((1, -1), (0, 0), (1, 0)), ((0, 0), (1, 0), (0, 1)))
BACK_SOURCE = ((1, -1), (0, 0), (1, 0), (0, 1))
FINE_SOURCE = ((3, -1), (0, 0), (1, 0), (2, 0), (3, 0), (0, 1))
PAIR_ORDER = (1, 2, 3, 0)
FINE_ORDER = (1, 2, 3, 4, 5, 0)


def train_kernel(
    coarse,
    cot,
    w1,
    w2,
    w3,
    w4,
    w5,
    b1,
    b2,
    b3,
    b4,
    b5,
    fine,
    whole,
    rows_in,
    cot_in,
    known,
    pack,
    mask,
    t_c1,
    m_c1,
    x1,
    t64,
    x2,
    x3,
    t3,
    x4,
    t4,
    x5,
    ay,
    t_cot,
    m_cot,
    xc,
    g5,
    t_g4,
    g4,
    t_g3,
    g3,
    g2,
    v1,
    v3,
    v4,
    v4f,
    v4b,
    v3b,
    v2b,
    v5f,
    v5b,
    acc,
    z5,
    turned,
    lined,
    wide,
    in_a,
    sum_a,
    in_b,
    in_c,
    in_d,
    keep_sem,
    row_send,
    row_recv,
    far_send,
    far_recv,
    cot_send,
    cot_recv,
    hop_send,
    hop_recv,
):
    gx = lax.axis_index("gx")
    gy = lax.axis_index("gy")

    def peer(step_x, step_y):
        return ((gx + step_x + 8) % 8, (gy + step_y + 16) % 16)

    barrier = pltpu.get_barrier_semaphore()
    for step_x in (-1, 0, 1):
        for step_y in range(16):
            if step_x != 0 or step_y != 0:
                pl.semaphore_signal(
                    barrier, inc=1, device_id=peer(step_x, step_y), device_id_type=MESH_ID
                )
    spot_now, core = coordinates()
    partner = device_at(spot_now, 1 - core)
    helpers = [partner]
    for axis in range(3):
        for step in (1, 2, 3):
            near = along(spot_now, axis, step)
            helpers += [device_at(near, core), device_at(near, 1 - core)]
            for more in (1, 2, 3):
                helpers.append(device_at(along(near, (axis + 1) % 3, more), core))
    for helper in helpers:
        pl.semaphore_signal(barrier, inc=1, device_id=helper, device_id_type=MESH_ID)
    locals_ = [
        pltpu.make_async_copy(
            cot, cot_in.at[1, :, pl.ds(16, 64), :], keep_sem.at[0]
        ),
        pltpu.make_async_copy(
            coarse.at[:, pl.ds(window(gy), 256)], rows_in.at[6 + gy], keep_sem.at[1]
        ),
    ]
    for copy in locals_:
        copy.start()
    base_row = gx * 16
    base_col = gy * 32

    place = iota((SPAN, 128), 0)
    line = over(place, STRIDE)
    col = place - line * STRIDE
    left = jnp.where(col >= 40, 1, 0)
    row = line - 7 + left + base_row
    col = col - left * STRIDE + base_col
    ok = (row >= 0) & (row < 128) & (col >= 0) & (col < 512)
    mask[...] = jnp.where(ok, 1.0, 0.0)

    def kept(start, count):
        return mask[slab(start, count), 0:1]

    lane = iota((256, 256), 1)
    natural = iota((256, 256), 0)
    wanted = (lane - over(lane, 64) * 64) * 4 + over(lane, 64)
    to_phase = one_hot(natural == wanted)
    wanted_back = (natural - over(natural, 64) * 64) * 4 + over(natural, 64)
    to_natural = one_hot(lane == wanted_back)
    v3[...] = mm(w3[...], to_phase).astype(BF)
    v4[...] = mm(w4[...], to_phase).astype(BF)
    bias3 = exact_right(jnp.broadcast_to(b3[...], (8, 256)), to_phase)[0:1]
    bias4 = exact_right(jnp.broadcast_to(b4[...], (8, 256)), to_phase)[0:1]

    v1[...] = jnp.zeros(v1.shape, BF)
    for r in range(3):
        for s in range(3):
            v1[s * 48 + r * 16 : s * 48 + r * 16 + 12, :] = w1[r * 3 + s]
    for r in range(3):
        for position, c4 in enumerate(PAIR_ORDER):
            for q in range(2):
                s = c4 - q
                target = (slice(position * 64, position * 64 + 64), slice(q * 256, q * 256 + 256))
                if 0 <= s <= 2:
                    v4f[r, target[0], target[1]] = v4[(r * 3 + s) * 64 : (r * 3 + s) * 64 + 64, :]
                else:
                    v4f[r, target[0], target[1]] = jnp.zeros((64, 256), BF)
    for u in range(4):
        for a in range(2):
            for b in range(2):
                for position, v in enumerate(PAIR_ORDER):
                    r, s = a + 2 - u, b + 2 - v
                    at = (slice((2 * a + b) * 64, (2 * a + b) * 64 + 64),)
                    at = at + (slice(position * 256, position * 256 + 256),)
                    if 0 <= r <= 2 and 0 <= s <= 2:
                        tap = (r * 3 + s) * 64
                        v4b[u, at[0], at[1]] = v4[tap : tap + 64, :]
                    else:
                        v4b[u, at[0], at[1]] = jnp.zeros((64, 256), BF)
    for u in range(3):
        for v in range(3):
            tap = ((2 - u) * 3 + 2 - v) * 64
            v3b[u, :, v * 256 : v * 256 + 256] = v3[tap : tap + 64, :]
            v2b[u, :, v * 64 : v * 64 + 64] = w2[tap : tap + 64, :]

    pl.semaphore_wait(barrier, 47 + len(helpers))

    def remote(src, dst, send_sem, recv_sem, target):
        return pltpu.make_async_remote_copy(
            src_ref=src,
            dst_ref=dst,
            send_sem=send_sem,
            recv_sem=recv_sem,
            device_id=target,
            device_id_type=MESH_ID,
        )

    def row_copy(step, dst_row, send_sem, recv_sem, step_x):
        target = peer(step_x, step)
        return remote(
            coarse.at[:, pl.ds(window(target[1]), 256)],
            rows_in.at[dst_row],
            send_sem,
            recv_sem,
            target,
        )

    cot_copies = []
    parts = ((16, 48, 0), (64, 0, 16), (16, 0, 80))
    for index_x, step_x in enumerate((1, 0, -1)):
        count, src_row, dst_row = parts[index_x]
        for index_y, step_y in enumerate((1, 0, -1)):
            if step_x == 0 and step_y == 0:
                continue
            cot_copies.append(
                remote(
                    cot.at[:, pl.ds(src_row, count), :],
                    cot_in.at[index_y, :, pl.ds(dst_row, count), :],
                    cot_send.at[index_x, index_y],
                    cot_recv.at[index_x, index_y],
                    peer(step_x, step_y),
                )
            )
    for copy in cot_copies:
        copy.start()

    copies = []
    for step in range(1, 16):
        copies.append(row_copy(step, 6 + gy, row_send.at[step], row_recv.at[step], 0))
    for copy in copies:
        copy.start()

    def far(step_x, dst_row, slot):
        return [
            row_copy(step, dst_row, far_send.at[step], far_recv.at[slot], step_x)
            for step in range(16)
        ]

    @pl.when(gy < 6)
    def _():
        for copy in far(-1, 22 + gy, 6 + gy):
            copy.start()

    @pl.when(gy >= 10)
    def _():
        for copy in far(1, gy - 10, gy - 10):
            copy.start()

    def await_rows():
        locals_[1].wait()
        for step in range(1, 16):
            row_copy(
                step, 6 + (gy - step + 16) % 16, row_send.at[step], row_recv.at[step], 0
            ).wait_recv()
        for slot in range(12):
            dst_row = slot if slot < 6 else 16 + slot
            row_copy(1, dst_row, far_send.at[0], far_recv.at[slot], 0).wait_recv()

    def await_cot():
        locals_[0].wait()
        for copy in cot_copies:
            copy.wait_recv()

    def drain_gather():
        for copy in copies + cot_copies:
            copy.wait_send()

        @pl.when(gy < 6)
        def _():
            for copy in far(-1, 22 + gy, 6 + gy):
                copy.wait_send()

        @pl.when(gy >= 10)
        def _():
            for copy in far(1, gy - 10, gy - 10):
                copy.wait_send()


    flows = [
        Flow(number, spot_now, core, pack, whole, *FLOWS[number])
        for number in range(len(FLOWS))
    ]
    refs = (in_a, sum_a, in_b, in_c, in_d)
    sems = (hop_send, hop_recv)
    for flow in flows:
        flow.refs = refs
        flow.sems = sems

    def progress(numbers, stage):
        for number in numbers:
            flows[number].advance(stage)

    def spread_out(width, group):
        lanes = iota((12, width), 1)
        spread = one_hot((lanes - over(lanes, group) * group) == iota((12, width), 0))
        for tap in range(9):
            wide[tap * 64 : tap * 64 + 64, 0:width] = mm_tn(w5[tap], spread)

    spread_out(432, 12)
    lanes6 = iota((64, 432), 1)
    cell6 = over(lanes6, 12)
    col6 = over(cell6, 6)
    row6 = cell6 - col6 * 6
    for big_r in range(4):
        for big_c in range(4):
            value = jnp.zeros((64, 432), F32)
            for r in range(3):
                for s in range(3):
                    tap = (r * 3 + s) * 64
                    value = jnp.where(
                        (row6 == big_r + 2 - r) & (col6 == big_c + 2 - s),
                        wide[tap : tap + 64, :],
                        value,
                    )
            at = (big_r * 4 + big_c) * 64
            v5b[at : at + 64, :] = value.astype(BF)

    t64[0:8, :] = jnp.zeros((8, 64), F32)
    for ref in (t3, t4, t_g3, t_g4):
        for tile in range(ref.shape[0]):
            ref[tile, 0:8, :] = jnp.zeros((8, 128), F32)
            ref[tile, ref.shape[1] - 8 :, :] = jnp.zeros((8, 128), F32)
    begin, count = start_of(3), count_of(3)
    for a in range(2):
        x4[a, begin - 48 : begin, :] = jnp.zeros((48, 256), BF)
        x4[a, begin + count : begin + count + 48, :] = jnp.zeros((48, 256), BF)

    t_c1[...] = jnp.zeros(t_c1.shape, F32)
    t_cot[...] = jnp.zeros(t_cot.shape, F32)
    known[...] = jnp.zeros(known.shape, F32)
    for first, last in ((2560, 2816),):
        pack[first:last, :] = jnp.zeros((last - first, 128), F32)

    await_cot()
    fine_row = iota((96, 128), 0) - 16 + gx * 64
    row_ok = (fine_row >= 0) & (fine_row < 512)
    for o in range(12):
        for third in range(3):
            value = cot_in[third, o].astype(F32)
            ay[third, pl.ds(o, 96, stride=12), :] = jnp.where(row_ok, value, 0.0)
    spot = iota((288, 384), 0)
    tap_col = over(spot, 48)
    want = (spot - tap_col * 48 - 8) * 4 + tap_col - 1
    real = want + gy * 128
    pick = one_hot((iota((288, 384), 1) == want + 128) & (real >= 0) & (real < 2048))
    value = None
    for third in range(3):
        term = mm_nt(pick[:, third * 128 : third * 128 + 128], ay[third].astype(BF))
        value = term if value is None else value + term
    m_cot[...] = value
    for i in range(-3, 19):
        for v in range(6):
            at = (i + 7) * STRIDE - 8
            t_cot[at : at + 48, v * 72 : v * 72 + 72] = m_cot[
                v * 48 : v * 48 + 48, (4 * i + 15) * 12 : (4 * i + 15) * 12 + 72
            ]
    xc[...] = t_cot[...].astype(BF)
    for big_c in range(4):
        at = (big_c + 1) * 72 + 12
        g5[:, big_c * 48 : big_c * 48 + 48] = inner(t_cot, 0, slice(at, at + 48)).astype(BF)

    spot = iota((144, 256), 0)
    tap_col = over(spot, 48)
    want = spot - tap_col * 48 - 8 + tap_col - 1 + base_col
    first = jnp.clip(jnp.right_shift(base_col - 8, 7), 0, 2) * 128
    pick = one_hot((want == iota((144, 256), 1) + first) & (want >= 0) & (want < 512))
    await_rows()
    for k in range(28):
        present = (base_row - 6 + k >= 0) & (base_row - 6 + k < 128)
        known[k * 16 : k * 16 + 12, :] = jnp.where(present, rows_in[k].astype(F32), 0.0)
    m_c1[...] = mm_nt(pick, known[...].astype(BF))
    for i in range(-5, 21):
        for s in range(3):
            at = (i + 7) * STRIDE - 8
            t_c1[at : at + 48, s * 48 : s * 48 + 48] = m_c1[
                s * 48 : s * 48 + 48, (i + 5) * 16 : (i + 5) * 16 + 48
            ]
    x1[...] = t_c1[...].astype(BF)

    def three_shifts(target, begin, count):
        t64[8 + count : 16 + count, :] = jnp.zeros((8, 64), F32)
        for s in range(3):
            target[begin : begin + count, s * 64 : s * 64 + 64] = t64[7 + s : 7 + s + count, :].astype(BF)

    begin, count = start_of(5), count_of(5)

    def one(at):
        z = mm(x1[slab(begin + at, 256), :], v1[...]) + b1[...]
        t64[pl.ds(pl.multiple_of(8 + at, 8), 256), :] = (
            jnp.tanh(z) * kept(begin + at, 256)
        )

    blocks(count, 256, one)
    three_shifts(x2, begin, count)

    begin2, count2 = start_of(4), count_of(4)

    def two(at):
        z = b2[...]
        for r in range(3):
            z = z + mm(x2[slab(begin2 + 48 * (r - 1) + at, 592), :], w2[192 * r : 192 * r + 192, :])
        t64[pl.ds(pl.multiple_of(8 + at, 8), 592), :] = jnp.tanh(z) * kept(begin2 + at, 592)

    blocks(count2, 592, two)
    three_shifts(x3, begin2, count2)

    begin3, count3 = start_of(3), count_of(3)

    def three(at):
        z = bias3
        for r in range(3):
            z = z + mm(x3[slab(begin3 + 48 * (r - 1) + at, 272), :], v3[192 * r : 192 * r + 192, :])
        z = jnp.tanh(z) * kept(begin3 + at, 272)
        for a in range(2):
            t3[a, pl.ds(pl.multiple_of(8 + at, 8), 272), :] = z[:, a * 128 : a * 128 + 128]

    blocks(count3, 272, three)
    for a in range(2):
        at = slice(begin3, begin3 + count3)
        x4[a, at, 0:128] = t3[a, 8 : 8 + count3, :].astype(BF)
        x4[a, at, 128:192] = t3[a, 9 : 9 + count3, 0:64].astype(BF)
        x4[a, at, 192:256] = t3[a, 7 : 7 + count3, 64:128].astype(BF)

    def four(at):
        for p in range(2):
            z = jnp.concatenate([bias4, bias4], axis=1)
            for r in range(3):
                a, d = ROW_SOURCE[p][r]
                z = z + mm(x4[a, slab(begin3 + 48 * d + at, 272), :], v4f[r])
            z = jnp.tanh(z) * kept(begin3 + at, 272)
            for half in range(2):
                for q in range(2):
                    t4[4 * p + 2 * half + q, pl.ds(pl.multiple_of(8 + at, 8), 272), :] = z[
                        :, q * 256 + half * 128 : q * 256 + half * 128 + 128
                    ]

    blocks(count3, 272, four)
    for big_r in range(4):
        at = slice(begin3, begin3 + count3)
        x5[big_r, at, 0:128] = t4[2 * big_r, 8 : 8 + count3, :].astype(BF)
        x5[big_r, at, 128:256] = t4[2 * big_r + 1, 8 : 8 + count3, :].astype(BF)
        x5[big_r, at, 256:320] = t4[2 * big_r, 9 : 9 + count3, 0:64].astype(BF)
        x5[big_r, at, 320:384] = t4[2 * big_r + 1, 7 : 7 + count3, 64:128].astype(BF)

    def back_four(at):
        here = slab(begin3 + at, 272)
        keep = kept(begin3 + at, 272)
        for big_r in range(4):
            value = mm_nt(xc[here, :], v5b[big_r * 256 : big_r * 256 + 256, :])
            act = x5[big_r, here, 0:256].astype(F32)
            value = value * (1.0 - act * act) * keep
            for q in range(2):
                t_g4[2 * big_r + q, pl.ds(pl.multiple_of(8 + at, 8), 272), :] = value[
                    :, q * 128 : q * 128 + 128
                ]

    blocks(count3, 272, back_four)
    for p in range(2):
        at = slice(begin3, begin3 + count3)
        for half in range(2):
            src = (2 * p + half) * 2
            dst = half * 128
            for q in range(2):
                g4[p, at, q * 256 + dst : q * 256 + dst + 128] = t_g4[
                    src + q, 8 : 8 + count3, :
                ].astype(BF)
            g4[p, at, 512 + dst : 640 + dst] = t_g4[src, 9 : 9 + count3, :].astype(BF)
            g4[p, at, 768 + dst : 896 + dst] = t_g4[src + 1, 7 : 7 + count3, :].astype(BF)

    sums4 = jnp.zeros((1, 256), F32)
    for p in range(2):
        value = inner(g4.at[p], 0, slice(0, 512))
        sums = jnp.sum(value.astype(F32), axis=0, keepdims=True)
        sums4 = sums4 + sums[:, 0:256] + sums[:, 256:512]
        for r in range(3):
            a, d = ROW_SOURCE[p][r]
            term = mm_tn(inner(x4.at[a], d, slice(0, 256)), value)
            if p == 0:
                acc[r, 0:256, :] = term
            else:
                acc[r, 0:256, :] = acc[r, 0:256, :] + term
    for r in range(3):
        for s in range(3):
            one_at = PAIR_ORDER.index(s) * 64
            two_at = PAIR_ORDER.index(s + 1) * 64
            value = acc[r, one_at : one_at + 64, 0:256] + acc[r, two_at : two_at + 64, 256:512]
            value = exact_right(value, to_natural)
            at = (r * 3 + s) * 64
            pack[at : at + 64, :] = value[:, 0:128]
            pack[576 + at : 640 + at, :] = value[:, 128:256]
    sums4 = exact_right(jnp.broadcast_to(sums4, (8, 256)), to_natural)
    pack[2720:2721, :] = sums4[0:1, 0:128]
    pack[2721:2722, :] = sums4[0:1, 128:256]

    progress(LAYER_FOUR, 0)

    begin2, count2 = start_of(2), count_of(2)

    def back_three(at):
        value = None
        for u in range(4):
            p, d = BACK_SOURCE[u]
            term = mm_nt(g4[p, slab(begin2 + 48 * d + at, 496), :], v4b[u])
            value = term if value is None else value + term
        here = slab(begin2 + at, 496)
        act = jnp.concatenate([x4[0, here, 0:128], x4[1, here, 0:128]], axis=1).astype(F32)
        value = value * (1.0 - act * act) * kept(begin2 + at, 496)
        for a in range(2):
            t_g3[a, pl.ds(pl.multiple_of(8 + at, 8), 496), :] = value[:, a * 128 : a * 128 + 128]

    blocks(count2, 496, back_three)
    for v in range(3):
        for a in range(2):
            at = v * 256 + a * 128
            g3[begin2 : begin2 + count2, at : at + 128] = t_g3[a, 7 + v : 7 + v + count2, :].astype(BF)

    value = inner(g3, 0, slice(256, 512))
    sums3 = jnp.sum(value.astype(F32), axis=0, keepdims=True)
    for r in range(3):
        term = mm_tn(inner(x3, r - 1, slice(0, 192)), value)
        term = exact_right(term, to_natural)
        at = 1152 + r * 192
        pack[at : at + 192, :] = term[:, 0:128]
        pack[576 + at : 768 + at, :] = term[:, 128:256]
    sums3 = exact_right(jnp.broadcast_to(sums3, (8, 256)), to_natural)
    pack[2722:2723, :] = sums3[0:1, 0:128]
    pack[2723:2724, :] = sums3[0:1, 128:256]

    progress(LAYER_THREE, 0)
    progress(LAYER_FOUR, 1)

    lanes5 = iota((384, 192), 1)
    cell5 = over(lanes5, 12)
    col5 = over(cell5, 4)
    row5 = cell5 - col5 * 4
    for r in range(3):
        acc[r, 0:384, 0:192] = jnp.zeros((384, 192), F32)
    for t in range(6):
        big_r, d = FINE_SOURCE[t]
        z5[0:384, 0:192] = mm_tn(inner(x5.at[big_r], d, slice(0, 384)), g5[...])
        for r in range(max(0, t - 3), min(2, t) + 1):
            acc[r, 0:384, 0:192] = jnp.where(row5 == t - r, z5[0:384, 0:192], acc[r, 0:384, 0:192])
    fold_lane = iota((16, 192), 1)
    fold = one_hot((fold_lane - over(fold_lane, 12) * 12) == iota((16, 192), 0))
    col5 = col5[0:64]
    for r in range(3):
        for s in range(3):
            value = jnp.zeros((64, 192), F32)
            for big_c in range(4):
                position = FINE_ORDER.index(big_c + s)
                value = jnp.where(
                    col5 == big_c, acc[r, position * 64 : position * 64 + 64, 0:192], value
                )
            tap = r * 3 + s
            parts = three_parts(value)
            value = (mm_nt(fold, parts[2]) + mm_nt(fold, parts[1])) + mm_nt(fold, parts[0])
            at, lanes = last_place(tap)
            pack[at : at + 12, lanes] = value[0:12]
    sums5 = jnp.sum(g5[...].astype(F32), axis=0, keepdims=True)
    fold_lane = iota((192, 128), 0)
    fold = one_hot((fold_lane - over(fold_lane, 12) * 12) == iota((192, 128), 1))
    pack[2725:2726, :] = exact_right(jnp.broadcast_to(sums5, (8, 192)), fold)[0:1]

    begin1, count1 = start_of(1), count_of(1)

    def back_two(at):
        value = None
        for u in range(3):
            term = mm_nt(g3[slab(begin1 + 48 * (u - 1) + at, 448), :], v3b[u])
            value = term if value is None else value + term
        act = x3[slab(begin1 + at, 448), 64:128].astype(F32)
        t64[pl.ds(pl.multiple_of(8 + at, 8), 448), :] = (
            value * (1.0 - act * act) * kept(begin1 + at, 448)
        )

    blocks(count1, 448, back_two)
    three_shifts(g2, begin1, count1)

    progress(LAYER_FOUR, 2)
    progress(LAYER_THREE, 1)

    value = inner(g2, 0, slice(64, 128))
    sums2 = jnp.sum(value.astype(F32), axis=0, keepdims=True)
    for r in range(3):
        term = mm_tn(inner(x2, r - 1, slice(0, 192)), value)
        for s in range(3):
            tap = r * 3 + s
            at = 2304 + 64 * (tap // 2)
            pack[at : at + 64, 64 * (tap % 2) : 64 * (tap % 2) + 64] = term[s * 64 : s * 64 + 64, :]
    value = None
    for u in range(3):
        term = mm_nt(inner(g2, u - 1, slice(0, 192)), v2b[u])
        value = term if value is None else value + term
    act = inner(x2, 0, slice(64, 128)).astype(F32)
    value = (value * (1.0 - act * act)).astype(BF)
    sums1 = jnp.sum(value.astype(F32), axis=0, keepdims=True)
    pack[2724:2725, 0:64] = sums2
    pack[2724:2725, 64:128] = sums1
    term = mm_tn(inner(x1, 0, slice(0, 144)), value)
    for r in range(3):
        for s in range(3):
            tap = r * 3 + s
            at, lanes = first_place(tap)
            pack[at : at + 12, lanes] = term[s * 48 + r * 16 : s * 48 + r * 16 + 12, :]
    progress(OTHERS, 0)

    spread_out(256, 16)
    lanes5 = iota((64, 256), 1)
    cell5 = over(lanes5, 16)
    col5 = over(cell5, 4)
    row5 = cell5 - col5 * 4
    for t in range(6):
        for position, v in enumerate(FINE_ORDER):
            value = jnp.zeros((64, 256), F32)
            for r in range(max(0, t - 3), min(2, t) + 1):
                for s in range(max(0, v - 3), min(2, v) + 1):
                    tap = (r * 3 + s) * 64
                    value = jnp.where(
                        (row5 == t - r) & (col5 == v - s), wide[tap : tap + 64, 0:256], value
                    )
            v5f[t, position * 64 : position * 64 + 64, :] = value.astype(BF)
    progress(LAYER_FOUR, 3)
    progress(LAYER_THREE, 2)
    z = jnp.zeros((512, 256), F32)
    for t in range(6):
        big_r, d = FINE_SOURCE[t]
        z = z + mm(inner(x5.at[big_r], d, slice(0, 384)), v5f[t])
    z5[...] = z
    progress(OTHERS, 1)
    for i in range(16):
        for big_c in range(4):
            turned[big_c * 32 : big_c * 32 + 32, i * 64 : i * 64 + 64] = z5[
                i * 32 : i * 32 + 32, big_c * 64 : big_c * 64 + 64
            ]
    spot = iota((128, 128), 0)
    column = over(spot, 32)
    weave = one_hot(iota((128, 128), 1) == (spot - column * 32) * 4 + column)
    parts = three_parts(turned[...])
    lined[...] = (mm_tn(parts[2], weave) + mm_tn(parts[1], weave)) + mm_tn(parts[0], weave)
    progress(LAYER_FOUR, 4)
    progress(LAYER_THREE, 3)
    for o in range(12):
        fine[o] = lined[pl.ds(o, 64, stride=16), :] + b5[0:1, o : o + 1]
    drain_gather()
    progress(OTHERS, 2)
    for number in LAYER_FOUR:
        flows[number].settle()
    progress(LAYER_FOUR, 5)
    progress(LAYER_THREE, 4)
    for number in LAYER_THREE + OTHERS:
        flows[number].settle()
    for number in LAYER_FOUR:
        flows[number].drain()
    progress(OTHERS, 3)
    progress(LAYER_THREE, 5)
    for number in LAYER_THREE + OTHERS:
        flows[number].drain()


def train_of(coarse, cot, weights, biases):
    count3 = count_of(3) + 16
    scratch = (
        ((28, 12, 256), BF),
        ((3, 12, 96, 128), BF),
        ((448, 256), F32),
        ((PACK, 128), F32),
        ((SPAN, 128), F32),
        ((SPAN, 144), F32),
        ((144, 448), F32),
        ((SPAN, 144), BF),
        ((count_of(5) + 16, 64), F32),
        ((SPAN, 192), BF),
        ((SPAN, 192), BF),
        ((2, count3, 128), F32),
        ((2, SPAN, 256), BF),
        ((8, count3, 128), F32),
        ((4, SPAN, 384), BF),
        ((3, 1152, 128), F32),
        ((SPAN, 432), F32),
        ((288, 1152), F32),
        ((SPAN, 432), BF),
        ((512, 192), BF),
        ((8, count3, 128), F32),
        ((2, SPAN, 1024), BF),
        ((2, count_of(2) + 16, 128), F32),
        ((SPAN, 768), BF),
        ((SPAN, 192), BF),
        ((144, 64), BF),
        ((576, 256), BF),
        ((576, 256), BF),
        ((3, 256, 512), BF),
        ((4, 256, 1024), BF),
        ((3, 64, 768), BF),
        ((3, 64, 192), BF),
        ((6, 384, 256), BF),
        ((1024, 432), BF),
        ((3, 384, 512), F32),
        ((512, 256), F32),
        ((128, 1024), F32),
        ((1024, 128), F32),
        ((576, 432), F32),
        ((8, PACK // 8, 128), F32),
        ((PACK // 8, 128), F32),
        ((3, 64, 128), F32),
        ((4, 64, 128), F32),
        ((16, 96, 128), F32),
    )
    counts = ((2,), (16,), (16,), (16,), (12,), (3, 3), (3, 3), (9, 32), (9, 32))
    vmem = pl.BlockSpec(memory_space=pltpu.VMEM)
    return pl.pallas_call(
        train_kernel,
        out_shape=[
            jax.ShapeDtypeStruct((12, 64, 128), F32),
            jax.ShapeDtypeStruct((PACK, 128), BF),
        ],
        in_specs=[vmem] * 12,
        out_specs=[vmem] * 2,
        scratch_shapes=[pltpu.VMEM(shape, kind) for shape, kind in scratch]
        + [pltpu.SemaphoreType.DMA(shape) for shape in counts],
        compiler_params=pltpu.CompilerParams(
            vmem_limit_bytes=66000000, collective_id=0, has_side_effects=True
        ),
        name="train_tile",
    )(coarse, cot, *weights, *biases)


def unpack_kernel(
    scale, fine_in, whole_in, fine, out_w1, out_w2, out_w3, out_w4, out_w5, out_b1, out_b2, out_b3, out_b4, out_b5, whole
):
    fine[...] = fine_in[...]
    whole[...] = whole_in[...].astype(F32) * scale
    for index, target in ((0, out_w4), (1152, out_w3)):
        target[:, 0:128] = whole[index : index + 576, :]
        target[:, 128:256] = whole[index + 576 : index + 1152, :]
    for tap in range(9):
        lanes = slice(64 * (tap % 2), 64 * (tap % 2) + 64)
        at = 2304 + 64 * (tap // 2)
        out_w2[tap * 64 : tap * 64 + 64, :] = whole[at : at + 64, lanes]
        first, side = first_place(tap)
        out_w1[tap] = whole[first : first + 12, side]
        first, side = last_place(tap)
        out_w5[tap] = whole[first : first + 12, side]
    for index, target in ((2720, out_b4), (2722, out_b3)):
        target[:, 0:128] = whole[index : index + 1, :]
        target[:, 128:256] = whole[index + 1 : index + 2, :]
    out_b2[...] = whole[2724:2725, 0:64]
    out_b1[...] = whole[2724:2725, 64:128]
    out_b5[...] = whole[2725:2726, 0:12]


def unpack_of(fine, whole, scale):
    shapes = ((12, 64, 128), (9, 12, 64), (576, 64), (576, 256), (576, 256), (9, 12, 64))
    shapes = shapes + ((1, 64), (1, 64), (1, 256), (1, 256), (1, 12))
    vmem = pl.BlockSpec(memory_space=pltpu.VMEM)
    return pl.pallas_call(
        functools.partial(unpack_kernel, scale),
        out_shape=[jax.ShapeDtypeStruct(shape, F32) for shape in shapes],
        in_specs=[vmem] * 2,
        out_specs=[vmem] * 11,
        scratch_shapes=[pltpu.VMEM((PACK, 128), F32)],
        name="unpack",
    )(fine, whole)


def local(
    coarse,
    weight_one,
    weight_two,
    weight_three,
    weight_four,
    weight_five,
    bias_one,
    bias_two,
    bias_three,
    bias_four,
    bias_five,
    cotangent,
):
    weights = (
        weight_one.reshape(9, 12, 64),
        weight_two.reshape(576, 64),
        weight_three.reshape(576, 256),
        weight_four.reshape(576, 256),
        weight_five.transpose(0, 1, 3, 2).reshape(9, 12, 64),
    )
    biases = tuple(
        bias.reshape(1, -1) for bias in (bias_one, bias_two, bias_three, bias_four, bias_five)
    )
    fine, whole = train_of(coarse.reshape(12, 512), cotangent, weights, biases)
    results = unpack_of(fine, whole, float(16 * 128 * 512) ** -0.5)
    return (
        results[0],
        results[1].reshape(3, 3, 12, 64),
        results[2].reshape(3, 3, 64, 64),
        results[3].reshape(3, 3, 64, 256),
        results[4].reshape(3, 3, 64, 256),
        results[5].reshape(3, 3, 12, 64).transpose(0, 1, 3, 2),
    ) + tuple(result.reshape(-1) for result in results[6:])


def solution(mesh):
    in_specs = (
        P(None, ("gx", "gy"), None),
        P(),
        P(),
        P(),
        P(),
        P(),
        P(),
        P(),
        P(),
        P(),
        P(),
        P(None, "gx", "gy"),
    )
    out_specs = (P(None, "gx", "gy"), P(), P(), P(), P(), P(), P(), P(), P(), P(), P())
    return jax.shard_map(local, mesh=mesh, in_specs=in_specs, out_specs=out_specs, check_vma=False)
```
